512 devices in a mesh: gx: 16 (over x, y_hi, core), gy: 32 (over y_lo, z).
Axes of the slice: x: 4, y: 8 (y_hi: 2, y_lo: 4; y = y_hi * 4 + y_lo), z: 8, core: 2. Of those that a mesh axis runs over, the one named last changes fastest.
Arguments:
- bond_mask: int32 [3, 256, 512, 128], P(None, 'gx', 'gy'), may hold values 0 or 1
- levels: float32 [2, 3], replicated, may hold values from 0.3 to 3
- electrode: int32 [2, 256, 512], P(None, 'gx', 'gy'), may hold values 0 or 1
- leakage: float32 [256, 512, 128], P('gx', 'gy'), may hold values from 0.05 to 0.5
- source: float32 [256, 512, 128], P('gx', 'gy'), may hold values from -72 to 72
- weight: float32 [256, 512, 128], P('gx', 'gy'), may hold values from -72 to 72
Outputs:
- potential: float32 [256, 512, 128], P('gx', 'gy')
- adjoint: float32 [256, 512, 128], P('gx', 'gy')
- sensitivity: float32 [3, 256, 512, 128], P(None, 'gx', 'gy')
The draws below stay inside these ranges and needn't reach their ends.
All inputs are finite; a program needn't handle non-finite values. No bound on the sum of `bond_mask` or of `electrode` on one device may be relied on, other than what follows from the above.
Results may differ from the reference program's by a relative error of at most 0.0003.
Values sent between devices are 32-bit elements; how exact they have to be, the bound alone decides.
No kernel may reach another device: no remote copies, remote signals or barrier semaphores. Data moves between devices by JAX's collectives and lax.ppermute only.
A program may use at most 64 MiB of HBM per device.

```python
import math
import jax
import jax.numpy as jnp

NZ = 128
ITERS = 4
NX = 256
NY = 512


def rough_field(key):
    ix = (jnp.arange(NX, dtype=jnp.float32) / max(NX - 1, 1))[:, None, None]
    iy = (jnp.arange(NY, dtype=jnp.float32) / max(NY - 1, 1))[None, :, None]
    base = jnp.clip(jax.random.normal(key, (NX, NY, NZ), jnp.float32), -6.0, 6.0)
    amp = jnp.sqrt(1.0 + 2.0 * ix) * jnp.sqrt(1.0 + 2.0 * iy)
    return 4.0 * amp * base


def draw_source(key, part):
    return rough_field(jax.random.fold_in(key, 3))


def draw_weight(key, part):
    return rough_field(jax.random.fold_in(key, 7))


def touch_ends(array, rng, least, top_value):
    longest = array.shape.index(max(array.shape))
    spots = []
    for shift in (0, 1):
        where = [jax.random.randint(jax.random.fold_in(rng, axis), (), 0, length) for axis, length in enumerate(array.shape)]
        where[longest] = (where[longest] + shift) % array.shape[longest]
        spots.append(tuple(where))
    return array.at[spots[0]].set(least).at[spots[1]].set(top_value)


def block_levels(own_key, shape, shards, least, top_value):
    level = 1.0
    for dim, parts in shards:
        heights = jax.random.uniform(jax.random.fold_in(jax.random.fold_in(own_key, 6), dim), (parts,), jnp.float32, least / len(shards), top_value / len(shards))
        level = level * jnp.repeat(jnp.exp(heights), shape[dim] // parts).reshape((-1,) + (1,) * (len(shape) - 1 - dim))
    return level


def setup_inputs(seed: int = 0) -> dict:
    key_of = jax.random.split(jax.random.key(seed), 7)
    bond_mask = touch_ends((jax.random.randint(key_of[0], (3, NX, NY, NZ), 0, 20) < 7).astype(jnp.int32), jax.random.fold_in(key_of[0], 1), 0, 1)
    levels = jnp.clip(jax.random.uniform(key_of[1], (2, 3), jnp.float32, 0.3, 3.0), 0.3, 3.0)
    electrode = touch_ends((jax.random.randint(key_of[2], (2, NX, NY), 0, 2) < 1).astype(jnp.int32), jax.random.fold_in(key_of[2], 1), 0, 1)
    leakage = jnp.clip(jnp.exp(math.log(0.5) - 2.3025851 * jax.random.uniform(key_of[3], (NX, NY, NZ), jnp.float32) ** block_levels(key_of[3], (NX, NY, NZ), ((0, 16), (1, 32)), -0.2, 0.2)), 0.05, 0.5)
    source = draw_source(jax.random.fold_in(key_of[6], 71), 0)
    weight = draw_weight(jax.random.fold_in(key_of[6], 71), 0)
    return {"bond_mask": bond_mask, "levels": levels, "electrode": electrode, "leakage": leakage, "source": source, "weight": weight}


def shift_up(v):
    padded = jnp.pad(v, ((0, 1), (0, 1), (0, 1)))
    return padded[1:, :-1, :-1], padded[:-1, 1:, :-1], padded[:-1, :-1, 1:]


def shift_down(v):
    padded = jnp.pad(v, ((1, 0), (1, 0), (1, 0)))
    return padded[:-1, 1:, 1:], padded[1:, :-1, 1:], padded[1:, 1:, :-1]


def reference(bond_mask, levels, electrode, leakage, source, weight):
    shape = (NX, NY, NZ)
    ix = jnp.arange(NX)[:, None, None]
    iy = jnp.arange(NY)[None, :, None]
    iz = jnp.arange(NZ)[None, None, :]
    inside = jnp.stack([jnp.broadcast_to(ix < NX - 1, shape), jnp.broadcast_to(iy < NY - 1, shape), jnp.broadcast_to(iz < NZ - 1, shape)]).astype(jnp.float32)
    cond = jnp.where(bond_mask == 1, levels[1][:, None, None, None], levels[0][:, None, None, None]) * inside
    below_x = shift_down(cond[0])[0]
    below_y = shift_down(cond[1])[1]
    below_z = shift_down(cond[2])[2]
    elec = electrode.astype(jnp.float32)
    first = jnp.where(iz == 0, elec[0][:, :, None], 0.0)
    last = jnp.where(iz == NZ - 1, elec[1][:, :, None], 0.0)
    diag = leakage + first + last + cond[0] + cond[1] + cond[2] + below_x + below_y + below_z

    def operate(v):
        up_x, up_y, up_z = shift_up(v)
        dn_x, dn_y, dn_z = shift_down(v)
        beside = cond[0] * up_x + below_x * dn_x + cond[1] * up_y + below_y * dn_y + cond[2] * up_z + below_z * dn_z
        return diag * v - beside

    def solve(rhs):
        x = jnp.zeros(shape, jnp.float32)
        r = rhs
        z = r / diag
        p = z
        rz = jnp.sum(r * z)
        for step in range(ITERS):
            q = operate(p)
            alpha = rz / jnp.sum(p * q)
            x = x + alpha * p
            r = r - alpha * q
            if step + 1 < ITERS:
                z = r / diag
                fresh = jnp.sum(r * z)
                p = z + (fresh / rz) * p
                rz = fresh
        return x

    potential = solve(source + first)
    adjoint = solve(weight + last)
    pu = shift_up(potential)
    au = shift_up(adjoint)
    sens = jnp.stack([-(adjoint - au[d]) * (potential - pu[d]) * inside[d] for d in range(3)])
    return potential, adjoint, sens
```

```python
import functools

import jax
import jax.numpy as jnp
from jax import lax
from jax.experimental import pallas as pl
from jax.experimental.pallas import tpu as pltpu
from jax.sharding import PartitionSpec as P

DEPTH = 4
SUMS = 14
SIDE = 64


def swapped(low_side, high_side, axis):
    count = lax.axis_size(axis)
    even = lax.axis_index(axis) % 2 == 0
    inner = [(i, i ^ 1) for i in range(count)]
    outer = [(i, i + 1) for i in range(1, count - 1, 2)]
    outer = outer + [(target, source) for source, target in outer]
    one = lax.ppermute(jnp.where(even, high_side, low_side), axis, inner)
    two = lax.ppermute(jnp.where(even, low_side, high_side), axis, outer)
    return jnp.where(even, two, one), jnp.where(even, one, two)


def up_y(v):
    return pltpu.roll(v, v.shape[0] - 1, 0)


def dn_y(v):
    return pltpu.roll(v, 1, 0)


def up_z(v):
    return pltpu.roll(v, v.shape[1] - 1, 1)


def dn_z(v):
    return pltpu.roll(v, 1, 1)


def basis_kernel(own_ref, rim_ref, sums_ref, p0, p1, p2, p3, diag, inv, v0):
    cx = own_ref.shape[2]
    planes = own_ref.shape[1]

    def field(f, x):
        return jnp.concatenate([own_ref[f, x], rim_ref[f, x]], axis=0)

    def prepare(x, carry):
        cy, cz = field(4, x), field(5, x)
        d = field(2, x) + field(3, x) + field(3, x - 1) + cy + dn_y(cy) + cz + dn_z(cz)
        r = jnp.where(d > 0.0, 1.0 / d, 0.0)
        diag[x] = d
        inv[x] = r
        v0[0, x] = field(0, x) * r
        v0[1, x] = field(1, x) * r
        return carry

    lax.fori_loop(1, planes, prepare, 0)

    def jacobi(ref, x):
        above, below = field(3, x), field(3, x - 1)
        cy, cz, r = field(4, x), field(5, x), inv[x]
        out = []
        for s in range(2):
            v = ref[s, x]
            beside = above * ref[s, x + 1] + below * ref[s, x - 1]
            beside = beside + cy * up_y(v) + dn_y(cy * v)
            beside = beside + cz * up_z(v) + dn_z(cz * v)
            out.append((v, r * beside))
        return out

    def first(x, carry):
        for s, (v, w) in enumerate(jacobi(v0, x)):
            p0[s, x] = v + w
            p1[s, x] = v - w
        return carry

    lax.fori_loop(2, planes - 1, first, 0)

    def second(x, carry):
        for s, (v, w) in enumerate(jacobi(p0, x)):
            p2[s, x] = v - w
        return carry

    lax.fori_loop(3, planes - 2, second, 0)

    def third(x, carry):
        for s, (v, w) in enumerate(jacobi(p2, x)):
            p3[s, x] = w
        return carry

    lax.fori_loop(4, planes - 3, third, 0)

    def folded(t):
        return sum(t[8 * i : 8 * i + 8] for i in range(1, cx // 8)) + t[0:8] if cx > 8 else t

    def moments(x, carry):
        out = []
        d = diag[x][:cx]
        gx, gy, gz = own_ref[3, x], own_ref[4, x], own_ref[5, x]
        for s in range(2):
            b = own_ref[s, x]
            q = p3[s, x]
            q0, q1, q2, q3 = p0[s, x][:cx], p1[s, x][:cx], p2[s, x][:cx], q[:cx]
            a0 = d * q2
            a1 = d * (2.0 * q1 - q2)
            a2 = d * (q2 - q3)
            links = gx * p3[s, x + 1][:cx] + gy * up_y(q)[:cx] + gz * up_z(q3)
            terms = [a0 * q0, a0 * q1, a0 * q2, a0 * q3, a1 * q1, a1 * q2, a1 * q3]
            terms += [a2 * q2, a2 * q3, (d * q3 - 2.0 * links) * q3]
            terms += [b * q0, b * q1, b * q2, b * q3]
            out += [c + folded(t) for c, t in zip(carry[s * SUMS :], terms)]
        return tuple(out)

    zero = jnp.zeros((8, 128), jnp.float32)
    totals = lax.fori_loop(4, planes - 4, moments, (zero,) * (2 * SUMS))
    lanes = lax.broadcasted_iota(jnp.int32, (1, 128), 1)
    row = jnp.zeros((1, 128), jnp.float32)
    for k, t in enumerate(totals):
        at = k if k < SUMS else SIDE + k - SUMS
        whole = jnp.sum(jnp.sum(t, axis=0, keepdims=True), axis=1, keepdims=True)
        row = row + jnp.where(lanes == at, whole, 0.0)
    sums_ref[...] = row


def combine_kernel(edge_ref, sums_ref, p0, p1, p2, p3, pot_ref, adj_ref, sens_ref, both):
    cx, cy, nz = pot_ref.shape
    total = jnp.sum(jnp.sum(sums_ref[...], axis=0), axis=0, keepdims=True)
    pair = jnp.concatenate([total, pltpu.roll(total, 128 - SIDE, 1)], axis=0)
    lanes = lax.broadcasted_iota(jnp.int32, (2, 128), 1)
    picked = [jnp.sum(jnp.where(lanes == k, pair, 0.0), axis=1, keepdims=True) for k in range(SUMS)]
    energy = {}
    order = iter(picked)
    for i in range(4):
        for j in range(i, 4):
            energy[i, j] = energy[j, i] = next(order)
    right = [next(order) for _ in range(4)]
    scale = [1.0 / jnp.sqrt(energy[i, i]) for i in range(4)]
    m = {(i, j): energy[i, j] * scale[i] * scale[j] for i in range(4) for j in range(4)}
    g = [right[i] * scale[i] for i in range(4)]
    pivot = [None] * 4
    for k in range(4):
        pivot[k] = jnp.where(m[k, k] > 4e-7, 1.0 / m[k, k], 0.0)
        for i in range(k + 1, 4):
            f = m[i, k] * pivot[k]
            for j in range(k, 4):
                m[i, j] = m[i, j] - f * m[k, j]
            g[i] = g[i] - f * g[k]
    c = [None] * 4
    for k in (3, 2, 1, 0):
        t = g[k]
        for j in range(k + 1, 4):
            t = t - m[k, j] * c[j]
        c[k] = t * pivot[k]
    c = [c[k] * scale[k] for k in range(4)]

    def mix(x, carry):
        for s in range(2):
            v = sum(c[k][s : s + 1] * ref[s, x + DEPTH] for k, ref in ((1, p1), (2, p2), (3, p3)))
            both[s, x] = v + c[0][s : s + 1] * p0[s, x + DEPTH]
        return carry

    lax.fori_loop(0, cx + 1, mix, 0)
    rows = lax.broadcasted_iota(jnp.int32, (cy, nz), 0)
    cols = lax.broadcasted_iota(jnp.int32, (cy, nz), 1)
    end_x, end_y = edge_ref[0], edge_ref[1]
    in_y = jnp.where((rows == cy - 1) & (end_y == 1), 0.0, 1.0)
    in_z = jnp.where(cols == nz - 1, 0.0, 1.0)

    def finish(x, carry):
        p, a = both[0, x], both[1, x]
        pot, adj = p[:cy], a[:cy]
        pot_ref[x] = pot
        adj_ref[x] = adj
        in_x = jnp.where((x == cx - 1) & (end_x == 1), 0.0, 1.0)
        sens_ref[0, x] = -(adj - both[1, x + 1][:cy]) * (pot - both[0, x + 1][:cy]) * in_x
        sens_ref[1, x] = -(adj - up_y(a)[:cy]) * (pot - up_y(p)[:cy]) * in_y
        sens_ref[2, x] = -(adj - up_z(adj)) * (pot - up_z(pot)) * in_z
        return carry

    lax.fori_loop(0, cx, finish, 0)


def body(bond_mask, levels, electrode, leakage, source, weight):
    cx, cy, nz = leakage.shape
    shape = (cx, cy, nz)
    nx, ny = lax.axis_size("gx"), lax.axis_size("gy")
    ix, iy = lax.axis_index("gx"), lax.axis_index("gy")
    row_x = ix * cx + lax.broadcasted_iota(jnp.int32, (cx, 1, 1), 0)
    row_y = iy * cy + lax.broadcasted_iota(jnp.int32, (1, cy, 1), 1)
    col_z = lax.broadcasted_iota(jnp.int32, (1, 1, nz), 2)
    inside = jnp.stack(
        [
            jnp.broadcast_to(row_x < cx * nx - 1, shape),
            jnp.broadcast_to(row_y < cy * ny - 1, shape),
            jnp.broadcast_to(col_z < nz - 1, shape),
        ]
    ).astype(jnp.float32)
    cond = (
        jnp.where(bond_mask == 1, levels[1][:, None, None, None], levels[0][:, None, None, None])
        * inside
    )
    elec = electrode.astype(jnp.float32)
    first = jnp.where(col_z == 0, elec[0][:, :, None], 0.0)
    last = jnp.where(col_z == nz - 1, elec[1][:, :, None], 0.0)
    fields = jnp.stack(
        [source + first, weight + last, leakage + first + last, cond[0], cond[1], cond[2]]
    )
    low, high = swapped(fields[:, :DEPTH], fields[:, cx - DEPTH :], "gx")
    wide = jnp.concatenate([low, fields, high], axis=1)
    low, high = swapped(wide[:, :, :DEPTH], wide[:, :, cy - DEPTH :], "gy")
    rim = jnp.concatenate([high, low], axis=2)
    planes, rows = cx + 2 * DEPTH, cy + 2 * DEPTH
    vmem = pl.BlockSpec(memory_space=pltpu.VMEM)
    block = jax.ShapeDtypeStruct((2, planes, rows, nz), jnp.float32)
    sums, *basis = pl.pallas_call(
        basis_kernel,
        out_shape=[jax.ShapeDtypeStruct((1, 128), jnp.float32)] + [block] * 4,
        in_specs=[vmem] * 2,
        out_specs=[vmem] * 5,
        scratch_shapes=[
            pltpu.VMEM((planes, rows, nz), jnp.float32),
            pltpu.VMEM((planes, rows, nz), jnp.float32),
            pltpu.VMEM((2, planes, rows, nz), jnp.float32),
        ],
        compiler_params=pltpu.CompilerParams(vmem_limit_bytes=24 * 2**20),
        name="basis",
    )(wide, rim)
    parts = nx * ny
    spread = jnp.broadcast_to(sums[None], (parts, 1, 128))
    gathered = lax.all_to_all(spread, ("gx", "gy"), 0, 0, tiled=True)
    edge = jnp.stack([ix == nx - 1, iy == ny - 1]).astype(jnp.int32)
    return pl.pallas_call(
        combine_kernel,
        out_shape=[
            jax.ShapeDtypeStruct(shape, jnp.float32),
            jax.ShapeDtypeStruct(shape, jnp.float32),
            jax.ShapeDtypeStruct((3, *shape), jnp.float32),
        ],
        in_specs=[pl.BlockSpec(memory_space=pltpu.SMEM)] + [vmem] * 5,
        out_specs=[vmem] * 3,
        scratch_shapes=[pltpu.VMEM((2, cx + 1, rows, nz), jnp.float32)],
        compiler_params=pltpu.CompilerParams(vmem_limit_bytes=24 * 2**20),
        name="combine",
    )(edge, gathered.reshape(parts // 8, 8, 128), *basis)


def solution(mesh):
    return jax.shard_map(
        body,
        mesh=mesh,
        in_specs=(
            P(None, "gx", "gy", None),
            P(),
            P(None, "gx", "gy"),
            P("gx", "gy", None),
            P("gx", "gy", None),
            P("gx", "gy", None),
        ),
        out_specs=(P("gx", "gy", None), P("gx", "gy", None), P(None, "gx", "gy", None)),
        check_vma=False,
    )
```

```python
import functools

import jax
import jax.numpy as jnp
from jax import lax
from jax.experimental import pallas as pl
from jax.experimental.pallas import tpu as pltpu
from jax.sharding import PartitionSpec as P

DEPTH = 4
SUMS = 14
SLOTS = 22
SIDE = 64


def swapped(low_side, high_side, axis):
    count = lax.axis_size(axis)
    even = lax.axis_index(axis) % 2 == 0
    inner = [(i, i ^ 1) for i in range(count)]
    outer = [(i, i + 1) for i in range(1, count - 1, 2)]
    outer = outer + [(target, source) for source, target in outer]
    one = lax.ppermute(jnp.where(even, high_side, low_side), axis, inner)
    two = lax.ppermute(jnp.where(even, low_side, high_side), axis, outer)
    return jnp.where(even, two, one), jnp.where(even, one, two)


def slot(f, j, above=False):
    start = (0, 4, 8, 12, 15, 19)[f]
    return start + j - (0 if above or f in (0, 1, 2, 4) else 1)


def slab(fields, above):
    cx = fields.shape[1]
    out = []
    for f in range(6):
        count = 3 if f in (3, 5) else DEPTH
        out.append(fields[f, :count] if above else fields[f, cx - count :])
    return jnp.concatenate(out, axis=0)


def up_y(v):
    return pltpu.roll(v, v.shape[0] - 1, 0)


def dn_y(v):
    return pltpu.roll(v, 1, 0)


def up_z(v):
    return pltpu.roll(v, v.shape[1] - 1, 1)


def dn_z(v):
    return pltpu.roll(v, 1, 1)


def basis_kernel(own_ref, side_ref, rim_ref, corner_ref, sums_ref, p0, p1, p2, p3, diag, inv, v0):
    cx = own_ref.shape[2]
    planes = cx + 2 * DEPTH

    def field(f, x):
        if DEPTH <= x < DEPTH + cx:
            return jnp.concatenate([own_ref[f, x - DEPTH], rim_ref[f, x - DEPTH]], axis=0)
        k = slot(f, x) if x < DEPTH else SLOTS + slot(f, x - DEPTH - cx, above=True)
        return jnp.concatenate([side_ref[k], corner_ref[k]], axis=0)

    rows = lax.broadcasted_iota(jnp.int32, (cx + 2 * DEPTH, 128), 0)
    seam = (rows == 0) | (rows == cx)
    for x in range(1, planes):
        d = field(2, x) + jnp.where(seam, dn_y(field(4, x)), 0.0)
        if x in (DEPTH, DEPTH + cx):
            d = d + field(3, x - 1)
        r = jnp.where(d > 0.0, 1.0 / d, 0.0)
        diag[x] = d
        inv[x] = r
        v0[0, x] = field(0, x) * r
        v0[1, x] = field(1, x) * r

    def jacobi(ref, x):
        above, below = field(3, x), field(3, x - 1)
        cy, cz, r = field(4, x), field(5, x), inv[x]
        out = []
        for s in range(2):
            v = ref[s, x]
            beside = above * ref[s, x + 1] + below * ref[s, x - 1]
            beside = beside + cy * up_y(v) + dn_y(cy * v)
            beside = beside + cz * up_z(v) + dn_z(cz * v)
            out.append((v, r * beside))
        return out

    for x in range(2, planes - 1):
        for s, (v, w) in enumerate(jacobi(v0, x)):
            p0[s, x] = v + w
            p1[s, x] = v - w
    for x in range(3, planes - 2):
        for s, (v, w) in enumerate(jacobi(p0, x)):
            p2[s, x] = v - w
    for x in range(4, planes - 3):
        for s, (v, w) in enumerate(jacobi(p2, x)):
            p3[s, x] = w

    def folded(t):
        return sum(t[8 * i : 8 * i + 8] for i in range(1, cx // 8)) + t[0:8] if cx > 8 else t

    totals = [jnp.zeros((8, 128), jnp.float32)] * (2 * SUMS)
    for s in range(2):
        for x in range(DEPTH, planes - DEPTH):
            d = diag[x][:cx]
            gx, gy, gz = own_ref[3, x - DEPTH], own_ref[4, x - DEPTH], own_ref[5, x - DEPTH]
            b = own_ref[s, x - DEPTH]
            q = p3[s, x]
            q0, q1, q2, q3 = p0[s, x][:cx], p1[s, x][:cx], p2[s, x][:cx], q[:cx]
            a0 = d * q2
            a1 = d * (2.0 * q1 - q2)
            a2 = d * (q2 - q3)
            links = gx * p3[s, x + 1][:cx] + gy * up_y(q)[:cx] + gz * up_z(q3)
            terms = [a0 * q0, a0 * q1, a0 * q2, a0 * q3, a1 * q1, a1 * q2, a1 * q3]
            terms += [a2 * q2, a2 * q3, (d * q3 - 2.0 * links) * q3]
            terms += [b * q0, b * q1, b * q2, b * q3]
            for k, t in enumerate(terms):
                totals[s * SUMS + k] = totals[s * SUMS + k] + folded(t)
    lanes = lax.broadcasted_iota(jnp.int32, (1, 128), 1)
    row = jnp.zeros((1, 128), jnp.float32)
    for k, t in enumerate(totals):
        at = k if k < SUMS else SIDE + k - SUMS
        whole = jnp.sum(jnp.sum(t, axis=0, keepdims=True), axis=1, keepdims=True)
        row = row + jnp.where(lanes == at, whole, 0.0)
    sums_ref[...] = row


def combine_kernel(edge_ref, sums_ref, p0, p1, p2, p3, pot_ref, adj_ref, sens_ref, both):
    cx, cy, nz = pot_ref.shape
    total = jnp.sum(jnp.sum(sums_ref[...], axis=0), axis=0, keepdims=True)
    pair = jnp.concatenate([total, pltpu.roll(total, 128 - SIDE, 1)], axis=0)
    lanes = lax.broadcasted_iota(jnp.int32, (2, 128), 1)
    picked = [jnp.sum(jnp.where(lanes == k, pair, 0.0), axis=1, keepdims=True) for k in range(SUMS)]
    energy = {}
    order = iter(picked)
    for i in range(4):
        for j in range(i, 4):
            energy[i, j] = energy[j, i] = next(order)
    right = [next(order) for _ in range(4)]
    scale = [1.0 / jnp.sqrt(energy[i, i]) for i in range(4)]
    m = {(i, j): energy[i, j] * scale[i] * scale[j] for i in range(4) for j in range(4)}
    g = [right[i] * scale[i] for i in range(4)]
    pivot = [None] * 4
    for k in range(4):
        pivot[k] = jnp.where(m[k, k] > 4e-7, 1.0 / m[k, k], 0.0)
        for i in range(k + 1, 4):
            f = m[i, k] * pivot[k]
            for j in range(k, 4):
                m[i, j] = m[i, j] - f * m[k, j]
            g[i] = g[i] - f * g[k]
    c = [None] * 4
    for k in (3, 2, 1, 0):
        t = g[k]
        for j in range(k + 1, 4):
            t = t - m[k, j] * c[j]
        c[k] = t * pivot[k]
    c = [c[k] * scale[k] for k in range(4)]

    def mix(x, carry):
        for s in range(2):
            v = sum(c[k][s : s + 1] * ref[s, x + DEPTH] for k, ref in ((1, p1), (2, p2), (3, p3)))
            both[s, x] = v + c[0][s : s + 1] * p0[s, x + DEPTH]
        return carry

    lax.fori_loop(0, cx + 1, mix, 0)
    rows = lax.broadcasted_iota(jnp.int32, (cy, nz), 0)
    cols = lax.broadcasted_iota(jnp.int32, (cy, nz), 1)
    end_x, end_y = edge_ref[0], edge_ref[1]
    in_y = jnp.where((rows == cy - 1) & (end_y == 1), 0.0, 1.0)
    in_z = jnp.where(cols == nz - 1, 0.0, 1.0)

    def finish(x, carry):
        p, a = both[0, x], both[1, x]
        pot, adj = p[:cy], a[:cy]
        pot_ref[x] = pot
        adj_ref[x] = adj
        in_x = jnp.where((x == cx - 1) & (end_x == 1), 0.0, 1.0)
        sens_ref[0, x] = -(adj - both[1, x + 1][:cy]) * (pot - both[0, x + 1][:cy]) * in_x
        sens_ref[1, x] = -(adj - up_y(a)[:cy]) * (pot - up_y(p)[:cy]) * in_y
        sens_ref[2, x] = -(adj - up_z(adj)) * (pot - up_z(pot)) * in_z
        return carry

    lax.fori_loop(0, cx, finish, 0)


def body(bond_mask, levels, electrode, leakage, source, weight):
    cx, cy, nz = leakage.shape
    shape = (cx, cy, nz)
    nx, ny = lax.axis_size("gx"), lax.axis_size("gy")
    ix, iy = lax.axis_index("gx"), lax.axis_index("gy")
    row_x = ix * cx + lax.broadcasted_iota(jnp.int32, (cx, 1, 1), 0)
    row_y = iy * cy + lax.broadcasted_iota(jnp.int32, (1, cy, 1), 1)
    col_z = lax.broadcasted_iota(jnp.int32, (1, 1, nz), 2)
    inside = jnp.stack(
        [
            jnp.broadcast_to(row_x < cx * nx - 1, shape),
            jnp.broadcast_to(row_y < cy * ny - 1, shape),
            jnp.broadcast_to(col_z < nz - 1, shape),
        ]
    ).astype(jnp.float32)
    cond = (
        jnp.where(bond_mask == 1, levels[1][:, None, None, None], levels[0][:, None, None, None])
        * inside
    )
    elec = electrode.astype(jnp.float32)
    first = jnp.where(col_z == 0, elec[0][:, :, None], 0.0)
    last = jnp.where(col_z == nz - 1, elec[1][:, :, None], 0.0)
    shifted = [
        jnp.concatenate([jnp.zeros((1, cy, nz)), cond[0, :-1]], axis=0),
        jnp.concatenate([jnp.zeros((cx, 1, nz)), cond[1, :, :-1]], axis=1),
        jnp.concatenate([jnp.zeros((cx, cy, 1)), cond[2, :, :, :-1]], axis=2),
    ]
    part = leakage + first + last + cond[0] + cond[1] + cond[2] + sum(shifted)
    fields = jnp.stack([source + first, weight + last, part, cond[0], cond[1], cond[2]])
    low, high = swapped(slab(fields, True), slab(fields, False), "gx")
    side = jnp.concatenate([low, high], axis=0)
    low, high = swapped(fields[:, :, :DEPTH], fields[:, :, cy - DEPTH :], "gy")
    rim = jnp.concatenate([high, low], axis=2)
    low, high = swapped(side[:, :DEPTH], side[:, cy - DEPTH :], "gy")
    corner = jnp.concatenate([high, low], axis=1)
    planes, rows = cx + 2 * DEPTH, cy + 2 * DEPTH
    vmem = pl.BlockSpec(memory_space=pltpu.VMEM)
    block = jax.ShapeDtypeStruct((2, planes, rows, nz), jnp.float32)
    sums, *basis = pl.pallas_call(
        basis_kernel,
        out_shape=[jax.ShapeDtypeStruct((1, 128), jnp.float32)] + [block] * 4,
        in_specs=[vmem] * 4,
        out_specs=[vmem] * 5,
        scratch_shapes=[
            pltpu.VMEM((planes, rows, nz), jnp.float32),
            pltpu.VMEM((planes, rows, nz), jnp.float32),
            pltpu.VMEM((2, planes, rows, nz), jnp.float32),
        ],
        compiler_params=pltpu.CompilerParams(vmem_limit_bytes=24 * 2**20),
        name="basis",
    )(fields, side, rim, corner)
    parts = nx * ny
    spread = jnp.broadcast_to(sums[None], (parts, 1, 128))
    gathered = lax.all_to_all(spread, ("gx", "gy"), 0, 0, tiled=True)
    edge = jnp.stack([ix == nx - 1, iy == ny - 1]).astype(jnp.int32)
    return pl.pallas_call(
        combine_kernel,
        out_shape=[
            jax.ShapeDtypeStruct(shape, jnp.float32),
            jax.ShapeDtypeStruct(shape, jnp.float32),
            jax.ShapeDtypeStruct((3, *shape), jnp.float32),
        ],
        in_specs=[pl.BlockSpec(memory_space=pltpu.SMEM)] + [vmem] * 5,
        out_specs=[vmem] * 3,
        scratch_shapes=[pltpu.VMEM((2, cx + 1, rows, nz), jnp.float32)],
        compiler_params=pltpu.CompilerParams(vmem_limit_bytes=24 * 2**20),
        name="combine",
    )(edge, gathered.reshape(parts // 8, 8, 128), *basis)


def solution(mesh):
    return jax.shard_map(
        body,
        mesh=mesh,
        in_specs=(
            P(None, "gx", "gy", None),
            P(),
            P(None, "gx", "gy"),
            P("gx", "gy", None),
            P("gx", "gy", None),
            P("gx", "gy", None),
        ),
        out_specs=(P("gx", "gy", None), P("gx", "gy", None), P(None, "gx", "gy", None)),
        check_vma=False,
    )
```

```python
import functools

import jax
import jax.numpy as jnp
from jax import lax
from jax.experimental import pallas as pl
from jax.experimental.pallas import tpu as pltpu
from jax.sharding import PartitionSpec as P

DEPTH = 4
SUMS = 14
SLOTS = 22
SIDE = 64


def swapped(one, two, axis, even):
    count = lax.axis_size(axis)
    inner = [(i, i ^ 1) for i in range(count)]
    outer = [(i, i + 1) for i in range(1, count - 1, 2)]
    outer = outer + [(target, source) for source, target in outer]
    two = lax.ppermute(two, axis, outer)
    one = lax.ppermute(one, axis, inner)
    return jnp.where(even, two, one), jnp.where(even, one, two)


def up_y(v):
    return pltpu.roll(v, v.shape[0] - 1, 0)


def dn_y(v):
    return pltpu.roll(v, 1, 0)


def up_z(v):
    return pltpu.roll(v, v.shape[1] - 1, 1)


def dn_z(v):
    return pltpu.roll(v, 1, 1)


def slot(f, j, above=False):
    start = (0, 4, 8, 12, 15, 19)[f]
    return start + j - (0 if above or f in (0, 1, 2, 4) else 1)


def slab():
    out = []
    for f in range(6):
        count = 3 if f in (3, 5) else DEPTH
        out += [(f, k, k - count) for k in range(count)]
    return out


def pack_kernel(flag_ref, level_ref, mask_ref, elec_ref, leak_ref, source_ref, weight_ref,
                own_ref, x_one, x_two, y_one, y_two):
    cx, cy, nz = leak_ref.shape
    rows = lax.broadcasted_iota(jnp.int32, (cy, nz), 0)
    cols = lax.broadcasted_iota(jnp.int32, (cy, nz), 1)
    even_x, even_y = flag_ref[0] == 1, flag_ref[1] == 1
    keep_x = jnp.where(flag_ref[2] == 1, 0.0, 1.0)
    keep_y = jnp.where((rows == cy - 1) & (flag_ref[3] == 1), 0.0, 1.0)
    keep_z = jnp.where(cols == nz - 1, 0.0, 1.0)
    square = lax.broadcasted_iota(jnp.int32, (cy, cy), 0) == lax.broadcasted_iota(jnp.int32, (cy, cy), 1)
    before = None
    for x in range(cx):
        c = [
            jnp.where(mask_ref[d, x] == 1, level_ref[1, d], level_ref[0, d]) for d in range(3)
        ]
        if x == cx - 1:
            c[0] = c[0] * keep_x
        c[1] = c[1] * keep_y
        c[2] = c[2] * keep_z
        ends = []
        for e, at in ((0, 0), (1, nz - 1)):
            row = jnp.broadcast_to(elec_ref[e, x : x + 1].astype(jnp.float32), (cy, cy))
            column = jnp.sum(jnp.where(square, row, 0.0), axis=1, keepdims=True)
            ends.append(jnp.where(cols == at, column, 0.0))
        part = leak_ref[x] + ends[0] + ends[1] + c[0] + c[1] + c[2]
        part = part + jnp.where(rows == 0, 0.0, dn_y(c[1])) + dn_z(c[2])
        if x:
            part = part + before
        before = c[0]
        own_ref[0, x] = source_ref[x] + ends[0]
        own_ref[1, x] = weight_ref[x] + ends[1]
        own_ref[2, x] = part
        for d in range(3):
            own_ref[3 + d, x] = c[d]
    for k, (f, above, below) in enumerate(slab()):
        low, high = own_ref[f, above], own_ref[f, cx + below]
        x_one[k] = jnp.where(even_x, high, low)
        x_two[k] = jnp.where(even_x, low, high)
    for f in range(6):
        for x in range(cx):
            low, high = own_ref[f, x, :DEPTH], own_ref[f, x, cy - DEPTH :]
            y_one[f, x] = jnp.where(even_y, high, low)
            y_two[f, x] = jnp.where(even_y, low, high)


def basis_kernel(own_ref, side_ref, rim_ref, corner_ref, sums_ref, p0, p1, p2, p3, diag, inv, v0):
    cx = own_ref.shape[2]
    planes = cx + 2 * DEPTH

    def field(f, x):
        if DEPTH <= x < DEPTH + cx:
            return jnp.concatenate([own_ref[f, x - DEPTH], rim_ref[f, x - DEPTH]], axis=0)
        k = slot(f, x) if x < DEPTH else SLOTS + slot(f, x - DEPTH - cx, above=True)
        return jnp.concatenate([side_ref[k], corner_ref[k]], axis=0)

    rows = lax.broadcasted_iota(jnp.int32, (cx + 2 * DEPTH, 128), 0)
    seam = (rows == 0) | (rows == cx)
    for x in range(1, planes):
        d = field(2, x) + jnp.where(seam, dn_y(field(4, x)), 0.0)
        if x in (DEPTH, DEPTH + cx):
            d = d + field(3, x - 1)
        r = jnp.where(d > 0.0, 1.0 / d, 0.0)
        diag[x] = d
        inv[x] = r
        v0[0, x] = field(0, x) * r
        v0[1, x] = field(1, x) * r

    def jacobi(ref, x):
        above, below = field(3, x), field(3, x - 1)
        cy, cz, r = field(4, x), field(5, x), inv[x]
        out = []
        for s in range(2):
            v = ref[s, x]
            beside = above * ref[s, x + 1] + below * ref[s, x - 1]
            beside = beside + cy * up_y(v) + dn_y(cy * v)
            beside = beside + cz * up_z(v) + dn_z(cz * v)
            out.append((v, r * beside))
        return out

    for x in range(2, planes - 1):
        for s, (v, w) in enumerate(jacobi(v0, x)):
            p0[s, x] = v + w
            p1[s, x] = v - w
    for x in range(3, planes - 2):
        for s, (v, w) in enumerate(jacobi(p0, x)):
            p2[s, x] = v - w
    for x in range(4, planes - 3):
        for s, (v, w) in enumerate(jacobi(p2, x)):
            p3[s, x] = w

    def folded(t):
        return sum(t[8 * i : 8 * i + 8] for i in range(1, cx // 8)) + t[0:8] if cx > 8 else t

    totals = [jnp.zeros((8, 128), jnp.float32)] * (2 * SUMS)
    for s in range(2):
        for x in range(DEPTH, planes - DEPTH):
            d = diag[x][:cx]
            gx, gy, gz = own_ref[3, x - DEPTH], own_ref[4, x - DEPTH], own_ref[5, x - DEPTH]
            b = own_ref[s, x - DEPTH]
            q = p3[s, x]
            q0, q1, q2, q3 = p0[s, x][:cx], p1[s, x][:cx], p2[s, x][:cx], q[:cx]
            a0 = d * q2
            a1 = d * (2.0 * q1 - q2)
            a2 = d * (q2 - q3)
            links = gx * p3[s, x + 1][:cx] + gy * up_y(q)[:cx] + gz * up_z(q3)
            terms = [a0 * q0, a0 * q1, a0 * q2, a0 * q3, a1 * q1, a1 * q2, a1 * q3]
            terms += [a2 * q2, a2 * q3, (d * q3 - 2.0 * links) * q3]
            terms += [b * q0, b * q1, b * q2, b * q3]
            for k, t in enumerate(terms):
                totals[s * SUMS + k] = totals[s * SUMS + k] + folded(t)
    lanes = lax.broadcasted_iota(jnp.int32, (1, 128), 1)
    row = jnp.zeros((1, 128), jnp.float32)
    for k, t in enumerate(totals):
        at = k if k < SUMS else SIDE + k - SUMS
        whole = jnp.sum(jnp.sum(t, axis=0, keepdims=True), axis=1, keepdims=True)
        row = row + jnp.where(lanes == at, whole, 0.0)
    for k in range(sums_ref.shape[0]):
        sums_ref[k] = jnp.broadcast_to(row, sums_ref.shape[1:])


def combine_kernel(edge_ref, sums_ref, p0, p1, p2, p3, pot_ref, adj_ref, sens_ref, both):
    cx, cy, nz = pot_ref.shape
    total = jnp.sum(jnp.sum(sums_ref[...], axis=0), axis=0, keepdims=True)
    pair = jnp.concatenate([total, pltpu.roll(total, 128 - SIDE, 1)], axis=0)
    lanes = lax.broadcasted_iota(jnp.int32, (2, 128), 1)
    picked = [jnp.sum(jnp.where(lanes == k, pair, 0.0), axis=1, keepdims=True) for k in range(SUMS)]
    energy = {}
    order = iter(picked)
    for i in range(4):
        for j in range(i, 4):
            energy[i, j] = energy[j, i] = next(order)
    right = [next(order) for _ in range(4)]
    scale = [1.0 / jnp.sqrt(energy[i, i]) for i in range(4)]
    m = {(i, j): energy[i, j] * scale[i] * scale[j] for i in range(4) for j in range(4)}
    g = [right[i] * scale[i] for i in range(4)]
    pivot = [None] * 4
    for k in range(4):
        pivot[k] = jnp.where(m[k, k] > 4e-7, 1.0 / m[k, k], 0.0)
        for i in range(k + 1, 4):
            f = m[i, k] * pivot[k]
            for j in range(k, 4):
                m[i, j] = m[i, j] - f * m[k, j]
            g[i] = g[i] - f * g[k]
    c = [None] * 4
    for k in (3, 2, 1, 0):
        t = g[k]
        for j in range(k + 1, 4):
            t = t - m[k, j] * c[j]
        c[k] = t * pivot[k]
    c = [c[k] * scale[k] for k in range(4)]

    for x in range(cx + 1):
        for s in range(2):
            v = sum(c[k][s : s + 1] * ref[s, x + DEPTH] for k, ref in ((1, p1), (2, p2), (3, p3)))
            both[s, x] = v + c[0][s : s + 1] * p0[s, x + DEPTH]
    rows = lax.broadcasted_iota(jnp.int32, (cy, nz), 0)
    cols = lax.broadcasted_iota(jnp.int32, (cy, nz), 1)
    in_x = jnp.where(edge_ref[2] == 1, 0.0, 1.0)
    in_y = jnp.where((rows == cy - 1) & (edge_ref[3] == 1), 0.0, 1.0)
    in_z = jnp.where(cols == nz - 1, 0.0, 1.0)
    for x in range(cx):
        p, a = both[0, x], both[1, x]
        pot, adj = p[:cy], a[:cy]
        pot_ref[x] = pot
        adj_ref[x] = adj
        along = -(adj - both[1, x + 1][:cy]) * (pot - both[0, x + 1][:cy])
        sens_ref[0, x] = along * in_x if x == cx - 1 else along
        sens_ref[1, x] = -(adj - up_y(a)[:cy]) * (pot - up_y(p)[:cy]) * in_y
        sens_ref[2, x] = -(adj - up_z(adj)) * (pot - up_z(pot)) * in_z


def body(bond_mask, levels, electrode, leakage, source, weight):
    cx, cy, nz = leakage.shape
    shape = (cx, cy, nz)
    nx, ny = lax.axis_size("gx"), lax.axis_size("gy")
    ix, iy = lax.axis_index("gx"), lax.axis_index("gy")
    even_x, even_y = ix % 2 == 0, iy % 2 == 0
    flags = jnp.stack([even_x, even_y, ix == nx - 1, iy == ny - 1]).astype(jnp.int32)
    vmem = pl.BlockSpec(memory_space=pltpu.VMEM)
    smem = pl.BlockSpec(memory_space=pltpu.SMEM)
    slots = jax.ShapeDtypeStruct((SLOTS, cy, nz), jnp.float32)
    strip = jax.ShapeDtypeStruct((6, cx, DEPTH, nz), jnp.float32)
    fields, x_one, x_two, y_one, y_two = pl.pallas_call(
        pack_kernel,
        out_shape=[jax.ShapeDtypeStruct((6, *shape), jnp.float32), slots, slots, strip, strip],
        in_specs=[smem] * 2 + [vmem] * 5,
        out_specs=[vmem] * 5,
        compiler_params=pltpu.CompilerParams(vmem_limit_bytes=24 * 2**20),
        name="pack",
    )(flags, levels, bond_mask, electrode, leakage, source, weight)
    low, high = swapped(x_one, x_two, "gx", even_x)
    side = jnp.concatenate([low, high], axis=0)
    first, last = side[:, :DEPTH], side[:, cy - DEPTH :]
    corner_one, corner_two = jnp.where(even_y, last, first), jnp.where(even_y, first, last)
    low, high = swapped(y_one, y_two, "gy", even_y)
    rim = jnp.concatenate([high, low], axis=2)
    low, high = swapped(corner_one, corner_two, "gy", even_y)
    corner = jnp.concatenate([high, low], axis=1)
    planes, rows = cx + 2 * DEPTH, cy + 2 * DEPTH
    block = jax.ShapeDtypeStruct((2, planes, rows, nz), jnp.float32)
    parts = nx * ny
    sums, *basis = pl.pallas_call(
        basis_kernel,
        out_shape=[jax.ShapeDtypeStruct((parts // 8, 8, 128), jnp.float32)] + [block] * 4,
        in_specs=[vmem] * 4,
        out_specs=[vmem] * 5,
        scratch_shapes=[
            pltpu.VMEM((planes, rows, nz), jnp.float32),
            pltpu.VMEM((planes, rows, nz), jnp.float32),
            pltpu.VMEM((2, planes, rows, nz), jnp.float32),
        ],
        compiler_params=pltpu.CompilerParams(vmem_limit_bytes=24 * 2**20),
        name="basis",
    )(fields, side, rim, corner)
    gathered = lax.all_to_all(sums.reshape(parts, 1, 128), ("gx", "gy"), 0, 0, tiled=True)
    return pl.pallas_call(
        combine_kernel,
        out_shape=[
            jax.ShapeDtypeStruct(shape, jnp.float32),
            jax.ShapeDtypeStruct(shape, jnp.float32),
            jax.ShapeDtypeStruct((3, *shape), jnp.float32),
        ],
        in_specs=[smem] + [vmem] * 5,
        out_specs=[vmem] * 3,
        scratch_shapes=[pltpu.VMEM((2, cx + 1, rows, nz), jnp.float32)],
        compiler_params=pltpu.CompilerParams(vmem_limit_bytes=24 * 2**20),
        name="combine",
    )(flags, gathered.reshape(parts // 8, 8, 128), *basis)


def solution(mesh):
    return jax.shard_map(
        body,
        mesh=mesh,
        in_specs=(
            P(None, "gx", "gy", None),
            P(),
            P(None, "gx", "gy"),
            P("gx", "gy", None),
            P("gx", "gy", None),
            P("gx", "gy", None),
        ),
        out_specs=(P("gx", "gy", None), P("gx", "gy", None), P(None, "gx", "gy", None)),
        check_vma=False,
    )
```

```python
import functools

import jax
import jax.numpy as jnp
from jax import lax
from jax.experimental import pallas as pl
from jax.experimental.pallas import tpu as pltpu
from jax.sharding import PartitionSpec as P

DEPTH = 4
SUMS = 14
SLOTS = 22
SIDE = 64


def traded(one, two, axis):
    count = lax.axis_size(axis)
    inner = [(i, i ^ 1) for i in range(count)]
    outer = [(i, i + 1) for i in range(1, count - 1, 2)]
    outer = outer + [(target, source) for source, target in outer]
    two = lax.ppermute(two, axis, outer)
    return lax.ppermute(one, axis, inner), two


def is_even(axis):
    return lax.axis_index(axis) % 2 == 0


def up_y(v):
    return pltpu.roll(v, v.shape[0] - 1, 0)


def dn_y(v):
    return pltpu.roll(v, 1, 0)


def up_z(v):
    return pltpu.roll(v, v.shape[1] - 1, 1)


def dn_z(v):
    return pltpu.roll(v, 1, 1)


def slot(f, j, above=False):
    start = (0, 4, 8, 12, 15, 19)[f]
    return start + j - (0 if above or f in (0, 1, 2, 4) else 1)


def slab():
    out = []
    for f in range(6):
        count = 3 if f in (3, 5) else DEPTH
        out += [(f, k, k - count) for k in range(count)]
    return out


def pack_kernel(level_hbm, mask_hbm, elec_hbm, leak_hbm, source_hbm, weight_hbm,
                own_ref, x_one, x_two, y_one, y_two,
                level_ref, mask_ref, elec_ref, leak_ref, source_ref, weight_ref, sems):
    cx, cy, nz = leak_ref.shape
    ix, iy = lax.axis_index("gx"), lax.axis_index("gy")
    whole = [(level_hbm, level_ref), (elec_hbm, elec_ref)]
    first = [pltpu.make_async_copy(a, b, sems.at[k]) for k, (a, b) in enumerate(whole)]
    half = cx // 2
    parts = []
    for h in range(2):
        at = pl.ds(h * half, half)
        pairs = [(mask_hbm.at[d, at], mask_ref.at[d, at]) for d in range(3)]
        pairs += [(leak_hbm.at[at], leak_ref.at[at]), (source_hbm.at[at], source_ref.at[at])]
        pairs += [(weight_hbm.at[at], weight_ref.at[at])]
        parts.append(
            [pltpu.make_async_copy(a, b, sems.at[2 + 6 * h + k]) for k, (a, b) in enumerate(pairs)]
        )
    for copy in first + parts[0] + parts[1]:
        copy.start()
    for copy in first + parts[0]:
        copy.wait()
    rows = lax.broadcasted_iota(jnp.int32, (cy, nz), 0)
    cols = lax.broadcasted_iota(jnp.int32, (cy, nz), 1)
    even_x, even_y = is_even("gx"), is_even("gy")
    keep_x = jnp.where(ix == lax.axis_size("gx") - 1, 0.0, 1.0)
    keep_y = jnp.where((rows == cy - 1) & (iy == lax.axis_size("gy") - 1), 0.0, 1.0)
    keep_z = jnp.where(cols == nz - 1, 0.0, 1.0)
    square = lax.broadcasted_iota(jnp.int32, (cy, cy), 0) == lax.broadcasted_iota(jnp.int32, (cy, cy), 1)
    before = None
    for x in range(cx):
        if x == half:
            for copy in parts[1]:
                copy.wait()
        c = [
            jnp.where(mask_ref[d, x] == 1, level_ref[1, d], level_ref[0, d]) for d in range(3)
        ]
        if x == cx - 1:
            c[0] = c[0] * keep_x
        c[1] = c[1] * keep_y
        c[2] = c[2] * keep_z
        ends = []
        for e, at in ((0, 0), (1, nz - 1)):
            row = jnp.broadcast_to(elec_ref[e, x : x + 1].astype(jnp.float32), (cy, cy))
            column = jnp.sum(jnp.where(square, row, 0.0), axis=1, keepdims=True)
            ends.append(jnp.where(cols == at, column, 0.0))
        part = leak_ref[x] + ends[0] + ends[1] + c[0] + c[1] + c[2]
        part = part + jnp.where(rows == 0, 0.0, dn_y(c[1])) + dn_z(c[2])
        if x:
            part = part + before
        before = c[0]
        own_ref[0, x] = source_ref[x] + ends[0]
        own_ref[1, x] = weight_ref[x] + ends[1]
        own_ref[2, x] = part
        for d in range(3):
            own_ref[3 + d, x] = c[d]
    for k, (f, above, below) in enumerate(slab()):
        low, high = own_ref[f, above], own_ref[f, cx + below]
        x_one[k] = jnp.where(even_x, high, low)
        x_two[k] = jnp.where(even_x, low, high)
    for f in range(6):
        for x in range(cx):
            low, high = own_ref[f, x, :DEPTH], own_ref[f, x, cy - DEPTH :]
            y_one[f, x] = jnp.where(even_y, high, low)
            y_two[f, x] = jnp.where(even_y, low, high)


def turn_kernel(y_one, y_two, rim_ref, c_one, c_two):
    cx = y_one.shape[1]
    even_x, even_y = is_even("gx"), is_even("gy")
    for f in range(6):
        for x in range(cx):
            one, two = y_one[f, x], y_two[f, x]
            low, high = jnp.where(even_y, two, one), jnp.where(even_y, one, two)
            rim_ref[f, x] = jnp.concatenate([high, low], axis=0)
    for k, (f, above, below) in enumerate(slab()):
        low, high = rim_ref[f, above], rim_ref[f, cx + below]
        c_one[k] = jnp.where(even_x, high, low)
        c_two[k] = jnp.where(even_x, low, high)


def basis_kernel(own_ref, x_one, x_two, rim_ref, c_one, c_two,
                 sums_ref, p0, p1, p2, p3, diag, inv, v0, side_ref, corner_ref):
    cx = own_ref.shape[2]
    planes = cx + 2 * DEPTH
    even = is_even("gx")
    for one, two, to in ((x_one, x_two, side_ref), (c_one, c_two, corner_ref)):
        for k in range(SLOTS):
            to[k] = jnp.where(even, two[k], one[k])
            to[SLOTS + k] = jnp.where(even, one[k], two[k])

    def field(f, x):
        if DEPTH <= x < DEPTH + cx:
            return jnp.concatenate([own_ref[f, x - DEPTH], rim_ref[f, x - DEPTH]], axis=0)
        k = slot(f, x) if x < DEPTH else SLOTS + slot(f, x - DEPTH - cx, above=True)
        return jnp.concatenate([side_ref[k], corner_ref[k]], axis=0)

    rows = lax.broadcasted_iota(jnp.int32, (cx + 2 * DEPTH, 128), 0)
    seam = (rows == 0) | (rows == cx)
    for x in range(1, planes):
        d = field(2, x) + jnp.where(seam, dn_y(field(4, x)), 0.0)
        if x in (DEPTH, DEPTH + cx):
            d = d + field(3, x - 1)
        r = jnp.where(d > 0.0, 1.0 / d, 0.0)
        diag[x] = d
        inv[x] = r
        v0[0, x] = field(0, x) * r
        v0[1, x] = field(1, x) * r

    def jacobi(ref, x):
        above, below = field(3, x), field(3, x - 1)
        cy, cz, r = field(4, x), field(5, x), inv[x]
        out = []
        for s in range(2):
            v = ref[s, x]
            beside = above * ref[s, x + 1] + below * ref[s, x - 1]
            beside = beside + cy * up_y(v) + dn_y(cy * v)
            beside = beside + cz * up_z(v) + dn_z(cz * v)
            out.append((v, r * beside))
        return out

    for x in range(2, planes - 1):
        for s, (v, w) in enumerate(jacobi(v0, x)):
            p0[s, x] = v + w
            p1[s, x] = v - w
    for x in range(3, planes - 2):
        for s, (v, w) in enumerate(jacobi(p0, x)):
            p2[s, x] = v - w
    for x in range(4, planes - 3):
        for s, (v, w) in enumerate(jacobi(p2, x)):
            p3[s, x] = w

    def folded(t):
        return sum(t[8 * i : 8 * i + 8] for i in range(1, cx // 8)) + t[0:8] if cx > 8 else t

    totals = [jnp.zeros((8, 128), jnp.float32)] * (2 * SUMS)
    for s in range(2):
        for x in range(DEPTH, planes - DEPTH):
            d = diag[x][:cx]
            gx, gy, gz = own_ref[3, x - DEPTH], own_ref[4, x - DEPTH], own_ref[5, x - DEPTH]
            b = own_ref[s, x - DEPTH]
            q = p3[s, x]
            q0, q1, q2, q3 = p0[s, x][:cx], p1[s, x][:cx], p2[s, x][:cx], q[:cx]
            a0 = d * q2
            a1 = d * (2.0 * q1 - q2)
            a2 = d * (q2 - q3)
            links = gx * p3[s, x + 1][:cx] + gy * up_y(q)[:cx] + gz * up_z(q3)
            terms = [a0 * q0, a0 * q1, a0 * q2, a0 * q3, a1 * q1, a1 * q2, a1 * q3]
            terms += [a2 * q2, a2 * q3, (d * q3 - 2.0 * links) * q3]
            terms += [b * q0, b * q1, b * q2, b * q3]
            for k, t in enumerate(terms):
                totals[s * SUMS + k] = totals[s * SUMS + k] + folded(t)
    lanes = lax.broadcasted_iota(jnp.int32, (1, 128), 1)
    row = jnp.zeros((1, 128), jnp.float32)
    for k, t in enumerate(totals):
        at = k if k < SUMS else SIDE + k - SUMS
        whole = jnp.sum(jnp.sum(t, axis=0, keepdims=True), axis=1, keepdims=True)
        row = row + jnp.where(lanes == at, whole, 0.0)
    for k in range(sums_ref.shape[0]):
        sums_ref[k] = jnp.broadcast_to(row, sums_ref.shape[1:])


def combine_kernel(sums_ref, p0, p1, p2, p3, pot_ref, adj_ref, sens_ref, both):
    cx, cy, nz = pot_ref.shape
    total = jnp.sum(jnp.sum(sums_ref[...], axis=0), axis=0, keepdims=True)
    pair = jnp.concatenate([total, pltpu.roll(total, 128 - SIDE, 1)], axis=0)
    lanes = lax.broadcasted_iota(jnp.int32, (2, 128), 1)
    picked = [jnp.sum(jnp.where(lanes == k, pair, 0.0), axis=1, keepdims=True) for k in range(SUMS)]
    energy = {}
    order = iter(picked)
    for i in range(4):
        for j in range(i, 4):
            energy[i, j] = energy[j, i] = next(order)
    right = [next(order) for _ in range(4)]
    scale = [1.0 / jnp.sqrt(energy[i, i]) for i in range(4)]
    m = {(i, j): energy[i, j] * scale[i] * scale[j] for i in range(4) for j in range(4)}
    g = [right[i] * scale[i] for i in range(4)]
    pivot = [None] * 4
    for k in range(4):
        pivot[k] = jnp.where(m[k, k] > 4e-7, 1.0 / m[k, k], 0.0)
        for i in range(k + 1, 4):
            f = m[i, k] * pivot[k]
            for j in range(k, 4):
                m[i, j] = m[i, j] - f * m[k, j]
            g[i] = g[i] - f * g[k]
    c = [None] * 4
    for k in (3, 2, 1, 0):
        t = g[k]
        for j in range(k + 1, 4):
            t = t - m[k, j] * c[j]
        c[k] = t * pivot[k]
    c = [c[k] * scale[k] for k in range(4)]

    for x in range(cx + 1):
        for s in range(2):
            v = sum(c[k][s : s + 1] * ref[s, x + DEPTH] for k, ref in ((1, p1), (2, p2), (3, p3)))
            both[s, x] = v + c[0][s : s + 1] * p0[s, x + DEPTH]
    rows = lax.broadcasted_iota(jnp.int32, (cy, nz), 0)
    cols = lax.broadcasted_iota(jnp.int32, (cy, nz), 1)
    in_x = jnp.where(lax.axis_index("gx") == lax.axis_size("gx") - 1, 0.0, 1.0)
    end_y = lax.axis_index("gy") == lax.axis_size("gy") - 1
    in_y = jnp.where((rows == cy - 1) & end_y, 0.0, 1.0)
    in_z = jnp.where(cols == nz - 1, 0.0, 1.0)
    for x in range(cx):
        p, a = both[0, x], both[1, x]
        pot, adj = p[:cy], a[:cy]
        pot_ref[x] = pot
        adj_ref[x] = adj
        along = -(adj - both[1, x + 1][:cy]) * (pot - both[0, x + 1][:cy])
        sens_ref[0, x] = along * in_x if x == cx - 1 else along
        sens_ref[1, x] = -(adj - up_y(a)[:cy]) * (pot - up_y(p)[:cy]) * in_y
        sens_ref[2, x] = -(adj - up_z(adj)) * (pot - up_z(pot)) * in_z


def body(bond_mask, levels, electrode, leakage, source, weight):
    cx, cy, nz = leakage.shape
    shape = (cx, cy, nz)
    given = (levels, bond_mask, electrode, leakage, source, weight)
    nx, ny = lax.axis_size("gx"), lax.axis_size("gy")
    vmem = pl.BlockSpec(memory_space=pltpu.VMEM)
    slots = jax.ShapeDtypeStruct((SLOTS, cy, nz), jnp.float32)
    strip = jax.ShapeDtypeStruct((6, cx, DEPTH, nz), jnp.float32)
    fields, x_one, x_two, y_one, y_two = pl.pallas_call(
        pack_kernel,
        out_shape=[jax.ShapeDtypeStruct((6, *shape), jnp.float32), slots, slots, strip, strip],
        in_specs=[pl.BlockSpec(memory_space=pltpu.HBM)] * 6,
        out_specs=[vmem] * 5,
        scratch_shapes=[
            pltpu.SMEM(levels.shape, jnp.float32),
            pltpu.VMEM(bond_mask.shape, jnp.int32),
            pltpu.VMEM(electrode.shape, jnp.int32),
            pltpu.VMEM(shape, jnp.float32),
            pltpu.VMEM(shape, jnp.float32),
            pltpu.VMEM(shape, jnp.float32),
            pltpu.SemaphoreType.DMA((14,)),
        ],
        compiler_params=pltpu.CompilerParams(vmem_limit_bytes=24 * 2**20),
        name="pack",
    )(*(pltpu.with_memory_space_constraint(a, pltpu.HBM) for a in given))
    x_one, x_two = traded(x_one, x_two, "gx")
    y_one, y_two = traded(y_one, y_two, "gy")
    rest = jax.ShapeDtypeStruct((SLOTS, 2 * DEPTH, nz), jnp.float32)
    rim, c_one, c_two = pl.pallas_call(
        turn_kernel,
        out_shape=[jax.ShapeDtypeStruct((6, cx, 2 * DEPTH, nz), jnp.float32), rest, rest],
        in_specs=[vmem] * 2,
        out_specs=[vmem] * 3,
        compiler_params=pltpu.CompilerParams(vmem_limit_bytes=24 * 2**20),
        name="turn",
    )(y_one, y_two)
    c_one, c_two = traded(c_one, c_two, "gx")
    planes, rows = cx + 2 * DEPTH, cy + 2 * DEPTH
    block = jax.ShapeDtypeStruct((2, planes, rows, nz), jnp.float32)
    parts = nx * ny
    sums, *basis = pl.pallas_call(
        basis_kernel,
        out_shape=[jax.ShapeDtypeStruct((parts // 8, 8, 128), jnp.float32)] + [block] * 4,
        in_specs=[vmem] * 6,
        out_specs=[vmem] * 5,
        scratch_shapes=[
            pltpu.VMEM((planes, rows, nz), jnp.float32),
            pltpu.VMEM((planes, rows, nz), jnp.float32),
            pltpu.VMEM((2, planes, rows, nz), jnp.float32),
            pltpu.VMEM((2 * SLOTS, cy, nz), jnp.float32),
            pltpu.VMEM((2 * SLOTS, 2 * DEPTH, nz), jnp.float32),
        ],
        compiler_params=pltpu.CompilerParams(vmem_limit_bytes=24 * 2**20),
        name="basis",
    )(fields, x_one, x_two, rim, c_one, c_two)
    gathered = lax.all_to_all(sums.reshape(parts, 1, 128), ("gx", "gy"), 0, 0, tiled=True)
    return pl.pallas_call(
        combine_kernel,
        out_shape=[
            jax.ShapeDtypeStruct(shape, jnp.float32),
            jax.ShapeDtypeStruct(shape, jnp.float32),
            jax.ShapeDtypeStruct((3, *shape), jnp.float32),
        ],
        in_specs=[vmem] * 5,
        out_specs=[vmem] * 3,
        scratch_shapes=[pltpu.VMEM((2, cx + 1, rows, nz), jnp.float32)],
        compiler_params=pltpu.CompilerParams(vmem_limit_bytes=24 * 2**20),
        name="combine",
    )(gathered.reshape(parts // 8, 8, 128), *basis)


def solution(mesh):
    return jax.shard_map(
        body,
        mesh=mesh,
        in_specs=(
            P(None, "gx", "gy", None),
            P(),
            P(None, "gx", "gy"),
            P("gx", "gy", None),
            P("gx", "gy", None),
            P("gx", "gy", None),
        ),
        out_specs=(P("gx", "gy", None), P("gx", "gy", None), P(None, "gx", "gy", None)),
        check_vma=False,
    )
```

```python
import functools

import jax
import jax.numpy as jnp
from jax import lax
from jax.experimental import pallas as pl
from jax.experimental.pallas import tpu as pltpu
from jax.sharding import PartitionSpec as P

DEPTH = 4
SUMS = 14
SLOTS = 21
SPARE = 4
TILES = 12
SIDE = 64


def traded(one, two, axis):
    count = lax.axis_size(axis)
    inner = [(i, i ^ 1) for i in range(count)]
    outer = [(i, i + 1) for i in range(1, count - 1, 2)]
    outer = outer + [(target, source) for source, target in outer]
    two = lax.ppermute(two, axis, outer)
    return lax.ppermute(one, axis, inner), two


def is_even(axis):
    return lax.axis_index(axis) % 2 == 0


def up_y(v):
    return pltpu.roll(v, v.shape[0] - 1, 0)


def dn_y(v):
    return pltpu.roll(v, 1, 0)


def up_z(v):
    return pltpu.roll(v, v.shape[1] - 1, 1)


def dn_z(v):
    return pltpu.roll(v, 1, 1)


def slot(f, j, above=False):
    start = (0, 4, 8, 12, 15, 18)[f]
    return start + j - (0 if above or f < 3 else 1)


def slab():
    out = []
    for f in range(6):
        count = DEPTH if f < 3 else 3
        out += [(f, k, k - count) for k in range(count)]
    return out


def pack_kernel(level_hbm, mask_hbm, elec_hbm, leak_hbm, source_hbm, weight_hbm,
                own_ref, x_one, x_two, y_one, y_two,
                level_ref, mask_ref, elec_ref, leak_ref, source_ref, weight_ref, sems):
    cx, cy, nz = leak_ref.shape
    ix, iy = lax.axis_index("gx"), lax.axis_index("gy")
    whole = [(level_hbm, level_ref), (elec_hbm, elec_ref)]
    first = [pltpu.make_async_copy(a, b, sems.at[k]) for k, (a, b) in enumerate(whole)]
    half = cx // 2
    parts = []
    for h in range(2):
        at = pl.ds(h * half, half)
        pairs = [(mask_hbm.at[d, at], mask_ref.at[d, at]) for d in range(3)]
        pairs += [(leak_hbm.at[at], leak_ref.at[at]), (source_hbm.at[at], source_ref.at[at])]
        pairs += [(weight_hbm.at[at], weight_ref.at[at])]
        parts.append(
            [pltpu.make_async_copy(a, b, sems.at[2 + 6 * h + k]) for k, (a, b) in enumerate(pairs)]
        )
    for copy in first + parts[0] + parts[1]:
        copy.start()
    for copy in first + parts[0]:
        copy.wait()
    rows = lax.broadcasted_iota(jnp.int32, (cy, nz), 0)
    cols = lax.broadcasted_iota(jnp.int32, (cy, nz), 1)
    even_x, even_y = is_even("gx"), is_even("gy")
    keep_x = jnp.where(ix == lax.axis_size("gx") - 1, 0.0, 1.0)
    keep_y = jnp.where((rows == cy - 1) & (iy == lax.axis_size("gy") - 1), 0.0, 1.0)
    keep_z = jnp.where(cols == nz - 1, 0.0, 1.0)
    square = lax.broadcasted_iota(jnp.int32, (cy, cy), 0) == lax.broadcasted_iota(jnp.int32, (cy, cy), 1)
    before = None
    for x in range(cx):
        if x == half:
            for copy in parts[1]:
                copy.wait()
        c = [
            jnp.where(mask_ref[d, x] == 1, level_ref[1, d], level_ref[0, d]) for d in range(3)
        ]
        if x == cx - 1:
            c[0] = c[0] * keep_x
        c[1] = c[1] * keep_y
        c[2] = c[2] * keep_z
        ends = []
        for e, at in ((0, 0), (1, nz - 1)):
            row = jnp.broadcast_to(elec_ref[e, x : x + 1].astype(jnp.float32), (cy, cy))
            column = jnp.sum(jnp.where(square, row, 0.0), axis=1, keepdims=True)
            ends.append(jnp.where(cols == at, column, 0.0))
        part = leak_ref[x] + ends[0] + ends[1] + c[0] + c[1] + c[2]
        part = part + jnp.where(rows == 0, 0.0, dn_y(c[1])) + dn_z(c[2])
        if x:
            part = part + before
        before = c[0]
        own_ref[0, x] = source_ref[x] + ends[0]
        own_ref[1, x] = weight_ref[x] + ends[1]
        own_ref[2, x] = part
        for d in range(3):
            own_ref[3 + d, x] = c[d]
    for k in range(SPARE):
        x_one[SLOTS + k] = jnp.zeros((cy, nz), jnp.float32)
        x_two[SLOTS + k] = jnp.zeros((cy, nz), jnp.float32)
    for k, (f, above, below) in enumerate(slab()):
        low, high = own_ref[f, above], own_ref[f, cx + below]
        x_one[k] = jnp.where(even_x, high, low)
        x_two[k] = jnp.where(even_x, low, high)
    for f in range(6):
        for x in range(cx):
            low, high = own_ref[f, x, :DEPTH], own_ref[f, x, cy - DEPTH :]
            y_one[f, x] = jnp.where(even_y, high, low)
            y_two[f, x] = jnp.where(even_y, low, high)


def turn_kernel(y_one, y_two, rim_ref, c_one, c_two):
    cx = y_one.shape[1]
    even_x, even_y = is_even("gx"), is_even("gy")
    for f in range(6):
        for x in range(cx):
            one, two = y_one[f, x], y_two[f, x]
            low, high = jnp.where(even_y, two, one), jnp.where(even_y, one, two)
            rim_ref[f, x] = jnp.concatenate([high, low], axis=0)
    at = lax.broadcasted_iota(jnp.int32, (8, 128), 0)
    for f in range(6):
        tiles = []
        for order in ((0, 1, 2, 3), (cx - 1, cx - 2, cx - 3, cx - 4)):
            near = rim_ref[f, order[0]]
            if f == 4:
                near = jnp.where(at == 4, pltpu.roll(rim_ref[f, order[3]], 5, 0), near)
            third = rim_ref[f, order[2]]
            far = jnp.where(at == 5, pltpu.roll(third, 6, 0), rim_ref[f, order[1]])
            far = jnp.where(at == 2, pltpu.roll(third, 2, 0), far)
            tiles.append((near, far))
        for k in range(2):
            low, high = tiles[0][k], tiles[1][k]
            c_one[2 * f + k] = jnp.where(even_x, high, low)
            c_two[2 * f + k] = jnp.where(even_x, low, high)


def side_kernel(x_one, x_two, side_ref):
    even = is_even("gx")
    for k in range(SLOTS):
        side_ref[k] = jnp.where(even, x_two[k], x_one[k])
        side_ref[SLOTS + k] = jnp.where(even, x_one[k], x_two[k])


def basis_kernel(own_ref, side_ref, rim_ref, c_one, c_two,
                 sums_ref, p0, p1, p2, p3, diag, inv, v0, corner_ref):
    cx = own_ref.shape[2]
    planes = cx + 2 * DEPTH
    even = is_even("gx")
    at = lax.broadcasted_iota(jnp.int32, (8, 128), 0)
    for f in range(6):
        for k in range(2):
            one, two = c_one[2 * f + k], c_two[2 * f + k]
            corner_ref[0, f, k] = jnp.where(even, two, one)
            corner_ref[1, f, k] = jnp.where(even, one, two)

    def corner(f, above, depth):
        if depth == 1:
            return corner_ref[above, f, 0]
        if depth == 2:
            return corner_ref[above, f, 1]
        if depth == 3:
            t = corner_ref[above, f, 1]
            return jnp.where(at == 0, pltpu.roll(t, 6, 0), pltpu.roll(t, 2, 0))
        if f == 4:
            return pltpu.roll(corner_ref[above, f, 0], 3, 0)
        return jnp.zeros((8, 128), jnp.float32)

    def field(f, x):
        if DEPTH <= x < DEPTH + cx:
            return jnp.concatenate([own_ref[f, x - DEPTH], rim_ref[f, x - DEPTH]], axis=0)
        above = int(x >= DEPTH)
        depth = x - DEPTH - cx + 1 if above else DEPTH - x
        if f > 2 and depth > 3:
            flat = jnp.zeros((cx, 128), jnp.float32)
        elif above:
            flat = side_ref[SLOTS + slot(f, depth - 1, above=True)]
        else:
            flat = side_ref[slot(f, x)]
        return jnp.concatenate([flat, corner(f, above, depth)], axis=0)

    rows = lax.broadcasted_iota(jnp.int32, (cx + 2 * DEPTH, 128), 0)
    seam = (rows == 0) | (rows == cx)
    for x in range(1, planes):
        d = field(2, x) + jnp.where(seam, dn_y(field(4, x)), 0.0)
        if x in (DEPTH, DEPTH + cx):
            d = d + field(3, x - 1)
        r = jnp.where(d > 0.0, 1.0 / d, 0.0)
        diag[x] = d
        inv[x] = r
        v0[0, x] = field(0, x) * r
        v0[1, x] = field(1, x) * r

    def jacobi(ref, x):
        above, below = field(3, x), field(3, x - 1)
        cy, cz, r = field(4, x), field(5, x), inv[x]
        out = []
        for s in range(2):
            v = ref[s, x]
            beside = above * ref[s, x + 1] + below * ref[s, x - 1]
            beside = beside + cy * up_y(v) + dn_y(cy * v)
            beside = beside + cz * up_z(v) + dn_z(cz * v)
            out.append((v, r * beside))
        return out

    for x in range(2, planes - 1):
        for s, (v, w) in enumerate(jacobi(v0, x)):
            p0[s, x] = v + w
            p1[s, x] = v - w
    for x in range(3, planes - 2):
        for s, (v, w) in enumerate(jacobi(p0, x)):
            p2[s, x] = v - w
    for x in range(4, planes - 3):
        for s, (v, w) in enumerate(jacobi(p2, x)):
            p3[s, x] = w

    def folded(t):
        return sum(t[8 * i : 8 * i + 8] for i in range(1, cx // 8)) + t[0:8] if cx > 8 else t

    totals = [jnp.zeros((8, 128), jnp.float32)] * (2 * SUMS)
    for s in range(2):
        for x in range(DEPTH, planes - DEPTH):
            d = diag[x][:cx]
            gx, gy, gz = own_ref[3, x - DEPTH], own_ref[4, x - DEPTH], own_ref[5, x - DEPTH]
            b = own_ref[s, x - DEPTH]
            q = p3[s, x]
            q0, q1, q2, q3 = p0[s, x][:cx], p1[s, x][:cx], p2[s, x][:cx], q[:cx]
            a0 = d * q2
            a1 = d * (2.0 * q1 - q2)
            a2 = d * (q2 - q3)
            links = gx * p3[s, x + 1][:cx] + gy * up_y(q)[:cx] + gz * up_z(q3)
            terms = [a0 * q0, a0 * q1, a0 * q2, a0 * q3, a1 * q1, a1 * q2, a1 * q3]
            terms += [a2 * q2, a2 * q3, (d * q3 - 2.0 * links) * q3]
            terms += [b * q0, b * q1, b * q2, b * q3]
            for k, t in enumerate(terms):
                totals[s * SUMS + k] = totals[s * SUMS + k] + folded(t)
    lanes = lax.broadcasted_iota(jnp.int32, (1, 128), 1)
    row = jnp.zeros((1, 128), jnp.float32)
    for k, t in enumerate(totals):
        at = k if k < SUMS else SIDE + k - SUMS
        whole = jnp.sum(jnp.sum(t, axis=0, keepdims=True), axis=1, keepdims=True)
        row = row + jnp.where(lanes == at, whole, 0.0)
    for k in range(sums_ref.shape[0]):
        sums_ref[k] = jnp.broadcast_to(row, sums_ref.shape[1:])


def combine_kernel(sums_ref, p0, p1, p2, p3, pot_ref, adj_ref, sens_ref, both):
    cx, cy, nz = pot_ref.shape
    total = jnp.sum(jnp.sum(sums_ref[...], axis=0), axis=0, keepdims=True)
    pair = jnp.concatenate([total, pltpu.roll(total, 128 - SIDE, 1)], axis=0)
    lanes = lax.broadcasted_iota(jnp.int32, (2, 128), 1)
    picked = [jnp.sum(jnp.where(lanes == k, pair, 0.0), axis=1, keepdims=True) for k in range(SUMS)]
    energy = {}
    order = iter(picked)
    for i in range(4):
        for j in range(i, 4):
            energy[i, j] = energy[j, i] = next(order)
    right = [next(order) for _ in range(4)]
    scale = [1.0 / jnp.sqrt(energy[i, i]) for i in range(4)]
    m = {(i, j): energy[i, j] * scale[i] * scale[j] for i in range(4) for j in range(4)}
    g = [right[i] * scale[i] for i in range(4)]
    pivot = [None] * 4
    for k in range(4):
        pivot[k] = jnp.where(m[k, k] > 4e-7, 1.0 / m[k, k], 0.0)
        for i in range(k + 1, 4):
            f = m[i, k] * pivot[k]
            for j in range(k, 4):
                m[i, j] = m[i, j] - f * m[k, j]
            g[i] = g[i] - f * g[k]
    c = [None] * 4
    for k in (3, 2, 1, 0):
        t = g[k]
        for j in range(k + 1, 4):
            t = t - m[k, j] * c[j]
        c[k] = t * pivot[k]
    c = [c[k] * scale[k] for k in range(4)]

    for x in range(cx + 1):
        for s in range(2):
            v = sum(c[k][s : s + 1] * ref[s, x + DEPTH] for k, ref in ((1, p1), (2, p2), (3, p3)))
            both[s, x] = v + c[0][s : s + 1] * p0[s, x + DEPTH]
    rows = lax.broadcasted_iota(jnp.int32, (cy, nz), 0)
    cols = lax.broadcasted_iota(jnp.int32, (cy, nz), 1)
    in_x = jnp.where(lax.axis_index("gx") == lax.axis_size("gx") - 1, 0.0, 1.0)
    end_y = lax.axis_index("gy") == lax.axis_size("gy") - 1
    in_y = jnp.where((rows == cy - 1) & end_y, 0.0, 1.0)
    in_z = jnp.where(cols == nz - 1, 0.0, 1.0)
    for x in range(cx):
        p, a = both[0, x], both[1, x]
        pot, adj = p[:cy], a[:cy]
        pot_ref[x] = pot
        adj_ref[x] = adj
        along = -(adj - both[1, x + 1][:cy]) * (pot - both[0, x + 1][:cy])
        sens_ref[0, x] = along * in_x if x == cx - 1 else along
        sens_ref[1, x] = -(adj - up_y(a)[:cy]) * (pot - up_y(p)[:cy]) * in_y
        sens_ref[2, x] = -(adj - up_z(adj)) * (pot - up_z(pot)) * in_z


def body(bond_mask, levels, electrode, leakage, source, weight):
    cx, cy, nz = leakage.shape
    shape = (cx, cy, nz)
    given = (levels, bond_mask, electrode, leakage, source, weight)
    nx, ny = lax.axis_size("gx"), lax.axis_size("gy")
    vmem = pl.BlockSpec(memory_space=pltpu.VMEM)
    slots = jax.ShapeDtypeStruct((SLOTS + SPARE, cy, nz), jnp.float32)
    strip = jax.ShapeDtypeStruct((6, cx, DEPTH, nz), jnp.float32)
    fields, x_one, x_two, y_one, y_two = pl.pallas_call(
        pack_kernel,
        out_shape=[jax.ShapeDtypeStruct((6, *shape), jnp.float32), slots, slots, strip, strip],
        in_specs=[pl.BlockSpec(memory_space=pltpu.HBM)] * 6,
        out_specs=[vmem] * 5,
        scratch_shapes=[
            pltpu.SMEM(levels.shape, jnp.float32),
            pltpu.VMEM(bond_mask.shape, jnp.int32),
            pltpu.VMEM(electrode.shape, jnp.int32),
            pltpu.VMEM(shape, jnp.float32),
            pltpu.VMEM(shape, jnp.float32),
            pltpu.VMEM(shape, jnp.float32),
            pltpu.SemaphoreType.DMA((14,)),
        ],
        compiler_params=pltpu.CompilerParams(vmem_limit_bytes=24 * 2**20),
        name="pack",
    )(*(pltpu.with_memory_space_constraint(a, pltpu.HBM) for a in given))
    x_one, x_two = traded(x_one, x_two, "gx")
    y_one, y_two = traded(y_one, y_two, "gy")
    side = pl.pallas_call(
        side_kernel,
        out_shape=jax.ShapeDtypeStruct((2 * SLOTS, cy, nz), jnp.float32),
        in_specs=[vmem] * 2,
        out_specs=vmem,
        compiler_params=pltpu.CompilerParams(vmem_limit_bytes=24 * 2**20),
        cost_estimate=pl.CostEstimate(flops=10**11, bytes_accessed=10**8, transcendentals=0),
        name="side",
    )(x_one, x_two)
    rest = jax.ShapeDtypeStruct((TILES, 2 * DEPTH, nz), jnp.float32)
    rim, c_one, c_two = pl.pallas_call(
        turn_kernel,
        out_shape=[jax.ShapeDtypeStruct((6, cx, 2 * DEPTH, nz), jnp.float32), rest, rest],
        in_specs=[vmem] * 2,
        out_specs=[vmem] * 3,
        compiler_params=pltpu.CompilerParams(vmem_limit_bytes=24 * 2**20),
        name="turn",
    )(y_one, y_two)
    c_one, c_two = traded(c_one, c_two, "gx")
    planes, rows = cx + 2 * DEPTH, cy + 2 * DEPTH
    block = jax.ShapeDtypeStruct((2, planes, rows, nz), jnp.float32)
    parts = nx * ny
    sums, *basis = pl.pallas_call(
        basis_kernel,
        out_shape=[jax.ShapeDtypeStruct((parts // 8, 8, 128), jnp.float32)] + [block] * 4,
        in_specs=[vmem] * 5,
        out_specs=[vmem] * 5,
        scratch_shapes=[
            pltpu.VMEM((planes, rows, nz), jnp.float32),
            pltpu.VMEM((planes, rows, nz), jnp.float32),
            pltpu.VMEM((2, planes, rows, nz), jnp.float32),
            pltpu.VMEM((2, 6, 2, 2 * DEPTH, nz), jnp.float32),
        ],
        compiler_params=pltpu.CompilerParams(vmem_limit_bytes=24 * 2**20),
        name="basis",
    )(fields, side, rim, c_one, c_two)
    gathered = lax.all_to_all(sums.reshape(parts, 1, 128), ("gx", "gy"), 0, 0, tiled=True)
    return pl.pallas_call(
        combine_kernel,
        out_shape=[
            jax.ShapeDtypeStruct(shape, jnp.float32),
            jax.ShapeDtypeStruct(shape, jnp.float32),
            jax.ShapeDtypeStruct((3, *shape), jnp.float32),
        ],
        in_specs=[vmem] * 5,
        out_specs=[vmem] * 3,
        scratch_shapes=[pltpu.VMEM((2, cx + 1, rows, nz), jnp.float32)],
        compiler_params=pltpu.CompilerParams(vmem_limit_bytes=24 * 2**20),
        name="combine",
    )(gathered.reshape(parts // 8, 8, 128), *basis)


def solution(mesh):
    return jax.shard_map(
        body,
        mesh=mesh,
        in_specs=(
            P(None, "gx", "gy", None),
            P(),
            P(None, "gx", "gy"),
            P("gx", "gy", None),
            P("gx", "gy", None),
            P("gx", "gy", None),
        ),
        out_specs=(P("gx", "gy", None), P("gx", "gy", None), P(None, "gx", "gy", None)),
        check_vma=False,
    )
```

```python
import functools

import jax
import jax.numpy as jnp
from jax import lax
from jax.experimental import pallas as pl
from jax.experimental.pallas import tpu as pltpu
from jax.sharding import PartitionSpec as P

DEPTH = 4
SUMS = 14
SLOTS = 21
TILES = 12
SIDE = 64


def traded(one, two, axis):
    count = lax.axis_size(axis)
    inner = [(i, i ^ 1) for i in range(count)]
    outer = [(i, i + 1) for i in range(1, count - 1, 2)]
    outer = outer + [(target, source) for source, target in outer]
    two = lax.ppermute(two, axis, outer)
    return lax.ppermute(one, axis, inner), two


def is_even(axis):
    return lax.axis_index(axis) % 2 == 0


def up_y(v):
    return pltpu.roll(v, v.shape[0] - 1, 0)


def dn_y(v):
    return pltpu.roll(v, 1, 0)


def up_z(v):
    return pltpu.roll(v, v.shape[1] - 1, 1)


def dn_z(v):
    return pltpu.roll(v, 1, 1)


def slot(f, j, above=False):
    start = (0, 4, 8, 12, 15, 18)[f]
    return start + j - (0 if above or f < 3 else 1)


def slab():
    out = []
    for f in range(6):
        count = DEPTH if f < 3 else 3
        out += [(f, k, k - count) for k in range(count)]
    return out


def pack_kernel(level_hbm, mask_hbm, elec_hbm, leak_hbm, source_hbm, weight_hbm,
                own_ref, x_one, x_two, y_one, y_two,
                level_ref, mask_ref, elec_ref, leak_ref, source_ref, weight_ref, sems):
    cx, cy, nz = leak_ref.shape
    ix, iy = lax.axis_index("gx"), lax.axis_index("gy")
    whole = [(level_hbm, level_ref), (elec_hbm, elec_ref)]
    first = [pltpu.make_async_copy(a, b, sems.at[k]) for k, (a, b) in enumerate(whole)]
    half = cx // 2
    parts = []
    for h in range(2):
        at = pl.ds(h * half, half)
        pairs = [(mask_hbm.at[d, at], mask_ref.at[d, at]) for d in range(3)]
        pairs += [(leak_hbm.at[at], leak_ref.at[at]), (source_hbm.at[at], source_ref.at[at])]
        pairs += [(weight_hbm.at[at], weight_ref.at[at])]
        parts.append(
            [pltpu.make_async_copy(a, b, sems.at[2 + 6 * h + k]) for k, (a, b) in enumerate(pairs)]
        )
    for copy in first + parts[0] + parts[1]:
        copy.start()
    for copy in first + parts[0]:
        copy.wait()
    rows = lax.broadcasted_iota(jnp.int32, (cy, nz), 0)
    cols = lax.broadcasted_iota(jnp.int32, (cy, nz), 1)
    even_x, even_y = is_even("gx"), is_even("gy")
    keep_x = jnp.where(ix == lax.axis_size("gx") - 1, 0.0, 1.0)
    keep_y = jnp.where((rows == cy - 1) & (iy == lax.axis_size("gy") - 1), 0.0, 1.0)
    keep_z = jnp.where(cols == nz - 1, 0.0, 1.0)
    square = lax.broadcasted_iota(jnp.int32, (cy, cy), 0) == lax.broadcasted_iota(jnp.int32, (cy, cy), 1)
    before = None
    for x in range(cx):
        if x == half:
            for copy in parts[1]:
                copy.wait()
        c = [
            jnp.where(mask_ref[d, x] == 1, level_ref[1, d], level_ref[0, d]) for d in range(3)
        ]
        if x == cx - 1:
            c[0] = c[0] * keep_x
        c[1] = c[1] * keep_y
        c[2] = c[2] * keep_z
        ends = []
        for e, at in ((0, 0), (1, nz - 1)):
            row = jnp.broadcast_to(elec_ref[e, x : x + 1].astype(jnp.float32), (cy, cy))
            column = jnp.sum(jnp.where(square, row, 0.0), axis=1, keepdims=True)
            ends.append(jnp.where(cols == at, column, 0.0))
        part = leak_ref[x] + ends[0] + ends[1] + c[0] + c[1] + c[2]
        part = part + jnp.where(rows == 0, 0.0, dn_y(c[1])) + dn_z(c[2])
        if x:
            part = part + before
        before = c[0]
        own_ref[0, x] = source_ref[x] + ends[0]
        own_ref[1, x] = weight_ref[x] + ends[1]
        own_ref[2, x] = part
        for d in range(3):
            own_ref[3 + d, x] = c[d]
    for k, (f, above, below) in enumerate(slab()):
        low, high = own_ref[f, above], own_ref[f, cx + below]
        x_one[k] = jnp.where(even_x, high, low)
        x_two[k] = jnp.where(even_x, low, high)
    for f in range(6):
        for x in range(cx):
            low, high = own_ref[f, x, :DEPTH], own_ref[f, x, cy - DEPTH :]
            y_one[f, x] = jnp.where(even_y, high, low)
            y_two[f, x] = jnp.where(even_y, low, high)


def turn_kernel(y_two, y_one, rim_ref, c_one, c_two):
    cx = y_one.shape[1]
    even_x, even_y = is_even("gx"), is_even("gy")
    for f in range(6):
        for x in range(cx):
            one, two = y_one[f, x], y_two[f, x]
            low, high = jnp.where(even_y, two, one), jnp.where(even_y, one, two)
            rim_ref[f, x] = jnp.concatenate([high, low], axis=0)
    at = lax.broadcasted_iota(jnp.int32, (8, 128), 0)
    for f in range(6):
        tiles = []
        for order in ((0, 1, 2, 3), (cx - 1, cx - 2, cx - 3, cx - 4)):
            near = rim_ref[f, order[0]]
            if f == 4:
                near = jnp.where(at == 4, pltpu.roll(rim_ref[f, order[3]], 5, 0), near)
            third = rim_ref[f, order[2]]
            far = jnp.where(at == 5, pltpu.roll(third, 6, 0), rim_ref[f, order[1]])
            far = jnp.where(at == 2, pltpu.roll(third, 2, 0), far)
            tiles.append((near, far))
        for k in range(2):
            low, high = tiles[0][k], tiles[1][k]
            c_one[2 * f + k] = jnp.where(even_x, high, low)
            c_two[2 * f + k] = jnp.where(even_x, low, high)


def basis_kernel(own_ref, rim_ref, x_two, x_one, c_two, c_one,
                 sums_ref, p0, p1, p2, p3, diag, inv, v0, side_ref, corner_ref):
    cx = own_ref.shape[2]
    planes = cx + 2 * DEPTH
    even = is_even("gx")
    at = lax.broadcasted_iota(jnp.int32, (8, 128), 0)
    for k in range(SLOTS):
        side_ref[k] = jnp.where(even, x_two[k], x_one[k])
        side_ref[SLOTS + k] = jnp.where(even, x_one[k], x_two[k])
    for f in range(6):
        for k in range(2):
            one, two = c_one[2 * f + k], c_two[2 * f + k]
            corner_ref[0, f, k] = jnp.where(even, two, one)
            corner_ref[1, f, k] = jnp.where(even, one, two)

    def corner(f, above, depth):
        if depth == 1:
            return corner_ref[above, f, 0]
        if depth == 2:
            return corner_ref[above, f, 1]
        if depth == 3:
            t = corner_ref[above, f, 1]
            return jnp.where(at == 0, pltpu.roll(t, 6, 0), pltpu.roll(t, 2, 0))
        if f == 4:
            return pltpu.roll(corner_ref[above, f, 0], 3, 0)
        return jnp.zeros((8, 128), jnp.float32)

    def field(f, x):
        if DEPTH <= x < DEPTH + cx:
            return jnp.concatenate([own_ref[f, x - DEPTH], rim_ref[f, x - DEPTH]], axis=0)
        above = int(x >= DEPTH)
        depth = x - DEPTH - cx + 1 if above else DEPTH - x
        if f > 2 and depth > 3:
            flat = jnp.zeros((cx, 128), jnp.float32)
        elif above:
            flat = side_ref[SLOTS + slot(f, depth - 1, above=True)]
        else:
            flat = side_ref[slot(f, x)]
        return jnp.concatenate([flat, corner(f, above, depth)], axis=0)

    rows = lax.broadcasted_iota(jnp.int32, (cx + 2 * DEPTH, 128), 0)
    seam = (rows == 0) | (rows == cx)
    for x in range(1, planes):
        d = field(2, x) + jnp.where(seam, dn_y(field(4, x)), 0.0)
        if x in (DEPTH, DEPTH + cx):
            d = d + field(3, x - 1)
        r = jnp.where(d > 0.0, 1.0 / d, 0.0)
        diag[x] = d
        inv[x] = r
        v0[0, x] = field(0, x) * r
        v0[1, x] = field(1, x) * r

    def jacobi(ref, x):
        above, below = field(3, x), field(3, x - 1)
        cy, cz, r = field(4, x), field(5, x), inv[x]
        out = []
        for s in range(2):
            v = ref[s, x]
            beside = above * ref[s, x + 1] + below * ref[s, x - 1]
            beside = beside + cy * up_y(v) + dn_y(cy * v)
            beside = beside + cz * up_z(v) + dn_z(cz * v)
            out.append((v, r * beside))
        return out

    for x in range(2, planes - 1):
        for s, (v, w) in enumerate(jacobi(v0, x)):
            p0[s, x] = v + w
            p1[s, x] = v - w
    for x in range(3, planes - 2):
        for s, (v, w) in enumerate(jacobi(p0, x)):
            p2[s, x] = v - w
    for x in range(4, planes - 3):
        for s, (v, w) in enumerate(jacobi(p2, x)):
            p3[s, x] = w

    def folded(t):
        return sum(t[8 * i : 8 * i + 8] for i in range(1, cx // 8)) + t[0:8] if cx > 8 else t

    totals = [jnp.zeros((8, 128), jnp.float32)] * (2 * SUMS)
    for s in range(2):
        for x in range(DEPTH, planes - DEPTH):
            d = diag[x][:cx]
            gx, gy, gz = own_ref[3, x - DEPTH], own_ref[4, x - DEPTH], own_ref[5, x - DEPTH]
            b = own_ref[s, x - DEPTH]
            q = p3[s, x]
            q0, q1, q2, q3 = p0[s, x][:cx], p1[s, x][:cx], p2[s, x][:cx], q[:cx]
            a0 = d * q2
            a1 = d * (2.0 * q1 - q2)
            a2 = d * (q2 - q3)
            links = gx * p3[s, x + 1][:cx] + gy * up_y(q)[:cx] + gz * up_z(q3)
            terms = [a0 * q0, a0 * q1, a0 * q2, a0 * q3, a1 * q1, a1 * q2, a1 * q3]
            terms += [a2 * q2, a2 * q3, (d * q3 - 2.0 * links) * q3]
            terms += [b * q0, b * q1, b * q2, b * q3]
            for k, t in enumerate(terms):
                totals[s * SUMS + k] = totals[s * SUMS + k] + folded(t)
    lanes = lax.broadcasted_iota(jnp.int32, (1, 128), 1)
    row = jnp.zeros((1, 128), jnp.float32)
    for k, t in enumerate(totals):
        at = k if k < SUMS else SIDE + k - SUMS
        whole = jnp.sum(jnp.sum(t, axis=0, keepdims=True), axis=1, keepdims=True)
        row = row + jnp.where(lanes == at, whole, 0.0)
    for k in range(sums_ref.shape[0]):
        sums_ref[k] = jnp.broadcast_to(row, sums_ref.shape[1:])


def combine_kernel(sums_ref, p0, p1, p2, p3, pot_ref, adj_ref, sens_ref, both):
    cx, cy, nz = pot_ref.shape
    total = jnp.sum(jnp.sum(sums_ref[...], axis=0), axis=0, keepdims=True)
    pair = jnp.concatenate([total, pltpu.roll(total, 128 - SIDE, 1)], axis=0)
    lanes = lax.broadcasted_iota(jnp.int32, (2, 128), 1)
    picked = [jnp.sum(jnp.where(lanes == k, pair, 0.0), axis=1, keepdims=True) for k in range(SUMS)]
    energy = {}
    order = iter(picked)
    for i in range(4):
        for j in range(i, 4):
            energy[i, j] = energy[j, i] = next(order)
    right = [next(order) for _ in range(4)]
    scale = [1.0 / jnp.sqrt(energy[i, i]) for i in range(4)]
    m = {(i, j): energy[i, j] * scale[i] * scale[j] for i in range(4) for j in range(4)}
    g = [right[i] * scale[i] for i in range(4)]
    pivot = [None] * 4
    for k in range(4):
        pivot[k] = jnp.where(m[k, k] > 4e-7, 1.0 / m[k, k], 0.0)
        for i in range(k + 1, 4):
            f = m[i, k] * pivot[k]
            for j in range(k, 4):
                m[i, j] = m[i, j] - f * m[k, j]
            g[i] = g[i] - f * g[k]
    c = [None] * 4
    for k in (3, 2, 1, 0):
        t = g[k]
        for j in range(k + 1, 4):
            t = t - m[k, j] * c[j]
        c[k] = t * pivot[k]
    c = [c[k] * scale[k] for k in range(4)]

    for x in range(cx + 1):
        for s in range(2):
            v = sum(c[k][s : s + 1] * ref[s, x + DEPTH] for k, ref in ((1, p1), (2, p2), (3, p3)))
            both[s, x] = v + c[0][s : s + 1] * p0[s, x + DEPTH]
    rows = lax.broadcasted_iota(jnp.int32, (cy, nz), 0)
    cols = lax.broadcasted_iota(jnp.int32, (cy, nz), 1)
    in_x = jnp.where(lax.axis_index("gx") == lax.axis_size("gx") - 1, 0.0, 1.0)
    end_y = lax.axis_index("gy") == lax.axis_size("gy") - 1
    in_y = jnp.where((rows == cy - 1) & end_y, 0.0, 1.0)
    in_z = jnp.where(cols == nz - 1, 0.0, 1.0)
    for x in range(cx):
        p, a = both[0, x], both[1, x]
        pot, adj = p[:cy], a[:cy]
        pot_ref[x] = pot
        adj_ref[x] = adj
        along = -(adj - both[1, x + 1][:cy]) * (pot - both[0, x + 1][:cy])
        sens_ref[0, x] = along * in_x if x == cx - 1 else along
        sens_ref[1, x] = -(adj - up_y(a)[:cy]) * (pot - up_y(p)[:cy]) * in_y
        sens_ref[2, x] = -(adj - up_z(adj)) * (pot - up_z(pot)) * in_z


def body(bond_mask, levels, electrode, leakage, source, weight):
    cx, cy, nz = leakage.shape
    shape = (cx, cy, nz)
    given = (levels, bond_mask, electrode, leakage, source, weight)
    nx, ny = lax.axis_size("gx"), lax.axis_size("gy")
    vmem = pl.BlockSpec(memory_space=pltpu.VMEM)
    slots = jax.ShapeDtypeStruct((SLOTS, cy, nz), jnp.float32)
    strip = jax.ShapeDtypeStruct((6, cx, DEPTH, nz), jnp.float32)
    fields, x_one, x_two, y_one, y_two = pl.pallas_call(
        pack_kernel,
        out_shape=[jax.ShapeDtypeStruct((6, *shape), jnp.float32), slots, slots, strip, strip],
        in_specs=[pl.BlockSpec(memory_space=pltpu.HBM)] * 6,
        out_specs=[vmem] * 5,
        scratch_shapes=[
            pltpu.SMEM(levels.shape, jnp.float32),
            pltpu.VMEM(bond_mask.shape, jnp.int32),
            pltpu.VMEM(electrode.shape, jnp.int32),
            pltpu.VMEM(shape, jnp.float32),
            pltpu.VMEM(shape, jnp.float32),
            pltpu.VMEM(shape, jnp.float32),
            pltpu.SemaphoreType.DMA((14,)),
        ],
        compiler_params=pltpu.CompilerParams(vmem_limit_bytes=24 * 2**20),
        name="pack",
    )(*(pltpu.with_memory_space_constraint(a, pltpu.HBM) for a in given))
    x_one, x_two = traded(x_one, x_two, "gx")
    y_one, y_two = traded(y_one, y_two, "gy")
    rest = jax.ShapeDtypeStruct((TILES, 2 * DEPTH, nz), jnp.float32)
    rim, c_one, c_two = pl.pallas_call(
        turn_kernel,
        out_shape=[jax.ShapeDtypeStruct((6, cx, 2 * DEPTH, nz), jnp.float32), rest, rest],
        in_specs=[vmem] * 2,
        out_specs=[vmem] * 3,
        compiler_params=pltpu.CompilerParams(vmem_limit_bytes=24 * 2**20),
        name="turn",
    )(y_two, y_one)
    c_one, c_two = traded(c_one, c_two, "gx")
    planes, rows = cx + 2 * DEPTH, cy + 2 * DEPTH
    block = jax.ShapeDtypeStruct((2, planes, rows, nz), jnp.float32)
    parts = nx * ny
    sums, *basis = pl.pallas_call(
        basis_kernel,
        out_shape=[jax.ShapeDtypeStruct((parts // 8, 8, 128), jnp.float32)] + [block] * 4,
        in_specs=[vmem] * 6,
        out_specs=[vmem] * 5,
        scratch_shapes=[
            pltpu.VMEM((planes, rows, nz), jnp.float32),
            pltpu.VMEM((planes, rows, nz), jnp.float32),
            pltpu.VMEM((2, planes, rows, nz), jnp.float32),
            pltpu.VMEM((2 * SLOTS, cy, nz), jnp.float32),
            pltpu.VMEM((2, 6, 2, 2 * DEPTH, nz), jnp.float32),
        ],
        compiler_params=pltpu.CompilerParams(vmem_limit_bytes=24 * 2**20),
        name="basis",
    )(fields, rim, x_two, x_one, c_two, c_one)
    gathered = lax.all_to_all(sums.reshape(parts, 1, 128), ("gx", "gy"), 0, 0, tiled=True)
    return pl.pallas_call(
        combine_kernel,
        out_shape=[
            jax.ShapeDtypeStruct(shape, jnp.float32),
            jax.ShapeDtypeStruct(shape, jnp.float32),
            jax.ShapeDtypeStruct((3, *shape), jnp.float32),
        ],
        in_specs=[vmem] * 5,
        out_specs=[vmem] * 3,
        scratch_shapes=[pltpu.VMEM((2, cx + 1, rows, nz), jnp.float32)],
        compiler_params=pltpu.CompilerParams(vmem_limit_bytes=24 * 2**20),
        name="combine",
    )(gathered.reshape(parts // 8, 8, 128), *basis)


def solution(mesh):
    return jax.shard_map(
        body,
        mesh=mesh,
        in_specs=(
            P(None, "gx", "gy", None),
            P(),
            P(None, "gx", "gy"),
            P("gx", "gy", None),
            P("gx", "gy", None),
            P("gx", "gy", None),
        ),
        out_specs=(P("gx", "gy", None), P("gx", "gy", None), P(None, "gx", "gy", None)),
        check_vma=False,
    )
```

```python
import functools

import jax
import jax.numpy as jnp
from jax import lax
from jax.experimental import pallas as pl
from jax.experimental.pallas import tpu as pltpu
from jax.sharding import PartitionSpec as P

DEPTH = 4
SUMS = 14
SLOTS = 15
TILES = 16
SIDE = 64


def traded(one, two, axis):
    count = lax.axis_size(axis)
    inner = [(i, i ^ 1) for i in range(count)]
    outer = [(i, i + 1) for i in range(1, count - 1, 2)]
    outer = outer + [(target, source) for source, target in outer]
    two = lax.ppermute(two, axis, outer)
    return lax.ppermute(one, axis, inner), two


def is_even(axis):
    return lax.axis_index(axis) % 2 == 0


def up_y(v):
    return pltpu.roll(v, v.shape[0] - 1, 0)


def dn_y(v):
    return pltpu.roll(v, 1, 0)


def up_z(v):
    return pltpu.roll(v, v.shape[1] - 1, 1)


def dn_z(v):
    return pltpu.roll(v, 1, 1)


def slot(f, j):
    return (0, 3, 6, 9, 11, 13)[f] + j


def sent(f):
    return 3 if f < 3 else 2


def slab():
    out = []
    for f in range(6):
        count = sent(f)
        out += [(f, k, k - count) for k in range(count)]
    return out


def pack_kernel(level_hbm, mask_hbm, elec_hbm, leak_hbm, source_hbm, weight_hbm,
                own_ref, x_one, x_two, y_one, y_two,
                level_ref, mask_ref, elec_ref, leak_ref, source_ref, weight_ref, sems):
    cx, cy, nz = leak_ref.shape
    ix, iy = lax.axis_index("gx"), lax.axis_index("gy")
    whole = [(level_hbm, level_ref), (elec_hbm, elec_ref)]
    first = [pltpu.make_async_copy(a, b, sems.at[k]) for k, (a, b) in enumerate(whole)]
    half = cx // 2
    parts = []
    for h in range(2):
        at = pl.ds(h * half, half)
        pairs = [(mask_hbm.at[d, at], mask_ref.at[d, at]) for d in range(3)]
        pairs += [(leak_hbm.at[at], leak_ref.at[at]), (source_hbm.at[at], source_ref.at[at])]
        pairs += [(weight_hbm.at[at], weight_ref.at[at])]
        parts.append(
            [pltpu.make_async_copy(a, b, sems.at[2 + 6 * h + k]) for k, (a, b) in enumerate(pairs)]
        )
    for copy in first + parts[0] + parts[1]:
        copy.start()
    for copy in first + parts[0]:
        copy.wait()
    rows = lax.broadcasted_iota(jnp.int32, (cy, nz), 0)
    cols = lax.broadcasted_iota(jnp.int32, (cy, nz), 1)
    even_x, even_y = is_even("gx"), is_even("gy")
    keep_x = jnp.where(ix == lax.axis_size("gx") - 1, 0.0, 1.0)
    keep_y = jnp.where((rows == cy - 1) & (iy == lax.axis_size("gy") - 1), 0.0, 1.0)
    keep_z = jnp.where(cols == nz - 1, 0.0, 1.0)
    square = lax.broadcasted_iota(jnp.int32, (cy, cy), 0) == lax.broadcasted_iota(jnp.int32, (cy, cy), 1)
    before = None
    for x in range(cx):
        if x == half:
            for copy in parts[1]:
                copy.wait()
        c = [
            jnp.where(mask_ref[d, x] == 1, level_ref[1, d], level_ref[0, d]) for d in range(3)
        ]
        if x == cx - 1:
            c[0] = c[0] * keep_x
        c[1] = c[1] * keep_y
        c[2] = c[2] * keep_z
        ends = []
        for e, at in ((0, 0), (1, nz - 1)):
            row = jnp.broadcast_to(elec_ref[e, x : x + 1].astype(jnp.float32), (cy, cy))
            column = jnp.sum(jnp.where(square, row, 0.0), axis=1, keepdims=True)
            ends.append(jnp.where(cols == at, column, 0.0))
        part = leak_ref[x] + ends[0] + ends[1] + c[0] + c[1] + c[2]
        part = part + jnp.where(rows == 0, 0.0, dn_y(c[1])) + dn_z(c[2])
        if x:
            part = part + before
        before = c[0]
        own_ref[0, x] = source_ref[x] + ends[0]
        own_ref[1, x] = weight_ref[x] + ends[1]
        own_ref[2, x] = part
        for d in range(3):
            own_ref[3 + d, x] = c[d]
    for k, (f, above, below) in enumerate(slab()):
        low, high = own_ref[f, above], own_ref[f, cx + below]
        x_one[k] = jnp.where(even_x, high, low)
        x_two[k] = jnp.where(even_x, low, high)
    for f in range(6):
        for x in range(cx):
            low, high = own_ref[f, x, :DEPTH], own_ref[f, x, cy - DEPTH :]
            y_one[f, x] = jnp.where(even_y, high, low)
            y_two[f, x] = jnp.where(even_y, low, high)


def neighbours(v, above, below, next_x, last_x, cy, cz):
    beside = above * next_x + below * last_x
    beside = beside + cy * up_y(v) + dn_y(cy * v)
    return beside + cz * up_z(v) + dn_z(cz * v)


def turn_kernel(y_two, y_one, own_ref, rim_ref, c_one, c_two):
    cx, cy = own_ref.shape[1:3]
    even_x, even_y = is_even("gx"), is_even("gy")
    for f in range(6):
        for x in range(cx):
            one, two = y_one[f, x], y_two[f, x]
            low, high = jnp.where(even_y, two, one), jnp.where(even_y, one, two)
            rim_ref[f, x] = jnp.concatenate([high, low], axis=0)
    def field(f, x):
        return jnp.concatenate([own_ref[f, x], rim_ref[f, x]], axis=0)

    rows = lax.broadcasted_iota(jnp.int32, (cx + 2 * DEPTH, 128), 0)
    seam = (rows == 0) | (rows == cx)

    def scaled(x):
        d = field(2, x) + jnp.where(seam, dn_y(field(4, x)), 0.0)
        r = jnp.where(d > 0.0, 1.0 / d, 0.0)
        return r, [field(s, x) * r for s in range(2)]

    summed = []
    for x in (2, cx - 2):
        (_, last), (r, here), (_, after) = scaled(x - 1), scaled(x), scaled(x + 1)
        row = []
        for s in range(2):
            v = here[s]
            beside = neighbours(v, field(3, x), field(3, x - 1), after[s], last[s], field(4, x), field(5, x))
            row.append(v + r * beside)
        summed.append(row)
    at = lax.broadcasted_iota(jnp.int32, (8, 128), 0)
    for f in range(6):
        tiles = []
        for e, order in enumerate(((0, 1, 2), (cx - 1, cx - 2, cx - 3))):
            near = rim_ref[f, order[0]]
            third = rim_ref[f, order[2]]
            far = jnp.where(at == 5, pltpu.roll(third, 6, 0), rim_ref[f, order[1]])
            far = jnp.where(at == 2, pltpu.roll(third, 2, 0), far)
            if f == 4:
                far = jnp.where(at == 3, pltpu.roll(own_ref[f, order[2], cy - 8 :], 4, 0), far)
            if f < 2:
                far = jnp.where(at == 3, pltpu.roll(summed[e][f][cy : cy + 8], 3, 0), far)
            tiles.append((near, far))
        for k in range(2):
            low, high = tiles[0][k], tiles[1][k]
            c_one[2 * f + k] = jnp.where(even_x, high, low)
            c_two[2 * f + k] = jnp.where(even_x, low, high)
    for s in range(2):
        for k in range(2):
            low, high = (summed[e][s][8 * k : 8 * k + 8] for e in range(2))
            c_one[12 + 2 * s + k] = jnp.where(even_x, high, low)
            c_two[12 + 2 * s + k] = jnp.where(even_x, low, high)


def basis_kernel(own_ref, rim_ref, x_two, x_one, c_two, c_one,
                 sums_ref, p0, p1, p2, p3, diag, inv, v0, side_ref, corner_ref):
    cx = own_ref.shape[2]
    planes = cx + 2 * DEPTH
    even = is_even("gx")
    at = lax.broadcasted_iota(jnp.int32, (8, 128), 0)
    for k in range(SLOTS):
        side_ref[k] = jnp.where(even, x_two[k], x_one[k])
        side_ref[SLOTS + k] = jnp.where(even, x_one[k], x_two[k])
    for f in range(6):
        for k in range(2):
            one, two = c_one[2 * f + k], c_two[2 * f + k]
            corner_ref[0, f, k] = jnp.where(even, two, one)
            corner_ref[1, f, k] = jnp.where(even, one, two)

    def corner(f, above, depth):
        if depth == 1:
            return corner_ref[above, f, 0]
        if depth == 2:
            return corner_ref[above, f, 1]
        t = corner_ref[above, f, 1]
        return jnp.where(at == 0, pltpu.roll(t, 6, 0), pltpu.roll(t, 2, 0))

    def field(f, x):
        if DEPTH <= x < DEPTH + cx:
            return jnp.concatenate([own_ref[f, x - DEPTH], rim_ref[f, x - DEPTH]], axis=0)
        above = int(x >= DEPTH)
        depth = x - DEPTH - cx + 1 if above else DEPTH - x
        count = sent(f)
        if depth > count:
            edge = jnp.where(at == 7, pltpu.roll(corner_ref[above, f, 1], 4, 0), 0.0)
            flat = jnp.concatenate([jnp.zeros((cx - 8, 128), jnp.float32), edge], axis=0)
        else:
            flat = side_ref[SLOTS + slot(f, depth - 1) if above else slot(f, count - depth)]
        return jnp.concatenate([flat, corner(f, above, depth)], axis=0)

    rows = lax.broadcasted_iota(jnp.int32, (cx + 2 * DEPTH, 128), 0)
    seam = (rows == 0) | (rows == cx)
    for x in range(2, planes - 1):
        d = field(2, x) + jnp.where(seam, dn_y(field(4, x)), 0.0)
        if x in (DEPTH, DEPTH + cx):
            d = d + field(3, x - 1)
        r = jnp.where(d > 0.0, 1.0 / d, 0.0)
        diag[x] = d
        inv[x] = r
        v0[0, x] = field(0, x) * r
        v0[1, x] = field(1, x) * r

    def jacobi(ref, x):
        above, below = field(3, x), field(3, x - 1)
        cy, cz, r = field(4, x), field(5, x), inv[x]
        out = []
        for s in range(2):
            v = ref[s, x]
            beside = neighbours(v, above, below, ref[s, x + 1], ref[s, x - 1], cy, cz)
            out.append((v, r * beside))
        return out

    for x in range(3, planes - 2):
        for s, (v, w) in enumerate(jacobi(v0, x)):
            p0[s, x] = v + w
            p1[s, x] = v - w
    for s in range(2):
        beyond = [jnp.where(at == 0, pltpu.roll(corner_ref[e, s, 1], 5, 0), 0.0) for e in range(2)]
        one = [c_one[12 + 2 * s + k] for k in range(2)]
        two = [c_two[12 + 2 * s + k] for k in range(2)]
        below = [jnp.where(even, b, a) for a, b in zip(one, two)]
        above = [jnp.where(even, a, b) for a, b in zip(one, two)]
        p0[s, 2] = jnp.concatenate(below + beyond[:1], axis=0)
        p0[s, planes - 2] = jnp.concatenate(above + beyond[1:], axis=0)
    for x in range(3, planes - 2):
        for s, (v, w) in enumerate(jacobi(p0, x)):
            p2[s, x] = v - w
    for x in range(4, planes - 3):
        for s, (v, w) in enumerate(jacobi(p2, x)):
            p3[s, x] = w

    def folded(t):
        return sum(t[8 * i : 8 * i + 8] for i in range(1, cx // 8)) + t[0:8] if cx > 8 else t

    totals = [jnp.zeros((8, 128), jnp.float32)] * (2 * SUMS)
    for s in range(2):
        for x in range(DEPTH, planes - DEPTH):
            d = diag[x][:cx]
            gx, gy, gz = own_ref[3, x - DEPTH], own_ref[4, x - DEPTH], own_ref[5, x - DEPTH]
            b = own_ref[s, x - DEPTH]
            q = p3[s, x]
            q0, q1, q2, q3 = p0[s, x][:cx], p1[s, x][:cx], p2[s, x][:cx], q[:cx]
            a0 = d * q2
            a1 = d * (2.0 * q1 - q2)
            a2 = d * (q2 - q3)
            links = gx * p3[s, x + 1][:cx] + gy * up_y(q)[:cx] + gz * up_z(q3)
            terms = [a0 * q0, a0 * q1, a0 * q2, a0 * q3, a1 * q1, a1 * q2, a1 * q3]
            terms += [a2 * q2, a2 * q3, (d * q3 - 2.0 * links) * q3]
            terms += [b * q0, b * q1, b * q2, b * q3]
            for k, t in enumerate(terms):
                totals[s * SUMS + k] = totals[s * SUMS + k] + folded(t)
    lanes = lax.broadcasted_iota(jnp.int32, (1, 128), 1)
    row = jnp.zeros((1, 128), jnp.float32)
    for k, t in enumerate(totals):
        at = k if k < SUMS else SIDE + k - SUMS
        whole = jnp.sum(jnp.sum(t, axis=0, keepdims=True), axis=1, keepdims=True)
        row = row + jnp.where(lanes == at, whole, 0.0)
    for k in range(sums_ref.shape[0]):
        sums_ref[k] = jnp.broadcast_to(row, sums_ref.shape[1:])


def combine_kernel(sums_ref, p0, p1, p2, p3, pot_ref, adj_ref, sens_ref, both):
    cx, cy, nz = pot_ref.shape
    total = jnp.sum(jnp.sum(sums_ref[...], axis=0), axis=0, keepdims=True)
    pair = jnp.concatenate([total, pltpu.roll(total, 128 - SIDE, 1)], axis=0)
    lanes = lax.broadcasted_iota(jnp.int32, (2, 128), 1)
    picked = [jnp.sum(jnp.where(lanes == k, pair, 0.0), axis=1, keepdims=True) for k in range(SUMS)]
    energy = {}
    order = iter(picked)
    for i in range(4):
        for j in range(i, 4):
            energy[i, j] = energy[j, i] = next(order)
    right = [next(order) for _ in range(4)]
    scale = [1.0 / jnp.sqrt(energy[i, i]) for i in range(4)]
    m = {(i, j): energy[i, j] * scale[i] * scale[j] for i in range(4) for j in range(4)}
    g = [right[i] * scale[i] for i in range(4)]
    pivot = [None] * 4
    for k in range(4):
        pivot[k] = jnp.where(m[k, k] > 4e-7, 1.0 / m[k, k], 0.0)
        for i in range(k + 1, 4):
            f = m[i, k] * pivot[k]
            for j in range(k, 4):
                m[i, j] = m[i, j] - f * m[k, j]
            g[i] = g[i] - f * g[k]
    c = [None] * 4
    for k in (3, 2, 1, 0):
        t = g[k]
        for j in range(k + 1, 4):
            t = t - m[k, j] * c[j]
        c[k] = t * pivot[k]
    c = [c[k] * scale[k] for k in range(4)]

    for x in range(cx + 1):
        for s in range(2):
            v = sum(c[k][s : s + 1] * ref[s, x + DEPTH] for k, ref in ((1, p1), (2, p2), (3, p3)))
            both[s, x] = v + c[0][s : s + 1] * p0[s, x + DEPTH]
    rows = lax.broadcasted_iota(jnp.int32, (cy, nz), 0)
    cols = lax.broadcasted_iota(jnp.int32, (cy, nz), 1)
    in_x = jnp.where(lax.axis_index("gx") == lax.axis_size("gx") - 1, 0.0, 1.0)
    end_y = lax.axis_index("gy") == lax.axis_size("gy") - 1
    in_y = jnp.where((rows == cy - 1) & end_y, 0.0, 1.0)
    in_z = jnp.where(cols == nz - 1, 0.0, 1.0)
    for x in range(cx):
        p, a = both[0, x], both[1, x]
        pot, adj = p[:cy], a[:cy]
        pot_ref[x] = pot
        adj_ref[x] = adj
        along = -(adj - both[1, x + 1][:cy]) * (pot - both[0, x + 1][:cy])
        sens_ref[0, x] = along * in_x if x == cx - 1 else along
        sens_ref[1, x] = -(adj - up_y(a)[:cy]) * (pot - up_y(p)[:cy]) * in_y
        sens_ref[2, x] = -(adj - up_z(adj)) * (pot - up_z(pot)) * in_z


def body(bond_mask, levels, electrode, leakage, source, weight):
    cx, cy, nz = leakage.shape
    shape = (cx, cy, nz)
    given = (levels, bond_mask, electrode, leakage, source, weight)
    nx, ny = lax.axis_size("gx"), lax.axis_size("gy")
    vmem = pl.BlockSpec(memory_space=pltpu.VMEM)
    slots = jax.ShapeDtypeStruct((SLOTS, cy, nz), jnp.float32)
    strip = jax.ShapeDtypeStruct((6, cx, DEPTH, nz), jnp.float32)
    fields, x_one, x_two, y_one, y_two = pl.pallas_call(
        pack_kernel,
        out_shape=[jax.ShapeDtypeStruct((6, *shape), jnp.float32), slots, slots, strip, strip],
        in_specs=[pl.BlockSpec(memory_space=pltpu.HBM)] * 6,
        out_specs=[vmem] * 5,
        scratch_shapes=[
            pltpu.SMEM(levels.shape, jnp.float32),
            pltpu.VMEM(bond_mask.shape, jnp.int32),
            pltpu.VMEM(electrode.shape, jnp.int32),
            pltpu.VMEM(shape, jnp.float32),
            pltpu.VMEM(shape, jnp.float32),
            pltpu.VMEM(shape, jnp.float32),
            pltpu.SemaphoreType.DMA((14,)),
        ],
        compiler_params=pltpu.CompilerParams(vmem_limit_bytes=24 * 2**20),
        name="pack",
    )(*(pltpu.with_memory_space_constraint(a, pltpu.HBM) for a in given))
    x_one, x_two = traded(x_one, x_two, "gx")
    y_one, y_two = traded(y_one, y_two, "gy")
    rest = jax.ShapeDtypeStruct((TILES, 2 * DEPTH, nz), jnp.float32)
    rim, c_one, c_two = pl.pallas_call(
        turn_kernel,
        out_shape=[jax.ShapeDtypeStruct((6, cx, 2 * DEPTH, nz), jnp.float32), rest, rest],
        in_specs=[vmem] * 3,
        out_specs=[vmem] * 3,
        compiler_params=pltpu.CompilerParams(vmem_limit_bytes=24 * 2**20),
        name="turn",
    )(y_two, y_one, fields)
    c_one, c_two = traded(c_one, c_two, "gx")
    planes, rows = cx + 2 * DEPTH, cy + 2 * DEPTH
    block = jax.ShapeDtypeStruct((2, planes, rows, nz), jnp.float32)
    parts = nx * ny
    sums, *basis = pl.pallas_call(
        basis_kernel,
        out_shape=[jax.ShapeDtypeStruct((parts // 8, 8, 128), jnp.float32)] + [block] * 4,
        in_specs=[vmem] * 6,
        out_specs=[vmem] * 5,
        scratch_shapes=[
            pltpu.VMEM((planes, rows, nz), jnp.float32),
            pltpu.VMEM((planes, rows, nz), jnp.float32),
            pltpu.VMEM((2, planes, rows, nz), jnp.float32),
            pltpu.VMEM((2 * SLOTS, cy, nz), jnp.float32),
            pltpu.VMEM((2, 6, 2, 2 * DEPTH, nz), jnp.float32),
        ],
        compiler_params=pltpu.CompilerParams(vmem_limit_bytes=24 * 2**20),
        name="basis",
    )(fields, rim, x_two, x_one, c_two, c_one)
    gathered = lax.all_to_all(sums.reshape(parts, 1, 128), ("gx", "gy"), 0, 0, tiled=True)
    return pl.pallas_call(
        combine_kernel,
        out_shape=[
            jax.ShapeDtypeStruct(shape, jnp.float32),
            jax.ShapeDtypeStruct(shape, jnp.float32),
            jax.ShapeDtypeStruct((3, *shape), jnp.float32),
        ],
        in_specs=[vmem] * 5,
        out_specs=[vmem] * 3,
        scratch_shapes=[pltpu.VMEM((2, cx + 1, rows, nz), jnp.float32)],
        compiler_params=pltpu.CompilerParams(vmem_limit_bytes=24 * 2**20),
        name="combine",
    )(gathered.reshape(parts // 8, 8, 128), *basis)


def solution(mesh):
    return jax.shard_map(
        body,
        mesh=mesh,
        in_specs=(
            P(None, "gx", "gy", None),
            P(),
            P(None, "gx", "gy"),
            P("gx", "gy", None),
            P("gx", "gy", None),
            P("gx", "gy", None),
        ),
        out_specs=(P("gx", "gy", None), P("gx", "gy", None), P(None, "gx", "gy", None)),
        check_vma=False,
    )
```

```python
import functools

import jax
import jax.numpy as jnp
from jax import lax
from jax.experimental import pallas as pl
from jax.experimental.pallas import tpu as pltpu
from jax.sharding import PartitionSpec as P

DEPTH = 4
SUMS = 14
SLOTS = 15
TILES = 16
SIDE = 64


def trade_one(value, axis):
    return lax.ppermute(value, axis, [(i, i ^ 1) for i in range(lax.axis_size(axis))])


def trade_two(value, axis):
    outer = [(i, i + 1) for i in range(1, lax.axis_size(axis) - 1, 2)]
    return lax.ppermute(value, axis, outer + [(target, source) for source, target in outer])


def is_even(axis):
    return lax.axis_index(axis) % 2 == 0


def up_y(v):
    return pltpu.roll(v, v.shape[0] - 1, 0)


def dn_y(v):
    return pltpu.roll(v, 1, 0)


def up_z(v):
    return pltpu.roll(v, v.shape[1] - 1, 1)


def dn_z(v):
    return pltpu.roll(v, 1, 1)


def slot(f, j):
    return (0, 3, 6, 9, 11, 13)[f] + j


def sent(f):
    return 3 if f < 3 else 2


def slab():
    out = []
    for f in range(6):
        count = sent(f)
        out += [(f, k, k - count) for k in range(count)]
    return out


def pack_kernel(level_hbm, mask_hbm, elec_hbm, leak_hbm, source_hbm, weight_hbm,
                own_ref, x_one, x_two, y_one, y_two,
                level_ref, mask_ref, elec_ref, leak_ref, source_ref, weight_ref, sems):
    cx, cy, nz = leak_ref.shape
    ix, iy = lax.axis_index("gx"), lax.axis_index("gy")
    whole = [(level_hbm, level_ref), (elec_hbm, elec_ref)]
    first = [pltpu.make_async_copy(a, b, sems.at[k]) for k, (a, b) in enumerate(whole)]
    half = cx // 2
    parts = []
    for h in range(2):
        at = pl.ds(h * half, half)
        pairs = [(mask_hbm.at[d, at], mask_ref.at[d, at]) for d in range(3)]
        pairs += [(leak_hbm.at[at], leak_ref.at[at]), (source_hbm.at[at], source_ref.at[at])]
        pairs += [(weight_hbm.at[at], weight_ref.at[at])]
        parts.append(
            [pltpu.make_async_copy(a, b, sems.at[2 + 6 * h + k]) for k, (a, b) in enumerate(pairs)]
        )
    for copy in first + parts[0] + parts[1]:
        copy.start()
    for copy in first + parts[0]:
        copy.wait()
    rows = lax.broadcasted_iota(jnp.int32, (cy, nz), 0)
    cols = lax.broadcasted_iota(jnp.int32, (cy, nz), 1)
    even_x, even_y = is_even("gx"), is_even("gy")
    keep_x = jnp.where(ix == lax.axis_size("gx") - 1, 0.0, 1.0)
    keep_y = jnp.where((rows == cy - 1) & (iy == lax.axis_size("gy") - 1), 0.0, 1.0)
    keep_z = jnp.where(cols == nz - 1, 0.0, 1.0)
    square = lax.broadcasted_iota(jnp.int32, (cy, cy), 0) == lax.broadcasted_iota(jnp.int32, (cy, cy), 1)
    before = None
    for x in range(cx):
        if x == half:
            for copy in parts[1]:
                copy.wait()
        c = [
            jnp.where(mask_ref[d, x] == 1, level_ref[1, d], level_ref[0, d]) for d in range(3)
        ]
        if x == cx - 1:
            c[0] = c[0] * keep_x
        c[1] = c[1] * keep_y
        c[2] = c[2] * keep_z
        ends = []
        for e, at in ((0, 0), (1, nz - 1)):
            row = jnp.broadcast_to(elec_ref[e, x : x + 1].astype(jnp.float32), (cy, cy))
            column = jnp.sum(jnp.where(square, row, 0.0), axis=1, keepdims=True)
            ends.append(jnp.where(cols == at, column, 0.0))
        part = leak_ref[x] + ends[0] + ends[1] + c[0] + c[1] + c[2]
        part = part + jnp.where(rows == 0, 0.0, dn_y(c[1])) + dn_z(c[2])
        if x:
            part = part + before
        before = c[0]
        own_ref[0, x] = source_ref[x] + ends[0]
        own_ref[1, x] = weight_ref[x] + ends[1]
        own_ref[2, x] = part
        for d in range(3):
            own_ref[3 + d, x] = c[d]
    for k, (f, above, below) in enumerate(slab()):
        low, high = own_ref[f, above], own_ref[f, cx + below]
        x_one[k] = jnp.where(even_x, high, low)
        x_two[k] = jnp.where(even_x, low, high)
    for f in range(6):
        for x in range(cx):
            low, high = own_ref[f, x, :DEPTH], own_ref[f, x, cy - DEPTH :]
            y_one[f, x] = jnp.where(even_y, high, low)
            y_two[f, x] = jnp.where(even_y, low, high)


def neighbours(v, above, below, next_x, last_x, cy, cz):
    beside = above * next_x + below * last_x
    beside = beside + cy * up_y(v) + dn_y(cy * v)
    return beside + cz * up_z(v) + dn_z(cz * v)


def turn_kernel(y_two, y_one, own_ref, x_one, rim_ref, one_ref, c_two):
    cx, cy = own_ref.shape[1:3]
    c_one = one_ref.at[pl.ds(2 * SLOTS, TILES)]
    for k in range(SLOTS):
        one_ref[2 * k] = x_one[k, :8]
        one_ref[2 * k + 1] = x_one[k, 8:]
    even_x, even_y = is_even("gx"), is_even("gy")
    for f in range(6):
        for x in range(cx):
            one, two = y_one[f, x], y_two[f, x]
            low, high = jnp.where(even_y, two, one), jnp.where(even_y, one, two)
            rim_ref[f, x] = jnp.concatenate([high, low], axis=0)
    def field(f, x):
        return jnp.concatenate([own_ref[f, x], rim_ref[f, x]], axis=0)

    rows = lax.broadcasted_iota(jnp.int32, (cx + 2 * DEPTH, 128), 0)
    seam = (rows == 0) | (rows == cx)

    def scaled(x):
        d = field(2, x) + jnp.where(seam, dn_y(field(4, x)), 0.0)
        r = jnp.where(d > 0.0, 1.0 / d, 0.0)
        return r, [field(s, x) * r for s in range(2)]

    summed = []
    for x in (2, cx - 2):
        (_, last), (r, here), (_, after) = scaled(x - 1), scaled(x), scaled(x + 1)
        row = []
        for s in range(2):
            v = here[s]
            beside = neighbours(v, field(3, x), field(3, x - 1), after[s], last[s], field(4, x), field(5, x))
            row.append(v + r * beside)
        summed.append(row)
    at = lax.broadcasted_iota(jnp.int32, (8, 128), 0)
    for f in range(6):
        tiles = []
        for e, order in enumerate(((0, 1, 2), (cx - 1, cx - 2, cx - 3))):
            near = rim_ref[f, order[0]]
            third = rim_ref[f, order[2]]
            far = jnp.where(at == 5, pltpu.roll(third, 6, 0), rim_ref[f, order[1]])
            far = jnp.where(at == 2, pltpu.roll(third, 2, 0), far)
            if f == 4:
                far = jnp.where(at == 3, pltpu.roll(own_ref[f, order[2], cy - 8 :], 4, 0), far)
            if f < 2:
                far = jnp.where(at == 3, pltpu.roll(summed[e][f][cy : cy + 8], 3, 0), far)
            tiles.append((near, far))
        for k in range(2):
            low, high = tiles[0][k], tiles[1][k]
            c_one[2 * f + k] = jnp.where(even_x, high, low)
            c_two[2 * f + k] = jnp.where(even_x, low, high)
    for s in range(2):
        for k in range(2):
            low, high = (summed[e][s][8 * k : 8 * k + 8] for e in range(2))
            c_one[12 + 2 * s + k] = jnp.where(even_x, high, low)
            c_two[12 + 2 * s + k] = jnp.where(even_x, low, high)


def slab_kernel(given_ref, out_ref):
    out_ref[...] = given_ref[...]


def far_kernel(slab_hbm, given_ref, out_ref):
    out_ref[...] = given_ref[...]


def basis_kernel(own_ref, rim_ref, x_two, c_two, one_ref,
                 sums_ref, p0, p1, p2, p3, diag, inv, v0, side_ref, corner_ref):
    cx = own_ref.shape[2]
    planes = cx + 2 * DEPTH
    even = is_even("gx")
    at = lax.broadcasted_iota(jnp.int32, (8, 128), 0)
    c_one = one_ref.at[pl.ds(2 * SLOTS, TILES)]
    for k in range(SLOTS):
        one = jnp.concatenate([one_ref[2 * k], one_ref[2 * k + 1]], axis=0)
        side_ref[k] = jnp.where(even, x_two[k], one)
        side_ref[SLOTS + k] = jnp.where(even, one, x_two[k])
    for f in range(6):
        for k in range(2):
            one, two = c_one[2 * f + k], c_two[2 * f + k]
            corner_ref[0, f, k] = jnp.where(even, two, one)
            corner_ref[1, f, k] = jnp.where(even, one, two)

    def corner(f, above, depth):
        if depth == 1:
            return corner_ref[above, f, 0]
        if depth == 2:
            return corner_ref[above, f, 1]
        t = corner_ref[above, f, 1]
        return jnp.where(at == 0, pltpu.roll(t, 6, 0), pltpu.roll(t, 2, 0))

    def field(f, x):
        if DEPTH <= x < DEPTH + cx:
            return jnp.concatenate([own_ref[f, x - DEPTH], rim_ref[f, x - DEPTH]], axis=0)
        above = int(x >= DEPTH)
        depth = x - DEPTH - cx + 1 if above else DEPTH - x
        count = sent(f)
        if depth > count:
            edge = jnp.where(at == 7, pltpu.roll(corner_ref[above, f, 1], 4, 0), 0.0)
            flat = jnp.concatenate([jnp.zeros((cx - 8, 128), jnp.float32), edge], axis=0)
        else:
            flat = side_ref[SLOTS + slot(f, depth - 1) if above else slot(f, count - depth)]
        return jnp.concatenate([flat, corner(f, above, depth)], axis=0)

    rows = lax.broadcasted_iota(jnp.int32, (cx + 2 * DEPTH, 128), 0)
    seam = (rows == 0) | (rows == cx)
    for x in range(2, planes - 1):
        d = field(2, x) + jnp.where(seam, dn_y(field(4, x)), 0.0)
        if x in (DEPTH, DEPTH + cx):
            d = d + field(3, x - 1)
        r = jnp.where(d > 0.0, 1.0 / d, 0.0)
        diag[x] = d
        inv[x] = r
        v0[0, x] = field(0, x) * r
        v0[1, x] = field(1, x) * r

    def jacobi(ref, x):
        above, below = field(3, x), field(3, x - 1)
        cy, cz, r = field(4, x), field(5, x), inv[x]
        out = []
        for s in range(2):
            v = ref[s, x]
            beside = neighbours(v, above, below, ref[s, x + 1], ref[s, x - 1], cy, cz)
            out.append((v, r * beside))
        return out

    for x in range(3, planes - 2):
        for s, (v, w) in enumerate(jacobi(v0, x)):
            p0[s, x] = v + w
            p1[s, x] = v - w
    for s in range(2):
        beyond = [jnp.where(at == 0, pltpu.roll(corner_ref[e, s, 1], 5, 0), 0.0) for e in range(2)]
        one = [c_one[12 + 2 * s + k] for k in range(2)]
        two = [c_two[12 + 2 * s + k] for k in range(2)]
        below = [jnp.where(even, b, a) for a, b in zip(one, two)]
        above = [jnp.where(even, a, b) for a, b in zip(one, two)]
        p0[s, 2] = jnp.concatenate(below + beyond[:1], axis=0)
        p0[s, planes - 2] = jnp.concatenate(above + beyond[1:], axis=0)
    for x in range(3, planes - 2):
        for s, (v, w) in enumerate(jacobi(p0, x)):
            p2[s, x] = v - w
    for x in range(4, planes - 3):
        for s, (v, w) in enumerate(jacobi(p2, x)):
            p3[s, x] = w

    def folded(t):
        return sum(t[8 * i : 8 * i + 8] for i in range(1, cx // 8)) + t[0:8] if cx > 8 else t

    totals = [jnp.zeros((8, 128), jnp.float32)] * (2 * SUMS)
    for s in range(2):
        for x in range(DEPTH, planes - DEPTH):
            d = diag[x][:cx]
            gx, gy, gz = own_ref[3, x - DEPTH], own_ref[4, x - DEPTH], own_ref[5, x - DEPTH]
            b = own_ref[s, x - DEPTH]
            q = p3[s, x]
            q0, q1, q2, q3 = p0[s, x][:cx], p1[s, x][:cx], p2[s, x][:cx], q[:cx]
            a0 = d * q2
            a1 = d * (2.0 * q1 - q2)
            a2 = d * (q2 - q3)
            links = gx * p3[s, x + 1][:cx] + gy * up_y(q)[:cx] + gz * up_z(q3)
            terms = [a0 * q0, a0 * q1, a0 * q2, a0 * q3, a1 * q1, a1 * q2, a1 * q3]
            terms += [a2 * q2, a2 * q3, (d * q3 - 2.0 * links) * q3]
            terms += [b * q0, b * q1, b * q2, b * q3]
            for k, t in enumerate(terms):
                totals[s * SUMS + k] = totals[s * SUMS + k] + folded(t)
    lanes = lax.broadcasted_iota(jnp.int32, (1, 128), 1)
    row = jnp.zeros((1, 128), jnp.float32)
    for k, t in enumerate(totals):
        at = k if k < SUMS else SIDE + k - SUMS
        whole = jnp.sum(jnp.sum(t, axis=0, keepdims=True), axis=1, keepdims=True)
        row = row + jnp.where(lanes == at, whole, 0.0)
    for k in range(sums_ref.shape[0]):
        sums_ref[k] = jnp.broadcast_to(row, sums_ref.shape[1:])


def combine_kernel(sums_ref, p0, p1, p2, p3, pot_ref, adj_ref, sens_ref, both):
    cx, cy, nz = pot_ref.shape
    total = jnp.sum(jnp.sum(sums_ref[...], axis=0), axis=0, keepdims=True)
    pair = jnp.concatenate([total, pltpu.roll(total, 128 - SIDE, 1)], axis=0)
    lanes = lax.broadcasted_iota(jnp.int32, (2, 128), 1)
    picked = [jnp.sum(jnp.where(lanes == k, pair, 0.0), axis=1, keepdims=True) for k in range(SUMS)]
    energy = {}
    order = iter(picked)
    for i in range(4):
        for j in range(i, 4):
            energy[i, j] = energy[j, i] = next(order)
    right = [next(order) for _ in range(4)]
    scale = [1.0 / jnp.sqrt(energy[i, i]) for i in range(4)]
    m = {(i, j): energy[i, j] * scale[i] * scale[j] for i in range(4) for j in range(4)}
    g = [right[i] * scale[i] for i in range(4)]
    pivot = [None] * 4
    for k in range(4):
        pivot[k] = jnp.where(m[k, k] > 4e-7, 1.0 / m[k, k], 0.0)
        for i in range(k + 1, 4):
            f = m[i, k] * pivot[k]
            for j in range(k, 4):
                m[i, j] = m[i, j] - f * m[k, j]
            g[i] = g[i] - f * g[k]
    c = [None] * 4
    for k in (3, 2, 1, 0):
        t = g[k]
        for j in range(k + 1, 4):
            t = t - m[k, j] * c[j]
        c[k] = t * pivot[k]
    c = [c[k] * scale[k] for k in range(4)]

    for x in range(cx + 1):
        for s in range(2):
            v = sum(c[k][s : s + 1] * ref[s, x + DEPTH] for k, ref in ((1, p1), (2, p2), (3, p3)))
            both[s, x] = v + c[0][s : s + 1] * p0[s, x + DEPTH]
    rows = lax.broadcasted_iota(jnp.int32, (cy, nz), 0)
    cols = lax.broadcasted_iota(jnp.int32, (cy, nz), 1)
    in_x = jnp.where(lax.axis_index("gx") == lax.axis_size("gx") - 1, 0.0, 1.0)
    end_y = lax.axis_index("gy") == lax.axis_size("gy") - 1
    in_y = jnp.where((rows == cy - 1) & end_y, 0.0, 1.0)
    in_z = jnp.where(cols == nz - 1, 0.0, 1.0)
    for x in range(cx):
        p, a = both[0, x], both[1, x]
        pot, adj = p[:cy], a[:cy]
        pot_ref[x] = pot
        adj_ref[x] = adj
        along = -(adj - both[1, x + 1][:cy]) * (pot - both[0, x + 1][:cy])
        sens_ref[0, x] = along * in_x if x == cx - 1 else along
        sens_ref[1, x] = -(adj - up_y(a)[:cy]) * (pot - up_y(p)[:cy]) * in_y
        sens_ref[2, x] = -(adj - up_z(adj)) * (pot - up_z(pot)) * in_z


def body(bond_mask, levels, electrode, leakage, source, weight):
    cx, cy, nz = leakage.shape
    shape = (cx, cy, nz)
    given = (levels, bond_mask, electrode, leakage, source, weight)
    nx, ny = lax.axis_size("gx"), lax.axis_size("gy")
    vmem = pl.BlockSpec(memory_space=pltpu.VMEM)
    slots = jax.ShapeDtypeStruct((SLOTS, cy, nz), jnp.float32)
    strip = jax.ShapeDtypeStruct((6, cx, DEPTH, nz), jnp.float32)
    fields, x_one, x_two, y_one, y_two = pl.pallas_call(
        pack_kernel,
        out_shape=[jax.ShapeDtypeStruct((6, *shape), jnp.float32), slots, slots, strip, strip],
        in_specs=[pl.BlockSpec(memory_space=pltpu.HBM)] * 6,
        out_specs=[vmem] * 5,
        scratch_shapes=[
            pltpu.SMEM(levels.shape, jnp.float32),
            pltpu.VMEM(bond_mask.shape, jnp.int32),
            pltpu.VMEM(electrode.shape, jnp.int32),
            pltpu.VMEM(shape, jnp.float32),
            pltpu.VMEM(shape, jnp.float32),
            pltpu.VMEM(shape, jnp.float32),
            pltpu.SemaphoreType.DMA((14,)),
        ],
        compiler_params=pltpu.CompilerParams(vmem_limit_bytes=24 * 2**20),
        name="pack",
    )(*(pltpu.with_memory_space_constraint(a, pltpu.HBM) for a in given))
    x_two = trade_two(x_two, "gx")
    y_one, y_two = trade_one(y_one, "gy"), trade_two(y_two, "gy")
    rest = jax.ShapeDtypeStruct((TILES, 2 * DEPTH, nz), jnp.float32)
    near = jax.ShapeDtypeStruct((2 * SLOTS + TILES, 2 * DEPTH, nz), jnp.float32)
    rim, one, c_two = pl.pallas_call(
        turn_kernel,
        out_shape=[jax.ShapeDtypeStruct((6, cx, 2 * DEPTH, nz), jnp.float32), near, rest],
        in_specs=[vmem] * 4,
        out_specs=[vmem] * 3,
        compiler_params=pltpu.CompilerParams(vmem_limit_bytes=24 * 2**20),
        name="turn",
    )(y_two, y_one, fields, x_one)
    c_two = trade_two(c_two, "gx")
    hint = pl.CostEstimate(flops=10**11, bytes_accessed=10**8, transcendentals=0)
    x_two = pl.pallas_call(
        slab_kernel,
        out_shape=slots,
        in_specs=[vmem],
        out_specs=vmem,
        compiler_params=pltpu.CompilerParams(vmem_limit_bytes=24 * 2**20),
        cost_estimate=hint,
        name="slab",
    )(x_two)
    c_two = pl.pallas_call(
        far_kernel,
        out_shape=rest,
        in_specs=[pl.BlockSpec(memory_space=pl.ANY), vmem],
        out_specs=vmem,
        compiler_params=pltpu.CompilerParams(vmem_limit_bytes=24 * 2**20),
        cost_estimate=hint,
        name="far",
    )(x_two, c_two)
    one = trade_one(one, "gx")
    planes, rows = cx + 2 * DEPTH, cy + 2 * DEPTH
    block = jax.ShapeDtypeStruct((2, planes, rows, nz), jnp.float32)
    parts = nx * ny
    sums, *basis = pl.pallas_call(
        basis_kernel,
        out_shape=[jax.ShapeDtypeStruct((parts // 8, 8, 128), jnp.float32)] + [block] * 4,
        in_specs=[vmem] * 5,
        out_specs=[vmem] * 5,
        scratch_shapes=[
            pltpu.VMEM((planes, rows, nz), jnp.float32),
            pltpu.VMEM((planes, rows, nz), jnp.float32),
            pltpu.VMEM((2, planes, rows, nz), jnp.float32),
            pltpu.VMEM((2 * SLOTS, cy, nz), jnp.float32),
            pltpu.VMEM((2, 6, 2, 2 * DEPTH, nz), jnp.float32),
        ],
        compiler_params=pltpu.CompilerParams(vmem_limit_bytes=24 * 2**20),
        name="basis",
    )(fields, rim, x_two, c_two, one)
    gathered = lax.all_to_all(sums.reshape(parts, 1, 128), ("gx", "gy"), 0, 0, tiled=True)
    return pl.pallas_call(
        combine_kernel,
        out_shape=[
            jax.ShapeDtypeStruct(shape, jnp.float32),
            jax.ShapeDtypeStruct(shape, jnp.float32),
            jax.ShapeDtypeStruct((3, *shape), jnp.float32),
        ],
        in_specs=[vmem] * 5,
        out_specs=[vmem] * 3,
        scratch_shapes=[pltpu.VMEM((2, cx + 1, rows, nz), jnp.float32)],
        compiler_params=pltpu.CompilerParams(vmem_limit_bytes=24 * 2**20),
        name="combine",
    )(gathered.reshape(parts // 8, 8, 128), *basis)


def solution(mesh):
    return jax.shard_map(
        body,
        mesh=mesh,
        in_specs=(
            P(None, "gx", "gy", None),
            P(),
            P(None, "gx", "gy"),
            P("gx", "gy", None),
            P("gx", "gy", None),
            P("gx", "gy", None),
        ),
        out_specs=(P("gx", "gy", None), P("gx", "gy", None), P(None, "gx", "gy", None)),
        check_vma=False,
    )
```

```python
import functools

import jax
import jax.numpy as jnp
from jax import lax
from jax.experimental import pallas as pl
from jax.experimental.pallas import tpu as pltpu
from jax.sharding import PartitionSpec as P

DEPTH = 4
SUMS = 14
SLOTS = 15
TILES = 16
SIDE = 64


def trade_one(value, axis):
    return lax.ppermute(value, axis, [(i, i ^ 1) for i in range(lax.axis_size(axis))])


def trade_two(value, axis):
    outer = [(i, i + 1) for i in range(1, lax.axis_size(axis) - 1, 2)]
    return lax.ppermute(value, axis, outer + [(target, source) for source, target in outer])


def is_even(axis):
    return lax.axis_index(axis) % 2 == 0


def up_y(v):
    return pltpu.roll(v, v.shape[0] - 1, 0)


def dn_y(v):
    return pltpu.roll(v, 1, 0)


def up_z(v):
    return pltpu.roll(v, v.shape[1] - 1, 1)


def dn_z(v):
    return pltpu.roll(v, 1, 1)


def slot(f, j):
    return (0, 3, 6, 9, 11, 13)[f] + j


def sent(f):
    return 3 if f < 3 else 2


def slab():
    out = []
    for f in range(6):
        count = sent(f)
        out += [(f, k, k - count) for k in range(count)]
    return out


def pack_kernel(level_hbm, mask_hbm, elec_hbm, leak_hbm, source_hbm, weight_hbm,
                own_ref, x_one, x_two, y_one, y_two,
                level_ref, mask_ref, elec_ref, leak_ref, source_ref, weight_ref, sems):
    cx, cy, nz = leak_ref.shape
    ix, iy = lax.axis_index("gx"), lax.axis_index("gy")
    whole = [(level_hbm, level_ref), (elec_hbm, elec_ref)]
    first = [pltpu.make_async_copy(a, b, sems.at[k]) for k, (a, b) in enumerate(whole)]
    half = cx // 2
    parts = []
    for h in range(2):
        at = pl.ds(h * half, half)
        pairs = [(mask_hbm.at[d, at], mask_ref.at[d, at]) for d in range(3)]
        pairs += [(leak_hbm.at[at], leak_ref.at[at]), (source_hbm.at[at], source_ref.at[at])]
        pairs += [(weight_hbm.at[at], weight_ref.at[at])]
        parts.append(
            [pltpu.make_async_copy(a, b, sems.at[2 + 6 * h + k]) for k, (a, b) in enumerate(pairs)]
        )
    for copy in first + parts[0] + parts[1]:
        copy.start()
    for copy in first + parts[0]:
        copy.wait()
    rows = lax.broadcasted_iota(jnp.int32, (cy, nz), 0)
    cols = lax.broadcasted_iota(jnp.int32, (cy, nz), 1)
    even_x, even_y = is_even("gx"), is_even("gy")
    keep_x = jnp.where(ix == lax.axis_size("gx") - 1, 0.0, 1.0)
    keep_y = jnp.where((rows == cy - 1) & (iy == lax.axis_size("gy") - 1), 0.0, 1.0)
    keep_z = jnp.where(cols == nz - 1, 0.0, 1.0)
    square = lax.broadcasted_iota(jnp.int32, (cy, cy), 0) == lax.broadcasted_iota(jnp.int32, (cy, cy), 1)
    before = None
    for x in range(cx):
        if x == half:
            for copy in parts[1]:
                copy.wait()
        c = [
            jnp.where(mask_ref[d, x] == 1, level_ref[1, d], level_ref[0, d]) for d in range(3)
        ]
        if x == cx - 1:
            c[0] = c[0] * keep_x
        c[1] = c[1] * keep_y
        c[2] = c[2] * keep_z
        ends = []
        for e, at in ((0, 0), (1, nz - 1)):
            row = jnp.broadcast_to(elec_ref[e, x : x + 1].astype(jnp.float32), (cy, cy))
            column = jnp.sum(jnp.where(square, row, 0.0), axis=1, keepdims=True)
            ends.append(jnp.where(cols == at, column, 0.0))
        part = leak_ref[x] + ends[0] + ends[1] + c[0] + c[1] + c[2]
        part = part + jnp.where(rows == 0, 0.0, dn_y(c[1])) + dn_z(c[2])
        if x:
            part = part + before
        before = c[0]
        own_ref[0, x] = source_ref[x] + ends[0]
        own_ref[1, x] = weight_ref[x] + ends[1]
        own_ref[2, x] = part
        for d in range(3):
            own_ref[3 + d, x] = c[d]
    for k, (f, above, below) in enumerate(slab()):
        low, high = own_ref[f, above], own_ref[f, cx + below]
        x_one[k] = jnp.where(even_x, high, low)
        x_two[k] = jnp.where(even_x, low, high)
    for f in range(6):
        for x in range(cx):
            low, high = own_ref[f, x, :DEPTH], own_ref[f, x, cy - DEPTH :]
            y_one[f, x] = jnp.where(even_y, high, low)
            y_two[f, x] = jnp.where(even_y, low, high)


def neighbours(v, above, below, next_x, last_x, cy, cz):
    beside = above * next_x + below * last_x
    beside = beside + cy * up_y(v) + dn_y(cy * v)
    return beside + cz * up_z(v) + dn_z(cz * v)


def turn_kernel(y_two, y_one, own_ref, x_one, rim_ref, one_ref, c_two):
    cx, cy = own_ref.shape[1:3]
    c_one = one_ref.at[pl.ds(2 * SLOTS, TILES)]
    for k in range(SLOTS):
        one_ref[2 * k] = x_one[k, :8]
        one_ref[2 * k + 1] = x_one[k, 8:]
    even_x, even_y = is_even("gx"), is_even("gy")
    for f in range(6):
        for x in range(cx):
            one, two = y_one[f, x], y_two[f, x]
            low, high = jnp.where(even_y, two, one), jnp.where(even_y, one, two)
            rim_ref[f, x] = jnp.concatenate([high, low], axis=0)
    def field(f, x):
        return jnp.concatenate([own_ref[f, x], rim_ref[f, x]], axis=0)

    rows = lax.broadcasted_iota(jnp.int32, (cx + 2 * DEPTH, 128), 0)
    seam = (rows == 0) | (rows == cx)

    def scaled(x):
        d = field(2, x) + jnp.where(seam, dn_y(field(4, x)), 0.0)
        r = jnp.where(d > 0.0, 1.0 / d, 0.0)
        return r, [field(s, x) * r for s in range(2)]

    summed = []
    for x in (2, cx - 2):
        (_, last), (r, here), (_, after) = scaled(x - 1), scaled(x), scaled(x + 1)
        row = []
        for s in range(2):
            v = here[s]
            beside = neighbours(v, field(3, x), field(3, x - 1), after[s], last[s], field(4, x), field(5, x))
            row.append(v + r * beside)
        summed.append(row)
    at = lax.broadcasted_iota(jnp.int32, (8, 128), 0)
    for f in range(6):
        tiles = []
        for e, order in enumerate(((0, 1, 2), (cx - 1, cx - 2, cx - 3))):
            near = rim_ref[f, order[0]]
            third = rim_ref[f, order[2]]
            far = jnp.where(at == 5, pltpu.roll(third, 6, 0), rim_ref[f, order[1]])
            far = jnp.where(at == 2, pltpu.roll(third, 2, 0), far)
            if f == 4:
                far = jnp.where(at == 3, pltpu.roll(own_ref[f, order[2], cy - 8 :], 4, 0), far)
            if f < 2:
                far = jnp.where(at == 3, pltpu.roll(summed[e][f][cy : cy + 8], 3, 0), far)
            tiles.append((near, far))
        for k in range(2):
            low, high = tiles[0][k], tiles[1][k]
            c_one[2 * f + k] = jnp.where(even_x, high, low)
            c_two[2 * f + k] = jnp.where(even_x, low, high)
    for s in range(2):
        for k in range(2):
            low, high = (summed[e][s][8 * k : 8 * k + 8] for e in range(2))
            c_one[12 + 2 * s + k] = jnp.where(even_x, high, low)
            c_two[12 + 2 * s + k] = jnp.where(even_x, low, high)


def slab_kernel(given_ref, out_ref):
    out_ref[...] = given_ref[...]


def far_kernel(slab_hbm, given_ref, out_ref):
    out_ref[...] = given_ref[...]


def basis_kernel(own_ref, rim_ref, x_two, c_two, one_ref,
                 sums_ref, p0, p1, p2, p3, diag, inv, v0, side_ref, corner_ref):
    cx = own_ref.shape[2]
    planes = cx + 2 * DEPTH
    even = is_even("gx")
    at = lax.broadcasted_iota(jnp.int32, (8, 128), 0)
    c_one = one_ref.at[pl.ds(2 * SLOTS, TILES)]
    for k in range(SLOTS):
        one = jnp.concatenate([one_ref[2 * k], one_ref[2 * k + 1]], axis=0)
        side_ref[k] = jnp.where(even, x_two[k], one)
        side_ref[SLOTS + k] = jnp.where(even, one, x_two[k])
    for f in range(6):
        for k in range(2):
            one, two = c_one[2 * f + k], c_two[2 * f + k]
            corner_ref[0, f, k] = jnp.where(even, two, one)
            corner_ref[1, f, k] = jnp.where(even, one, two)

    def corner(f, above, depth):
        if depth == 1:
            return corner_ref[above, f, 0]
        if depth == 2:
            return corner_ref[above, f, 1]
        t = corner_ref[above, f, 1]
        return jnp.where(at == 0, pltpu.roll(t, 6, 0), pltpu.roll(t, 2, 0))

    def field(f, x):
        if DEPTH <= x < DEPTH + cx:
            return jnp.concatenate([own_ref[f, x - DEPTH], rim_ref[f, x - DEPTH]], axis=0)
        above = int(x >= DEPTH)
        depth = x - DEPTH - cx + 1 if above else DEPTH - x
        count = sent(f)
        if depth > count:
            edge = jnp.where(at == 7, pltpu.roll(corner_ref[above, f, 1], 4, 0), 0.0)
            flat = jnp.concatenate([jnp.zeros((cx - 8, 128), jnp.float32), edge], axis=0)
        else:
            flat = side_ref[SLOTS + slot(f, depth - 1) if above else slot(f, count - depth)]
        return jnp.concatenate([flat, corner(f, above, depth)], axis=0)

    rows = lax.broadcasted_iota(jnp.int32, (cx + 2 * DEPTH, 128), 0)
    seam = (rows == 0) | (rows == cx)
    for x in range(2, planes - 1):
        d = field(2, x) + jnp.where(seam, dn_y(field(4, x)), 0.0)
        if x in (DEPTH, DEPTH + cx):
            d = d + field(3, x - 1)
        r = jnp.where(d > 0.0, 1.0 / d, 0.0)
        diag[x] = d
        inv[x] = r
        v0[0, x] = field(0, x) * r
        v0[1, x] = field(1, x) * r

    def jacobi(ref, x):
        above, below = field(3, x), field(3, x - 1)
        cy, cz, r = field(4, x), field(5, x), inv[x]
        out = []
        for s in range(2):
            v = ref[s, x]
            beside = neighbours(v, above, below, ref[s, x + 1], ref[s, x - 1], cy, cz)
            out.append((v, r * beside))
        return out

    for x in range(3, planes - 2):
        for s, (v, w) in enumerate(jacobi(v0, x)):
            p0[s, x] = v + w
            p1[s, x] = v - w
    for s in range(2):
        beyond = [jnp.where(at == 0, pltpu.roll(corner_ref[e, s, 1], 5, 0), 0.0) for e in range(2)]
        one = [c_one[12 + 2 * s + k] for k in range(2)]
        two = [c_two[12 + 2 * s + k] for k in range(2)]
        below = [jnp.where(even, b, a) for a, b in zip(one, two)]
        above = [jnp.where(even, a, b) for a, b in zip(one, two)]
        p0[s, 2] = jnp.concatenate(below + beyond[:1], axis=0)
        p0[s, planes - 2] = jnp.concatenate(above + beyond[1:], axis=0)
    for x in range(3, planes - 2):
        for s, (v, w) in enumerate(jacobi(p0, x)):
            p2[s, x] = v - w
    for x in range(4, planes - 3):
        for s, (v, w) in enumerate(jacobi(p2, x)):
            p3[s, x] = w

    def folded(t):
        return sum(t[8 * i : 8 * i + 8] for i in range(1, cx // 8)) + t[0:8] if cx > 8 else t

    totals = [jnp.zeros((8, 128), jnp.float32)] * (2 * SUMS)
    for s in range(2):
        for x in range(DEPTH, planes - DEPTH):
            d = diag[x][:cx]
            gx, gy, gz = own_ref[3, x - DEPTH], own_ref[4, x - DEPTH], own_ref[5, x - DEPTH]
            b = own_ref[s, x - DEPTH]
            q = p3[s, x]
            q0, q1, q2, q3 = p0[s, x][:cx], p1[s, x][:cx], p2[s, x][:cx], q[:cx]
            a0 = d * q2
            a1 = d * (2.0 * q1 - q2)
            a2 = d * (q2 - q3)
            links = gx * p3[s, x + 1][:cx] + gy * up_y(q)[:cx] + gz * up_z(q3)
            terms = [a0 * q0, a0 * q1, a0 * q2, a0 * q3, a1 * q1, a1 * q2, a1 * q3]
            terms += [a2 * q2, a2 * q3, (d * q3 - 2.0 * links) * q3]
            terms += [b * q0, b * q1, b * q2, b * q3]
            for k, t in enumerate(terms):
                totals[s * SUMS + k] = totals[s * SUMS + k] + folded(t)
    lanes = lax.broadcasted_iota(jnp.int32, (1, 128), 1)
    row = jnp.zeros((1, 128), jnp.float32)
    for k, t in enumerate(totals):
        at = k if k < SUMS else SIDE + k - SUMS
        whole = jnp.sum(jnp.sum(t, axis=0, keepdims=True), axis=1, keepdims=True)
        row = row + jnp.where(lanes == at, whole, 0.0)
    for k in range(sums_ref.shape[0]):
        sums_ref[k] = jnp.broadcast_to(row, sums_ref.shape[1:])


def combine_kernel(sums_ref, p0, p1, p2, p3, pot_ref, adj_ref, sens_ref, both):
    cx, cy, nz = pot_ref.shape
    total = jnp.sum(jnp.sum(sums_ref[...], axis=0), axis=0, keepdims=True)
    pair = jnp.concatenate([total, pltpu.roll(total, 128 - SIDE, 1)], axis=0)
    lanes = lax.broadcasted_iota(jnp.int32, (2, 128), 1)
    picked = [jnp.sum(jnp.where(lanes == k, pair, 0.0), axis=1, keepdims=True) for k in range(SUMS)]
    energy = {}
    order = iter(picked)
    for i in range(4):
        for j in range(i, 4):
            energy[i, j] = energy[j, i] = next(order)
    right = [next(order) for _ in range(4)]
    scale = [1.0 / jnp.sqrt(energy[i, i]) for i in range(4)]
    m = {(i, j): energy[i, j] * scale[i] * scale[j] for i in range(4) for j in range(4)}
    g = [right[i] * scale[i] for i in range(4)]
    pivot = [None] * 4
    for k in range(4):
        pivot[k] = jnp.where(m[k, k] > 4e-7, 1.0 / m[k, k], 0.0)
        for i in range(k + 1, 4):
            f = m[i, k] * pivot[k]
            for j in range(k, 4):
                m[i, j] = m[i, j] - f * m[k, j]
            g[i] = g[i] - f * g[k]
    c = [None] * 4
    for k in (3, 2, 1, 0):
        t = g[k]
        for j in range(k + 1, 4):
            t = t - m[k, j] * c[j]
        c[k] = t * pivot[k]
    c = [c[k] * scale[k] for k in range(4)]

    for x in range(cx + 1):
        for s in range(2):
            v = sum(c[k][s : s + 1] * ref[s, x + DEPTH] for k, ref in ((1, p1), (2, p2), (3, p3)))
            both[s, x] = v + c[0][s : s + 1] * p0[s, x + DEPTH]
    rows = lax.broadcasted_iota(jnp.int32, (cy, nz), 0)
    cols = lax.broadcasted_iota(jnp.int32, (cy, nz), 1)
    in_x = jnp.where(lax.axis_index("gx") == lax.axis_size("gx") - 1, 0.0, 1.0)
    end_y = lax.axis_index("gy") == lax.axis_size("gy") - 1
    in_y = jnp.where((rows == cy - 1) & end_y, 0.0, 1.0)
    in_z = jnp.where(cols == nz - 1, 0.0, 1.0)
    for x in range(cx):
        p, a = both[0, x], both[1, x]
        pot, adj = p[:cy], a[:cy]
        pot_ref[x] = pot
        adj_ref[x] = adj
        along = -(adj - both[1, x + 1][:cy]) * (pot - both[0, x + 1][:cy])
        sens_ref[0, x] = along * in_x if x == cx - 1 else along
        sens_ref[1, x] = -(adj - up_y(a)[:cy]) * (pot - up_y(p)[:cy]) * in_y
        sens_ref[2, x] = -(adj - up_z(adj)) * (pot - up_z(pot)) * in_z


def body(bond_mask, levels, electrode, leakage, source, weight):
    cx, cy, nz = leakage.shape
    shape = (cx, cy, nz)
    given = (levels, bond_mask, electrode, leakage, source, weight)
    nx, ny = lax.axis_size("gx"), lax.axis_size("gy")
    vmem = pl.BlockSpec(memory_space=pltpu.VMEM)
    slots = jax.ShapeDtypeStruct((SLOTS, cy, nz), jnp.float32)
    strip = jax.ShapeDtypeStruct((6, cx, DEPTH, nz), jnp.float32)
    fields, x_one, x_two, y_one, y_two = pl.pallas_call(
        pack_kernel,
        out_shape=[jax.ShapeDtypeStruct((6, *shape), jnp.float32), slots, slots, strip, strip],
        in_specs=[pl.BlockSpec(memory_space=pltpu.HBM)] * 6,
        out_specs=[vmem] * 5,
        scratch_shapes=[
            pltpu.SMEM(levels.shape, jnp.float32),
            pltpu.VMEM(bond_mask.shape, jnp.int32),
            pltpu.VMEM(electrode.shape, jnp.int32),
            pltpu.VMEM(shape, jnp.float32),
            pltpu.VMEM(shape, jnp.float32),
            pltpu.VMEM(shape, jnp.float32),
            pltpu.SemaphoreType.DMA((14,)),
        ],
        compiler_params=pltpu.CompilerParams(vmem_limit_bytes=24 * 2**20),
        name="pack",
    )(*(pltpu.with_memory_space_constraint(a, pltpu.HBM) for a in given))
    x_two = trade_two(x_two, "gx")
    y_one, y_two = trade_one(y_one, "gy"), trade_two(y_two, "gy")
    rest = jax.ShapeDtypeStruct((TILES, 2 * DEPTH, nz), jnp.float32)
    near = jax.ShapeDtypeStruct((2 * SLOTS + TILES, 2 * DEPTH, nz), jnp.float32)
    rim, one, c_two = pl.pallas_call(
        turn_kernel,
        out_shape=[jax.ShapeDtypeStruct((6, cx, 2 * DEPTH, nz), jnp.float32), near, rest],
        in_specs=[vmem] * 4,
        out_specs=[vmem] * 3,
        compiler_params=pltpu.CompilerParams(vmem_limit_bytes=24 * 2**20),
        name="turn",
    )(y_two, y_one, fields, x_one)
    c_two = trade_two(c_two, "gx")
    hint = pl.CostEstimate(flops=10**10, bytes_accessed=10**6, transcendentals=0)
    x_two = pl.pallas_call(
        slab_kernel,
        out_shape=slots,
        in_specs=[vmem],
        out_specs=vmem,
        compiler_params=pltpu.CompilerParams(vmem_limit_bytes=24 * 2**20),
        cost_estimate=hint,
        name="slab",
    )(x_two)
    c_two = pl.pallas_call(
        far_kernel,
        out_shape=rest,
        in_specs=[pl.BlockSpec(memory_space=pl.ANY), vmem],
        out_specs=vmem,
        compiler_params=pltpu.CompilerParams(vmem_limit_bytes=24 * 2**20),
        cost_estimate=hint,
        name="far",
    )(x_two, c_two)
    one = trade_one(one, "gx")
    planes, rows = cx + 2 * DEPTH, cy + 2 * DEPTH
    block = jax.ShapeDtypeStruct((2, planes, rows, nz), jnp.float32)
    parts = nx * ny
    sums, *basis = pl.pallas_call(
        basis_kernel,
        out_shape=[jax.ShapeDtypeStruct((parts // 8, 8, 128), jnp.float32)] + [block] * 4,
        in_specs=[vmem] * 5,
        out_specs=[vmem] * 5,
        scratch_shapes=[
            pltpu.VMEM((planes, rows, nz), jnp.float32),
            pltpu.VMEM((planes, rows, nz), jnp.float32),
            pltpu.VMEM((2, planes, rows, nz), jnp.float32),
            pltpu.VMEM((2 * SLOTS, cy, nz), jnp.float32),
            pltpu.VMEM((2, 6, 2, 2 * DEPTH, nz), jnp.float32),
        ],
        compiler_params=pltpu.CompilerParams(vmem_limit_bytes=24 * 2**20),
        name="basis",
    )(fields, rim, x_two, c_two, one)
    gathered = lax.all_to_all(sums.reshape(parts, 1, 128), ("gx", "gy"), 0, 0, tiled=True)
    return pl.pallas_call(
        combine_kernel,
        out_shape=[
            jax.ShapeDtypeStruct(shape, jnp.float32),
            jax.ShapeDtypeStruct(shape, jnp.float32),
            jax.ShapeDtypeStruct((3, *shape), jnp.float32),
        ],
        in_specs=[vmem] * 5,
        out_specs=[vmem] * 3,
        scratch_shapes=[pltpu.VMEM((2, cx + 1, rows, nz), jnp.float32)],
        compiler_params=pltpu.CompilerParams(vmem_limit_bytes=24 * 2**20),
        name="combine",
    )(gathered.reshape(parts // 8, 8, 128), *basis)


def solution(mesh):
    return jax.shard_map(
        body,
        mesh=mesh,
        in_specs=(
            P(None, "gx", "gy", None),
            P(),
            P(None, "gx", "gy"),
            P("gx", "gy", None),
            P("gx", "gy", None),
            P("gx", "gy", None),
        ),
        out_specs=(P("gx", "gy", None), P("gx", "gy", None), P(None, "gx", "gy", None)),
        check_vma=False,
    )
```

```python
import functools

import jax
import jax.numpy as jnp
from jax import lax
from jax.experimental import pallas as pl
from jax.experimental.pallas import tpu as pltpu
from jax.sharding import PartitionSpec as P

DEPTH = 4
SUMS = 14
SLOTS = 15
TILES = 16
SIDE = 64


def trade_one(value, axis):
    return lax.ppermute(value, axis, [(i, i ^ 1) for i in range(lax.axis_size(axis))])


def trade_two(value, axis):
    outer = [(i, i + 1) for i in range(1, lax.axis_size(axis) - 1, 2)]
    return lax.ppermute(value, axis, outer + [(target, source) for source, target in outer])


def is_even(axis):
    return lax.axis_index(axis) % 2 == 0


def up_y(v):
    return pltpu.roll(v, v.shape[0] - 1, 0)


def dn_y(v):
    return pltpu.roll(v, 1, 0)


def up_z(v):
    return pltpu.roll(v, v.shape[1] - 1, 1)


def dn_z(v):
    return pltpu.roll(v, 1, 1)


def slot(f, j):
    return (0, 3, 6, 9, 11, 13)[f] + j


def sent(f):
    return 3 if f < 3 else 2


def slab():
    out = []
    for f in range(6):
        count = sent(f)
        out += [(f, k, k - count) for k in range(count)]
    return out


def pack_kernel(level_hbm, mask_hbm, elec_hbm, leak_hbm, source_hbm, weight_hbm,
                own_ref, x_one, x_two, y_one, y_two,
                level_ref, mask_ref, elec_ref, leak_ref, source_ref, weight_ref, sems):
    cx, cy, nz = leak_ref.shape
    ix, iy = lax.axis_index("gx"), lax.axis_index("gy")
    whole = [(level_hbm, level_ref), (elec_hbm, elec_ref)]
    first = [pltpu.make_async_copy(a, b, sems.at[k]) for k, (a, b) in enumerate(whole)]
    half = cx // 2
    parts = []
    for h in range(2):
        at = pl.ds(h * half, half)
        pairs = [(mask_hbm.at[d, at], mask_ref.at[d, at]) for d in range(3)]
        pairs += [(leak_hbm.at[at], leak_ref.at[at]), (source_hbm.at[at], source_ref.at[at])]
        pairs += [(weight_hbm.at[at], weight_ref.at[at])]
        parts.append(
            [pltpu.make_async_copy(a, b, sems.at[2 + 6 * h + k]) for k, (a, b) in enumerate(pairs)]
        )
    for copy in first + parts[0] + parts[1]:
        copy.start()
    for copy in first + parts[0]:
        copy.wait()
    rows = lax.broadcasted_iota(jnp.int32, (cy, nz), 0)
    cols = lax.broadcasted_iota(jnp.int32, (cy, nz), 1)
    even_x, even_y = is_even("gx"), is_even("gy")
    keep_x = jnp.where(ix == lax.axis_size("gx") - 1, 0.0, 1.0)
    keep_y = jnp.where((rows == cy - 1) & (iy == lax.axis_size("gy") - 1), 0.0, 1.0)
    keep_z = jnp.where(cols == nz - 1, 0.0, 1.0)
    square = lax.broadcasted_iota(jnp.int32, (cy, cy), 0) == lax.broadcasted_iota(jnp.int32, (cy, cy), 1)
    before = None
    for x in range(cx):
        if x == half:
            for copy in parts[1]:
                copy.wait()
        c = [
            jnp.where(mask_ref[d, x] == 1, level_ref[1, d], level_ref[0, d]) for d in range(3)
        ]
        if x == cx - 1:
            c[0] = c[0] * keep_x
        c[1] = c[1] * keep_y
        c[2] = c[2] * keep_z
        ends = []
        for e, at in ((0, 0), (1, nz - 1)):
            row = jnp.broadcast_to(elec_ref[e, x : x + 1].astype(jnp.float32), (cy, cy))
            column = jnp.sum(jnp.where(square, row, 0.0), axis=1, keepdims=True)
            ends.append(jnp.where(cols == at, column, 0.0))
        part = leak_ref[x] + ends[0] + ends[1] + c[0] + c[1] + c[2]
        part = part + jnp.where(rows == 0, 0.0, dn_y(c[1])) + dn_z(c[2])
        if x:
            part = part + before
        before = c[0]
        own_ref[0, x] = source_ref[x] + ends[0]
        own_ref[1, x] = weight_ref[x] + ends[1]
        own_ref[2, x] = part
        for d in range(3):
            own_ref[3 + d, x] = c[d]
    for k, (f, above, below) in enumerate(slab()):
        low, high = own_ref[f, above], own_ref[f, cx + below]
        x_one[k] = jnp.where(even_x, high, low)
        x_two[k] = jnp.where(even_x, low, high)
    for f in range(6):
        for x in range(cx):
            low, high = own_ref[f, x, :DEPTH], own_ref[f, x, cy - DEPTH :]
            y_one[f, x] = jnp.where(even_y, high, low)
            y_two[f, x] = jnp.where(even_y, low, high)


def neighbours(v, above, below, next_x, last_x, cy, cz):
    beside = above * next_x + below * last_x
    beside = beside + cy * up_y(v) + dn_y(cy * v)
    return beside + cz * up_z(v) + dn_z(cz * v)


def turn_kernel(y_one, y_two, own_ref, x_one, rim_ref, one_ref, c_two):
    cx, cy = own_ref.shape[1:3]
    c_one = one_ref.at[pl.ds(2 * SLOTS, TILES)]
    for k in range(SLOTS):
        one_ref[2 * k] = x_one[k, :8]
        one_ref[2 * k + 1] = x_one[k, 8:]
    even_x, even_y = is_even("gx"), is_even("gy")
    for f in range(6):
        for x in range(cx):
            one, two = y_one[f, x], y_two[f, x]
            low, high = jnp.where(even_y, two, one), jnp.where(even_y, one, two)
            rim_ref[f, x] = jnp.concatenate([high, low], axis=0)
    def field(f, x):
        return jnp.concatenate([own_ref[f, x], rim_ref[f, x]], axis=0)

    rows = lax.broadcasted_iota(jnp.int32, (cx + 2 * DEPTH, 128), 0)
    seam = (rows == 0) | (rows == cx)

    def scaled(x):
        d = field(2, x) + jnp.where(seam, dn_y(field(4, x)), 0.0)
        r = jnp.where(d > 0.0, 1.0 / d, 0.0)
        return r, [field(s, x) * r for s in range(2)]

    summed = []
    for x in (2, cx - 2):
        (_, last), (r, here), (_, after) = scaled(x - 1), scaled(x), scaled(x + 1)
        row = []
        for s in range(2):
            v = here[s]
            beside = neighbours(v, field(3, x), field(3, x - 1), after[s], last[s], field(4, x), field(5, x))
            row.append(v + r * beside)
        summed.append(row)
    at = lax.broadcasted_iota(jnp.int32, (8, 128), 0)
    for f in range(6):
        tiles = []
        for e, order in enumerate(((0, 1, 2), (cx - 1, cx - 2, cx - 3))):
            near = rim_ref[f, order[0]]
            third = rim_ref[f, order[2]]
            far = jnp.where(at == 5, pltpu.roll(third, 6, 0), rim_ref[f, order[1]])
            far = jnp.where(at == 2, pltpu.roll(third, 2, 0), far)
            if f == 4:
                far = jnp.where(at == 3, pltpu.roll(own_ref[f, order[2], cy - 8 :], 4, 0), far)
            if f < 2:
                far = jnp.where(at == 3, pltpu.roll(summed[e][f][cy : cy + 8], 3, 0), far)
            tiles.append((near, far))
        for k in range(2):
            low, high = tiles[0][k], tiles[1][k]
            c_one[2 * f + k] = jnp.where(even_x, high, low)
            c_two[2 * f + k] = jnp.where(even_x, low, high)
    for s in range(2):
        for k in range(2):
            low, high = (summed[e][s][8 * k : 8 * k + 8] for e in range(2))
            c_one[12 + 2 * s + k] = jnp.where(even_x, high, low)
            c_two[12 + 2 * s + k] = jnp.where(even_x, low, high)


def slab_kernel(given_ref, out_ref):
    out_ref[...] = given_ref[...]


def far_kernel(slab_hbm, given_ref, out_ref):
    out_ref[...] = given_ref[...]


def basis_kernel(own_ref, rim_ref, x_two, c_two, one_ref,
                 sums_ref, p0, p1, p2, p3, diag, inv, v0, side_ref, corner_ref):
    cx = own_ref.shape[2]
    planes = cx + 2 * DEPTH
    even = is_even("gx")
    at = lax.broadcasted_iota(jnp.int32, (8, 128), 0)
    c_one = one_ref.at[pl.ds(2 * SLOTS, TILES)]
    for k in range(SLOTS):
        one = jnp.concatenate([one_ref[2 * k], one_ref[2 * k + 1]], axis=0)
        side_ref[k] = jnp.where(even, x_two[k], one)
        side_ref[SLOTS + k] = jnp.where(even, one, x_two[k])
    for f in range(6):
        for k in range(2):
            one, two = c_one[2 * f + k], c_two[2 * f + k]
            corner_ref[0, f, k] = jnp.where(even, two, one)
            corner_ref[1, f, k] = jnp.where(even, one, two)

    def corner(f, above, depth):
        if depth == 1:
            return corner_ref[above, f, 0]
        if depth == 2:
            return corner_ref[above, f, 1]
        t = corner_ref[above, f, 1]
        return jnp.where(at == 0, pltpu.roll(t, 6, 0), pltpu.roll(t, 2, 0))

    def field(f, x):
        if DEPTH <= x < DEPTH + cx:
            return jnp.concatenate([own_ref[f, x - DEPTH], rim_ref[f, x - DEPTH]], axis=0)
        above = int(x >= DEPTH)
        depth = x - DEPTH - cx + 1 if above else DEPTH - x
        count = sent(f)
        if depth > count:
            edge = jnp.where(at == 7, pltpu.roll(corner_ref[above, f, 1], 4, 0), 0.0)
            flat = jnp.concatenate([jnp.zeros((cx - 8, 128), jnp.float32), edge], axis=0)
        else:
            flat = side_ref[SLOTS + slot(f, depth - 1) if above else slot(f, count - depth)]
        return jnp.concatenate([flat, corner(f, above, depth)], axis=0)

    rows = lax.broadcasted_iota(jnp.int32, (cx + 2 * DEPTH, 128), 0)
    seam = (rows == 0) | (rows == cx)
    for x in range(2, planes - 1):
        d = field(2, x) + jnp.where(seam, dn_y(field(4, x)), 0.0)
        if x in (DEPTH, DEPTH + cx):
            d = d + field(3, x - 1)
        r = jnp.where(d > 0.0, 1.0 / d, 0.0)
        diag[x] = d
        inv[x] = r
        v0[0, x] = field(0, x) * r
        v0[1, x] = field(1, x) * r

    def jacobi(ref, x):
        above, below = field(3, x), field(3, x - 1)
        cy, cz, r = field(4, x), field(5, x), inv[x]
        out = []
        for s in range(2):
            v = ref[s, x]
            beside = neighbours(v, above, below, ref[s, x + 1], ref[s, x - 1], cy, cz)
            out.append((v, r * beside))
        return out

    for x in range(3, planes - 2):
        for s, (v, w) in enumerate(jacobi(v0, x)):
            p0[s, x] = v + w
            p1[s, x] = v - w
    for s in range(2):
        beyond = [jnp.where(at == 0, pltpu.roll(corner_ref[e, s, 1], 5, 0), 0.0) for e in range(2)]
        one = [c_one[12 + 2 * s + k] for k in range(2)]
        two = [c_two[12 + 2 * s + k] for k in range(2)]
        below = [jnp.where(even, b, a) for a, b in zip(one, two)]
        above = [jnp.where(even, a, b) for a, b in zip(one, two)]
        p0[s, 2] = jnp.concatenate(below + beyond[:1], axis=0)
        p0[s, planes - 2] = jnp.concatenate(above + beyond[1:], axis=0)
    for x in range(3, planes - 2):
        for s, (v, w) in enumerate(jacobi(p0, x)):
            p2[s, x] = v - w
    for x in range(4, planes - 3):
        for s, (v, w) in enumerate(jacobi(p2, x)):
            p3[s, x] = w

    def folded(t):
        return sum(t[8 * i : 8 * i + 8] for i in range(1, cx // 8)) + t[0:8] if cx > 8 else t

    totals = [jnp.zeros((8, 128), jnp.float32)] * (2 * SUMS)
    for s in range(2):
        for x in range(DEPTH, planes - DEPTH):
            d = diag[x][:cx]
            gx, gy, gz = own_ref[3, x - DEPTH], own_ref[4, x - DEPTH], own_ref[5, x - DEPTH]
            b = own_ref[s, x - DEPTH]
            q = p3[s, x]
            q0, q1, q2, q3 = p0[s, x][:cx], p1[s, x][:cx], p2[s, x][:cx], q[:cx]
            a0 = d * q2
            a1 = d * (2.0 * q1 - q2)
            a2 = d * (q2 - q3)
            links = gx * p3[s, x + 1][:cx] + gy * up_y(q)[:cx] + gz * up_z(q3)
            terms = [a0 * q0, a0 * q1, a0 * q2, a0 * q3, a1 * q1, a1 * q2, a1 * q3]
            terms += [a2 * q2, a2 * q3, (d * q3 - 2.0 * links) * q3]
            terms += [b * q0, b * q1, b * q2, b * q3]
            for k, t in enumerate(terms):
                totals[s * SUMS + k] = totals[s * SUMS + k] + folded(t)
    lanes = lax.broadcasted_iota(jnp.int32, (1, 128), 1)
    row = jnp.zeros((1, 128), jnp.float32)
    for k, t in enumerate(totals):
        at = k if k < SUMS else SIDE + k - SUMS
        whole = jnp.sum(jnp.sum(t, axis=0, keepdims=True), axis=1, keepdims=True)
        row = row + jnp.where(lanes == at, whole, 0.0)
    for k in range(sums_ref.shape[0]):
        sums_ref[k] = jnp.broadcast_to(row, sums_ref.shape[1:])


def combine_kernel(sums_ref, p0, p1, p2, p3, pot_ref, adj_ref, sens_ref, both):
    cx, cy, nz = pot_ref.shape
    total = jnp.sum(jnp.sum(sums_ref[...], axis=0), axis=0, keepdims=True)
    pair = jnp.concatenate([total, pltpu.roll(total, 128 - SIDE, 1)], axis=0)
    lanes = lax.broadcasted_iota(jnp.int32, (2, 128), 1)
    picked = [jnp.sum(jnp.where(lanes == k, pair, 0.0), axis=1, keepdims=True) for k in range(SUMS)]
    energy = {}
    order = iter(picked)
    for i in range(4):
        for j in range(i, 4):
            energy[i, j] = energy[j, i] = next(order)
    right = [next(order) for _ in range(4)]
    scale = [1.0 / jnp.sqrt(energy[i, i]) for i in range(4)]
    m = {(i, j): energy[i, j] * scale[i] * scale[j] for i in range(4) for j in range(4)}
    g = [right[i] * scale[i] for i in range(4)]
    pivot = [None] * 4
    for k in range(4):
        pivot[k] = jnp.where(m[k, k] > 4e-7, 1.0 / m[k, k], 0.0)
        for i in range(k + 1, 4):
            f = m[i, k] * pivot[k]
            for j in range(k, 4):
                m[i, j] = m[i, j] - f * m[k, j]
            g[i] = g[i] - f * g[k]
    c = [None] * 4
    for k in (3, 2, 1, 0):
        t = g[k]
        for j in range(k + 1, 4):
            t = t - m[k, j] * c[j]
        c[k] = t * pivot[k]
    c = [c[k] * scale[k] for k in range(4)]

    for x in range(cx + 1):
        for s in range(2):
            v = sum(c[k][s : s + 1] * ref[s, x + DEPTH] for k, ref in ((1, p1), (2, p2), (3, p3)))
            both[s, x] = v + c[0][s : s + 1] * p0[s, x + DEPTH]
    rows = lax.broadcasted_iota(jnp.int32, (cy, nz), 0)
    cols = lax.broadcasted_iota(jnp.int32, (cy, nz), 1)
    in_x = jnp.where(lax.axis_index("gx") == lax.axis_size("gx") - 1, 0.0, 1.0)
    end_y = lax.axis_index("gy") == lax.axis_size("gy") - 1
    in_y = jnp.where((rows == cy - 1) & end_y, 0.0, 1.0)
    in_z = jnp.where(cols == nz - 1, 0.0, 1.0)
    for x in range(cx):
        p, a = both[0, x], both[1, x]
        pot, adj = p[:cy], a[:cy]
        pot_ref[x] = pot
        adj_ref[x] = adj
        along = -(adj - both[1, x + 1][:cy]) * (pot - both[0, x + 1][:cy])
        sens_ref[0, x] = along * in_x if x == cx - 1 else along
        sens_ref[1, x] = -(adj - up_y(a)[:cy]) * (pot - up_y(p)[:cy]) * in_y
        sens_ref[2, x] = -(adj - up_z(adj)) * (pot - up_z(pot)) * in_z


def body(bond_mask, levels, electrode, leakage, source, weight):
    cx, cy, nz = leakage.shape
    shape = (cx, cy, nz)
    given = (levels, bond_mask, electrode, leakage, source, weight)
    nx, ny = lax.axis_size("gx"), lax.axis_size("gy")
    vmem = pl.BlockSpec(memory_space=pltpu.VMEM)
    slots = jax.ShapeDtypeStruct((SLOTS, cy, nz), jnp.float32)
    strip = jax.ShapeDtypeStruct((6, cx, DEPTH, nz), jnp.float32)
    fields, x_one, x_two, y_one, y_two = pl.pallas_call(
        pack_kernel,
        out_shape=[jax.ShapeDtypeStruct((6, *shape), jnp.float32), slots, slots, strip, strip],
        in_specs=[pl.BlockSpec(memory_space=pltpu.HBM)] * 6,
        out_specs=[vmem] * 5,
        scratch_shapes=[
            pltpu.SMEM(levels.shape, jnp.float32),
            pltpu.VMEM(bond_mask.shape, jnp.int32),
            pltpu.VMEM(electrode.shape, jnp.int32),
            pltpu.VMEM(shape, jnp.float32),
            pltpu.VMEM(shape, jnp.float32),
            pltpu.VMEM(shape, jnp.float32),
            pltpu.SemaphoreType.DMA((14,)),
        ],
        compiler_params=pltpu.CompilerParams(vmem_limit_bytes=24 * 2**20),
        name="pack",
    )(*(pltpu.with_memory_space_constraint(a, pltpu.HBM) for a in given))
    x_two = trade_two(x_two, "gx")
    y_one, y_two = trade_one(y_one, "gy"), trade_two(y_two, "gy")
    rest = jax.ShapeDtypeStruct((TILES, 2 * DEPTH, nz), jnp.float32)
    near = jax.ShapeDtypeStruct((2 * SLOTS + TILES, 2 * DEPTH, nz), jnp.float32)
    rim, one, c_two = pl.pallas_call(
        turn_kernel,
        out_shape=[jax.ShapeDtypeStruct((6, cx, 2 * DEPTH, nz), jnp.float32), near, rest],
        in_specs=[vmem] * 4,
        out_specs=[vmem] * 3,
        compiler_params=pltpu.CompilerParams(vmem_limit_bytes=24 * 2**20),
        name="turn",
    )(y_one, y_two, fields, x_one)
    c_two = trade_two(c_two, "gx")
    hint = pl.CostEstimate(flops=10**10, bytes_accessed=10**6, transcendentals=0)
    x_two = pl.pallas_call(
        slab_kernel,
        out_shape=slots,
        in_specs=[vmem],
        out_specs=vmem,
        compiler_params=pltpu.CompilerParams(vmem_limit_bytes=24 * 2**20),
        cost_estimate=hint,
        name="slab",
    )(x_two)
    c_two = pl.pallas_call(
        far_kernel,
        out_shape=rest,
        in_specs=[pl.BlockSpec(memory_space=pl.ANY), vmem],
        out_specs=vmem,
        compiler_params=pltpu.CompilerParams(vmem_limit_bytes=24 * 2**20),
        cost_estimate=hint,
        name="far",
    )(x_two, c_two)
    one = trade_one(one, "gx")
    planes, rows = cx + 2 * DEPTH, cy + 2 * DEPTH
    block = jax.ShapeDtypeStruct((2, planes, rows, nz), jnp.float32)
    parts = nx * ny
    sums, *basis = pl.pallas_call(
        basis_kernel,
        out_shape=[jax.ShapeDtypeStruct((parts // 8, 8, 128), jnp.float32)] + [block] * 4,
        in_specs=[vmem] * 5,
        out_specs=[vmem] * 5,
        scratch_shapes=[
            pltpu.VMEM((planes, rows, nz), jnp.float32),
            pltpu.VMEM((planes, rows, nz), jnp.float32),
            pltpu.VMEM((2, planes, rows, nz), jnp.float32),
            pltpu.VMEM((2 * SLOTS, cy, nz), jnp.float32),
            pltpu.VMEM((2, 6, 2, 2 * DEPTH, nz), jnp.float32),
        ],
        compiler_params=pltpu.CompilerParams(vmem_limit_bytes=24 * 2**20),
        name="basis",
    )(fields, rim, x_two, c_two, one)
    gathered = lax.all_to_all(sums.reshape(parts, 1, 128), ("gx", "gy"), 0, 0, tiled=True)
    return pl.pallas_call(
        combine_kernel,
        out_shape=[
            jax.ShapeDtypeStruct(shape, jnp.float32),
            jax.ShapeDtypeStruct(shape, jnp.float32),
            jax.ShapeDtypeStruct((3, *shape), jnp.float32),
        ],
        in_specs=[vmem] * 5,
        out_specs=[vmem] * 3,
        scratch_shapes=[pltpu.VMEM((2, cx + 1, rows, nz), jnp.float32)],
        compiler_params=pltpu.CompilerParams(vmem_limit_bytes=24 * 2**20),
        name="combine",
    )(gathered.reshape(parts // 8, 8, 128), *basis)


def solution(mesh):
    return jax.shard_map(
        body,
        mesh=mesh,
        in_specs=(
            P(None, "gx", "gy", None),
            P(),
            P(None, "gx", "gy"),
            P("gx", "gy", None),
            P("gx", "gy", None),
            P("gx", "gy", None),
        ),
        out_specs=(P("gx", "gy", None), P("gx", "gy", None), P(None, "gx", "gy", None)),
        check_vma=False,
    )
```

```python
import functools

import jax
import jax.numpy as jnp
from jax import lax
from jax.experimental import pallas as pl
from jax.experimental.pallas import tpu as pltpu
from jax.sharding import PartitionSpec as P

DEPTH = 4
SUMS = 14
SLOTS = 15
TILES = 16
SIDE = 64


def trade_one(value, axis):
    return lax.ppermute(value, axis, [(i, i ^ 1) for i in range(lax.axis_size(axis))])


def trade_two(value, axis):
    outer = [(i, i + 1) for i in range(1, lax.axis_size(axis) - 1, 2)]
    return lax.ppermute(value, axis, outer + [(target, source) for source, target in outer])


def is_even(axis):
    return lax.axis_index(axis) % 2 == 0


def up_y(v):
    return pltpu.roll(v, v.shape[0] - 1, 0)


def dn_y(v):
    return pltpu.roll(v, 1, 0)


def up_z(v):
    return pltpu.roll(v, v.shape[1] - 1, 1)


def dn_z(v):
    return pltpu.roll(v, 1, 1)


def slot(f, j):
    return (0, 3, 6, 9, 11, 13)[f] + j


def sent(f):
    return 3 if f < 3 else 2


def slab():
    out = []
    for f in range(6):
        count = sent(f)
        out += [(f, k, k - count) for k in range(count)]
    return out


def pack_kernel(level_hbm, mask_hbm, elec_hbm, leak_hbm, source_hbm, weight_hbm,
                own_ref, x_one, x_two, y_one, y_two,
                level_ref, mask_ref, elec_ref, leak_ref, source_ref, weight_ref, sems):
    cx, cy, nz = leak_ref.shape
    ix, iy = lax.axis_index("gx"), lax.axis_index("gy")
    whole = [(level_hbm, level_ref), (elec_hbm, elec_ref)]
    first = [pltpu.make_async_copy(a, b, sems.at[k]) for k, (a, b) in enumerate(whole)]
    half = cx // 2
    parts = []
    for h in range(2):
        at = pl.ds(h * half, half)
        pairs = [(mask_hbm.at[d, at], mask_ref.at[d, at]) for d in range(3)]
        pairs += [(leak_hbm.at[at], leak_ref.at[at]), (source_hbm.at[at], source_ref.at[at])]
        pairs += [(weight_hbm.at[at], weight_ref.at[at])]
        parts.append(
            [pltpu.make_async_copy(a, b, sems.at[2 + 6 * h + k]) for k, (a, b) in enumerate(pairs)]
        )
    for copy in first + parts[0] + parts[1]:
        copy.start()
    for copy in first + parts[0]:
        copy.wait()
    rows = lax.broadcasted_iota(jnp.int32, (cy, nz), 0)
    cols = lax.broadcasted_iota(jnp.int32, (cy, nz), 1)
    even_x, even_y = is_even("gx"), is_even("gy")
    keep_x = jnp.where(ix == lax.axis_size("gx") - 1, 0.0, 1.0)
    keep_y = jnp.where((rows == cy - 1) & (iy == lax.axis_size("gy") - 1), 0.0, 1.0)
    keep_z = jnp.where(cols == nz - 1, 0.0, 1.0)
    square = lax.broadcasted_iota(jnp.int32, (cy, cy), 0) == lax.broadcasted_iota(jnp.int32, (cy, cy), 1)
    before = None
    for x in range(cx):
        if x == half:
            for copy in parts[1]:
                copy.wait()
        c = [
            jnp.where(mask_ref[d, x] == 1, level_ref[1, d], level_ref[0, d]) for d in range(3)
        ]
        if x == cx - 1:
            c[0] = c[0] * keep_x
        c[1] = c[1] * keep_y
        c[2] = c[2] * keep_z
        ends = []
        for e, at in ((0, 0), (1, nz - 1)):
            row = jnp.broadcast_to(elec_ref[e, x : x + 1].astype(jnp.float32), (cy, cy))
            column = jnp.sum(jnp.where(square, row, 0.0), axis=1, keepdims=True)
            ends.append(jnp.where(cols == at, column, 0.0))
        part = leak_ref[x] + ends[0] + ends[1] + c[0] + c[1] + c[2]
        part = part + jnp.where(rows == 0, 0.0, dn_y(c[1])) + dn_z(c[2])
        if x:
            part = part + before
        before = c[0]
        own_ref[0, x] = source_ref[x] + ends[0]
        own_ref[1, x] = weight_ref[x] + ends[1]
        own_ref[2, x] = part
        for d in range(3):
            own_ref[3 + d, x] = c[d]
    for k, (f, above, below) in enumerate(slab()):
        low, high = own_ref[f, above], own_ref[f, cx + below]
        x_one[k] = jnp.where(even_x, high, low)
        x_two[k] = jnp.where(even_x, low, high)
    for f in range(6):
        for x in range(cx):
            low, high = own_ref[f, x, :DEPTH], own_ref[f, x, cy - DEPTH :]
            y_one[f, x] = jnp.where(even_y, high, low)
            y_two[f, x] = jnp.where(even_y, low, high)


def neighbours(v, above, below, next_x, last_x, cy, cz):
    beside = above * next_x + below * last_x
    beside = beside + cy * up_y(v) + dn_y(cy * v)
    return beside + cz * up_z(v) + dn_z(cz * v)


def turn_kernel(y_two, y_one, own_ref, x_one, rim_ref, one_ref, c_two):
    cx, cy = own_ref.shape[1:3]
    c_one = one_ref.at[pl.ds(2 * SLOTS, TILES)]
    for k in range(SLOTS):
        one_ref[2 * k] = x_one[k, :8]
        one_ref[2 * k + 1] = x_one[k, 8:]
    even_x, even_y = is_even("gx"), is_even("gy")
    for f in range(6):
        for x in range(cx):
            one, two = y_one[f, x], y_two[f, x]
            low, high = jnp.where(even_y, two, one), jnp.where(even_y, one, two)
            rim_ref[f, x] = jnp.concatenate([high, low], axis=0)
    def field(f, x):
        return jnp.concatenate([own_ref[f, x], rim_ref[f, x]], axis=0)

    rows = lax.broadcasted_iota(jnp.int32, (cx + 2 * DEPTH, 128), 0)
    seam = (rows == 0) | (rows == cx)

    def scaled(x):
        d = field(2, x) + jnp.where(seam, dn_y(field(4, x)), 0.0)
        r = jnp.where(d > 0.0, 1.0 / d, 0.0)
        return r, [field(s, x) * r for s in range(2)]

    summed = []
    for x in (2, cx - 2):
        (_, last), (r, here), (_, after) = scaled(x - 1), scaled(x), scaled(x + 1)
        row = []
        for s in range(2):
            v = here[s]
            beside = neighbours(v, field(3, x), field(3, x - 1), after[s], last[s], field(4, x), field(5, x))
            row.append(v + r * beside)
        summed.append(row)
    at = lax.broadcasted_iota(jnp.int32, (8, 128), 0)
    for f in range(6):
        tiles = []
        for e, order in enumerate(((0, 1, 2), (cx - 1, cx - 2, cx - 3))):
            near = rim_ref[f, order[0]]
            third = rim_ref[f, order[2]]
            far = jnp.where(at == 5, pltpu.roll(third, 6, 0), rim_ref[f, order[1]])
            far = jnp.where(at == 2, pltpu.roll(third, 2, 0), far)
            if f == 4:
                far = jnp.where(at == 3, pltpu.roll(own_ref[f, order[2], cy - 8 :], 4, 0), far)
            if f < 2:
                far = jnp.where(at == 3, pltpu.roll(summed[e][f][cy : cy + 8], 3, 0), far)
            tiles.append((near, far))
        for k in range(2):
            low, high = tiles[0][k], tiles[1][k]
            c_one[2 * f + k] = jnp.where(even_x, high, low)
            c_two[2 * f + k] = jnp.where(even_x, low, high)
    for s in range(2):
        for k in range(2):
            low, high = (summed[e][s][8 * k : 8 * k + 8] for e in range(2))
            c_one[12 + 2 * s + k] = jnp.where(even_x, high, low)
            c_two[12 + 2 * s + k] = jnp.where(even_x, low, high)


def slab_kernel(given_ref, out_ref):
    out_ref[...] = given_ref[...]


def far_kernel(slab_hbm, given_ref, out_ref):
    out_ref[...] = given_ref[...]


def basis_kernel(own_ref, rim_ref, x_two, c_two, one_ref,
                 sums_ref, p0, p1, p2, p3, diag, inv, v0, side_ref, corner_ref):
    cx = own_ref.shape[2]
    planes = cx + 2 * DEPTH
    even = is_even("gx")
    at = lax.broadcasted_iota(jnp.int32, (8, 128), 0)
    c_one = one_ref.at[pl.ds(2 * SLOTS, TILES)]
    for k in range(SLOTS):
        one = jnp.concatenate([one_ref[2 * k], one_ref[2 * k + 1]], axis=0)
        side_ref[k] = jnp.where(even, x_two[k], one)
        side_ref[SLOTS + k] = jnp.where(even, one, x_two[k])
    for f in range(6):
        for k in range(2):
            one, two = c_one[2 * f + k], c_two[2 * f + k]
            corner_ref[0, f, k] = jnp.where(even, two, one)
            corner_ref[1, f, k] = jnp.where(even, one, two)

    def corner(f, above, depth):
        if depth == 1:
            return corner_ref[above, f, 0]
        if depth == 2:
            return corner_ref[above, f, 1]
        t = corner_ref[above, f, 1]
        return jnp.where(at == 0, pltpu.roll(t, 6, 0), pltpu.roll(t, 2, 0))

    def field(f, x):
        if DEPTH <= x < DEPTH + cx:
            return jnp.concatenate([own_ref[f, x - DEPTH], rim_ref[f, x - DEPTH]], axis=0)
        above = int(x >= DEPTH)
        depth = x - DEPTH - cx + 1 if above else DEPTH - x
        count = sent(f)
        if depth > count:
            edge = jnp.where(at == 7, pltpu.roll(corner_ref[above, f, 1], 4, 0), 0.0)
            flat = jnp.concatenate([jnp.zeros((cx - 8, 128), jnp.float32), edge], axis=0)
        else:
            flat = side_ref[SLOTS + slot(f, depth - 1) if above else slot(f, count - depth)]
        return jnp.concatenate([flat, corner(f, above, depth)], axis=0)

    rows = lax.broadcasted_iota(jnp.int32, (cx + 2 * DEPTH, 128), 0)
    seam = (rows == 0) | (rows == cx)
    for x in range(2, planes - 1):
        d = field(2, x) + jnp.where(seam, dn_y(field(4, x)), 0.0)
        if x in (DEPTH, DEPTH + cx):
            d = d + field(3, x - 1)
        r = jnp.where(d > 0.0, 1.0 / d, 0.0)
        diag[x] = d
        inv[x] = r
        v0[0, x] = field(0, x) * r
        v0[1, x] = field(1, x) * r

    def jacobi(ref, x):
        above, below = field(3, x), field(3, x - 1)
        cy, cz, r = field(4, x), field(5, x), inv[x]
        out = []
        for s in range(2):
            v = ref[s, x]
            beside = neighbours(v, above, below, ref[s, x + 1], ref[s, x - 1], cy, cz)
            out.append((v, r * beside))
        return out

    for x in range(3, planes - 2):
        for s, (v, w) in enumerate(jacobi(v0, x)):
            p0[s, x] = v + w
            p1[s, x] = v - w
    for s in range(2):
        beyond = [jnp.where(at == 0, pltpu.roll(corner_ref[e, s, 1], 5, 0), 0.0) for e in range(2)]
        one = [c_one[12 + 2 * s + k] for k in range(2)]
        two = [c_two[12 + 2 * s + k] for k in range(2)]
        below = [jnp.where(even, b, a) for a, b in zip(one, two)]
        above = [jnp.where(even, a, b) for a, b in zip(one, two)]
        p0[s, 2] = jnp.concatenate(below + beyond[:1], axis=0)
        p0[s, planes - 2] = jnp.concatenate(above + beyond[1:], axis=0)
    for x in range(3, planes - 2):
        for s, (v, w) in enumerate(jacobi(p0, x)):
            p2[s, x] = v - w
    for x in range(4, planes - 3):
        for s, (v, w) in enumerate(jacobi(p2, x)):
            p3[s, x] = w

    def folded(t):
        return sum(t[8 * i : 8 * i + 8] for i in range(1, cx // 8)) + t[0:8] if cx > 8 else t

    totals = [jnp.zeros((8, 128), jnp.float32)] * (2 * SUMS)
    for s in range(2):
        for x in range(DEPTH, planes - DEPTH):
            d = diag[x][:cx]
            gx, gy, gz = own_ref[3, x - DEPTH], own_ref[4, x - DEPTH], own_ref[5, x - DEPTH]
            b = own_ref[s, x - DEPTH]
            q = p3[s, x]
            q0, q1, q2, q3 = p0[s, x][:cx], p1[s, x][:cx], p2[s, x][:cx], q[:cx]
            a0 = d * q2
            a1 = d * (2.0 * q1 - q2)
            a2 = d * (q2 - q3)
            links = gx * p3[s, x + 1][:cx] + gy * up_y(q)[:cx] + gz * up_z(q3)
            terms = [a0 * q0, a0 * q1, a0 * q2, a0 * q3, a1 * q1, a1 * q2, a1 * q3]
            terms += [a2 * q2, a2 * q3, (d * q3 - 2.0 * links) * q3]
            terms += [b * q0, b * q1, b * q2, b * q3]
            for k, t in enumerate(terms):
                totals[s * SUMS + k] = totals[s * SUMS + k] + folded(t)
    lanes = lax.broadcasted_iota(jnp.int32, (1, 128), 1)
    row = jnp.zeros((1, 128), jnp.float32)
    for k, t in enumerate(totals):
        at = k if k < SUMS else SIDE + k - SUMS
        whole = jnp.sum(jnp.sum(t, axis=0, keepdims=True), axis=1, keepdims=True)
        row = row + jnp.where(lanes == at, whole, 0.0)
    for k in range(sums_ref.shape[0]):
        sums_ref[k] = jnp.broadcast_to(row, sums_ref.shape[1:])


def combine_kernel(sums_ref, p0, p1, p2, p3, pot_ref, adj_ref, sens_ref, both):
    cx, cy, nz = pot_ref.shape
    total = jnp.sum(jnp.sum(sums_ref[...], axis=0), axis=0, keepdims=True)
    pair = jnp.concatenate([total, pltpu.roll(total, 128 - SIDE, 1)], axis=0)
    lanes = lax.broadcasted_iota(jnp.int32, (2, 128), 1)
    picked = [jnp.sum(jnp.where(lanes == k, pair, 0.0), axis=1, keepdims=True) for k in range(SUMS)]
    energy = {}
    order = iter(picked)
    for i in range(4):
        for j in range(i, 4):
            energy[i, j] = energy[j, i] = next(order)
    right = [next(order) for _ in range(4)]
    scale = [1.0 / jnp.sqrt(energy[i, i]) for i in range(4)]
    m = {(i, j): energy[i, j] * scale[i] * scale[j] for i in range(4) for j in range(4)}
    g = [right[i] * scale[i] for i in range(4)]
    pivot = [None] * 4
    for k in range(4):
        pivot[k] = jnp.where(m[k, k] > 4e-7, 1.0 / m[k, k], 0.0)
        for i in range(k + 1, 4):
            f = m[i, k] * pivot[k]
            for j in range(k, 4):
                m[i, j] = m[i, j] - f * m[k, j]
            g[i] = g[i] - f * g[k]
    c = [None] * 4
    for k in (3, 2, 1, 0):
        t = g[k]
        for j in range(k + 1, 4):
            t = t - m[k, j] * c[j]
        c[k] = t * pivot[k]
    c = [c[k] * scale[k] for k in range(4)]

    for x in range(cx + 1):
        for s in range(2):
            v = sum(c[k][s : s + 1] * ref[s, x + DEPTH] for k, ref in ((1, p1), (2, p2), (3, p3)))
            both[s, x] = v + c[0][s : s + 1] * p0[s, x + DEPTH]
    rows = lax.broadcasted_iota(jnp.int32, (cy, nz), 0)
    cols = lax.broadcasted_iota(jnp.int32, (cy, nz), 1)
    in_x = jnp.where(lax.axis_index("gx") == lax.axis_size("gx") - 1, 0.0, 1.0)
    end_y = lax.axis_index("gy") == lax.axis_size("gy") - 1
    in_y = jnp.where((rows == cy - 1) & end_y, 0.0, 1.0)
    in_z = jnp.where(cols == nz - 1, 0.0, 1.0)
    for x in range(cx):
        p, a = both[0, x], both[1, x]
        pot, adj = p[:cy], a[:cy]
        pot_ref[x] = pot
        adj_ref[x] = adj
        along = -(adj - both[1, x + 1][:cy]) * (pot - both[0, x + 1][:cy])
        sens_ref[0, x] = along * in_x if x == cx - 1 else along
        sens_ref[1, x] = -(adj - up_y(a)[:cy]) * (pot - up_y(p)[:cy]) * in_y
        sens_ref[2, x] = -(adj - up_z(adj)) * (pot - up_z(pot)) * in_z


def body(bond_mask, levels, electrode, leakage, source, weight):
    cx, cy, nz = leakage.shape
    shape = (cx, cy, nz)
    given = (levels, bond_mask, electrode, leakage, source, weight)
    nx, ny = lax.axis_size("gx"), lax.axis_size("gy")
    vmem = pl.BlockSpec(memory_space=pltpu.VMEM)
    slots = jax.ShapeDtypeStruct((SLOTS, cy, nz), jnp.float32)
    strip = jax.ShapeDtypeStruct((6, cx, DEPTH, nz), jnp.float32)
    fields, x_one, x_two, y_one, y_two = pl.pallas_call(
        pack_kernel,
        out_shape=[jax.ShapeDtypeStruct((6, *shape), jnp.float32), slots, slots, strip, strip],
        in_specs=[pl.BlockSpec(memory_space=pltpu.HBM)] * 6,
        out_specs=[vmem] * 5,
        scratch_shapes=[
            pltpu.SMEM(levels.shape, jnp.float32),
            pltpu.VMEM(bond_mask.shape, jnp.int32),
            pltpu.VMEM(electrode.shape, jnp.int32),
            pltpu.VMEM(shape, jnp.float32),
            pltpu.VMEM(shape, jnp.float32),
            pltpu.VMEM(shape, jnp.float32),
            pltpu.SemaphoreType.DMA((14,)),
        ],
        compiler_params=pltpu.CompilerParams(vmem_limit_bytes=24 * 2**20),
        name="pack",
    )(*(pltpu.with_memory_space_constraint(a, pltpu.HBM) for a in given))
    x_two = trade_two(x_two, "gx")
    y_one, y_two = trade_one(y_one, "gy"), trade_two(y_two, "gy")
    rest = jax.ShapeDtypeStruct((TILES, 2 * DEPTH, nz), jnp.float32)
    near = jax.ShapeDtypeStruct((2 * SLOTS + TILES, 2 * DEPTH, nz), jnp.float32)
    rim, one, c_two = pl.pallas_call(
        turn_kernel,
        out_shape=[jax.ShapeDtypeStruct((6, cx, 2 * DEPTH, nz), jnp.float32), near, rest],
        in_specs=[vmem] * 4,
        out_specs=[vmem] * 3,
        compiler_params=pltpu.CompilerParams(vmem_limit_bytes=24 * 2**20),
        name="turn",
    )(y_two, y_one, fields, x_one)
    c_two = trade_two(c_two, "gx")
    hint = pl.CostEstimate(flops=10**9, bytes_accessed=10**6, transcendentals=0)
    x_two = pl.pallas_call(
        slab_kernel,
        out_shape=slots,
        in_specs=[vmem],
        out_specs=vmem,
        compiler_params=pltpu.CompilerParams(vmem_limit_bytes=24 * 2**20),
        cost_estimate=hint,
        name="slab",
    )(x_two)
    c_two = pl.pallas_call(
        far_kernel,
        out_shape=rest,
        in_specs=[pl.BlockSpec(memory_space=pl.ANY), vmem],
        out_specs=vmem,
        compiler_params=pltpu.CompilerParams(vmem_limit_bytes=24 * 2**20),
        cost_estimate=hint,
        name="far",
    )(x_two, c_two)
    one = trade_one(one, "gx")
    planes, rows = cx + 2 * DEPTH, cy + 2 * DEPTH
    block = jax.ShapeDtypeStruct((2, planes, rows, nz), jnp.float32)
    parts = nx * ny
    sums, *basis = pl.pallas_call(
        basis_kernel,
        out_shape=[jax.ShapeDtypeStruct((parts // 8, 8, 128), jnp.float32)] + [block] * 4,
        in_specs=[vmem] * 5,
        out_specs=[vmem] * 5,
        scratch_shapes=[
            pltpu.VMEM((planes, rows, nz), jnp.float32),
            pltpu.VMEM((planes, rows, nz), jnp.float32),
            pltpu.VMEM((2, planes, rows, nz), jnp.float32),
            pltpu.VMEM((2 * SLOTS, cy, nz), jnp.float32),
            pltpu.VMEM((2, 6, 2, 2 * DEPTH, nz), jnp.float32),
        ],
        compiler_params=pltpu.CompilerParams(vmem_limit_bytes=24 * 2**20),
        name="basis",
    )(fields, rim, x_two, c_two, one)
    gathered = lax.all_to_all(sums.reshape(parts, 1, 128), ("gx", "gy"), 0, 0, tiled=True)
    return pl.pallas_call(
        combine_kernel,
        out_shape=[
            jax.ShapeDtypeStruct(shape, jnp.float32),
            jax.ShapeDtypeStruct(shape, jnp.float32),
            jax.ShapeDtypeStruct((3, *shape), jnp.float32),
        ],
        in_specs=[vmem] * 5,
        out_specs=[vmem] * 3,
        scratch_shapes=[pltpu.VMEM((2, cx + 1, rows, nz), jnp.float32)],
        compiler_params=pltpu.CompilerParams(vmem_limit_bytes=24 * 2**20),
        name="combine",
    )(gathered.reshape(parts // 8, 8, 128), *basis)


def solution(mesh):
    return jax.shard_map(
        body,
        mesh=mesh,
        in_specs=(
            P(None, "gx", "gy", None),
            P(),
            P(None, "gx", "gy"),
            P("gx", "gy", None),
            P("gx", "gy", None),
            P("gx", "gy", None),
        ),
        out_specs=(P("gx", "gy", None), P("gx", "gy", None), P(None, "gx", "gy", None)),
        check_vma=False,
    )
```
